32 devices in a mesh: ctx: 8 (over z, y), tp: 4 (over x, core).
Axes of the slice: x: 2, y: 2, z: 4, core: 2. Of those that a mesh axis runs over, the one named last changes fastest.
Arguments:
- tokens: bfloat16 [4096, 5376], P(('ctx', 'tp')), may hold values from -8 to 8
- positions: int32 [4096], replicated, may hold values from 0 to 16383, as said below
- w_query: bfloat16 [5376, 2048], P('ctx', 'tp'), may hold values from -1 to 1
- key_matrix: bfloat16 [5376, 1024], P('ctx', 'tp'), may hold values from -1 to 1
- value_matrix: bfloat16 [5376, 1024], P('ctx', 'tp'), may hold values from -0.078125 to 0.078125
- w_out: bfloat16 [2048, 5376], P('tp', 'ctx'), may hold values from -0.125 to 0.125
- gain_in: float32 [5376], replicated, may hold values from 0.1 to 1.9
- gain_query: float32 [128], replicated, may hold values from 0.5 to 14
- gain_key: float32 [128], replicated, may hold values from 0.5 to 14
- gain_post: float32 [5376], replicated, may hold values from 0.1 to 1.9
Outputs:
- layer_out: bfloat16 [4096, 5376], P(('ctx', 'tp'))
The draws below stay inside these ranges and needn't reach their ends.
Inputs may be any that keep to these rules, and one draw needn't show every extreme that they name: (positions) rise strictly along the tokens, by 1 to 4 from one token to the next, and the last token stands at 16383.
All inputs are finite; a program needn't handle non-finite values.
Results may differ from the reference program's by a relative error of at most 0.013.
The reference program's roundings to bfloat16 on the way count: a program that leaves them out, or rounds other values in their place, can miss the bound.
Values may be sent and summed in bfloat16 or wider, within the bound.
A program may use at most 128 MiB of HBM per device.

```python
import jax
import jax.numpy as jnp
from jax import lax

MODEL_WIDTH = 5376
QUERY_HEAD_COUNT = 16
KEY_VALUE_HEADS = 8
HEAD_SIZE = 128
QS = 168
LOOKBACK_WINDOW = 1024
TOK_DEV = 512
TOKEN_COUNT = 4096


def draw_tokens(key, part):
    sampled_values = jax.random.normal(jax.random.fold_in(key, 1), (TOKEN_COUNT, MODEL_WIDTH), jnp.float32)
    return jnp.clip(sampled_values, -8.0, 8.0).astype(jnp.bfloat16)


def draw_positions(key, part):
    jumps = jax.random.randint(jax.random.fold_in(key, 12), (TOKEN_COUNT,), 0, 8) == 0
    extra = jax.random.randint(jax.random.fold_in(key, 13), (TOKEN_COUNT,), 1, 4)
    step_sizes = 1 + jnp.where(jumps, extra, 0)
    relative = jnp.cumsum(step_sizes) - step_sizes[0]
    last_pos = 4 * TOKEN_COUNT - 1
    return (last_pos - relative[-1] + relative).astype(jnp.int32)


def grouped_query(key):
    sampled_values = jax.random.normal(jax.random.fold_in(key, 101), (MODEL_WIDTH, QUERY_HEAD_COUNT * HEAD_SIZE), jnp.float32)
    return jnp.clip(sampled_values, -6.0, 6.0) * MODEL_WIDTH ** (-0.5)


def draw_w_query(key, part):
    return grouped_query(key).astype(jnp.bfloat16)


def draw_key_matrix(key, part):
    sampled_values = jax.random.normal(jax.random.fold_in(key, 103), (MODEL_WIDTH, KEY_VALUE_HEADS * HEAD_SIZE), jnp.float32)
    return (jnp.clip(sampled_values, -6.0, 6.0) * MODEL_WIDTH ** (-0.5)).astype(jnp.bfloat16)


def draw_gain_query(key, part):
    sampled_values = jax.random.uniform(jax.random.fold_in(key, 202), (HEAD_SIZE,), jnp.float32, 0.5, 2.0)
    return sampled_values


def draw_gain_key(key, part):
    sampled_values = jax.random.uniform(jax.random.fold_in(key, 203), (HEAD_SIZE,), jnp.float32, 0.5, 2.0)
    return sampled_values


def level_of(key, extent, shards, smallest, high):
    def one(axis_at, blocks):
        draws = jax.random.uniform(jax.random.fold_in(jax.random.fold_in(key, 6), axis_at), (blocks,), jnp.float32, smallest / len(shards), high / len(shards))
        return jnp.repeat(jnp.exp(draws), extent[axis_at] // blocks).reshape((-1,) + (1,) * (len(extent) - axis_at - 1))

    factor_of = one(*shards[0])
    for cut in shards[1:]:
        factor_of = factor_of * one(*cut)
    return factor_of


def bell_draw(rng, shape, scale, limit, pieces=(), kind=jnp.bfloat16):
    array = jax.random.normal(rng, shape, jnp.float32) * scale
    if len(pieces) > 0:
        array = level_of(rng, shape, pieces, -0.22, 0.18) * array
    return jnp.clip(array, min=-limit, max=limit).astype(kind)


def setup_inputs(seed: int = 0) -> dict:
    key_list = jax.random.split(jax.random.key(seed), 11)
    tokens = draw_tokens(jax.random.fold_in(key_list[10], 71), 0)
    positions = draw_positions(jax.random.fold_in(key_list[10], 71), 0)
    w_query = draw_w_query(jax.random.fold_in(key_list[10], 71), 0)
    key_matrix = draw_key_matrix(jax.random.fold_in(key_list[10], 71), 0)
    value_matrix = bell_draw(key_list[4], (MODEL_WIDTH, KEY_VALUE_HEADS * HEAD_SIZE), MODEL_WIDTH ** -0.5, 0.078125, ((0, 8), (1, 4)))
    w_out = bell_draw(key_list[5], (QUERY_HEAD_COUNT * HEAD_SIZE, MODEL_WIDTH), (QUERY_HEAD_COUNT * HEAD_SIZE) ** -0.5, 0.125, ((0, 4), (1, 8)))
    gain_in = jnp.clip(1.0 + 0.18 * jax.random.normal(key_list[6], (MODEL_WIDTH,), jnp.float32), 0.1, 1.9)
    gain_query = draw_gain_query(jax.random.fold_in(key_list[10], 71), 0)
    gain_key = draw_gain_key(jax.random.fold_in(key_list[10], 71), 0)
    gain_post = jnp.clip(1.0 + 0.18 * jax.random.normal(key_list[9], (MODEL_WIDTH,), jnp.float32), 0.1, 1.9)
    return {"tokens": tokens, "positions": positions, "w_query": w_query, "key_matrix": key_matrix, "value_matrix": value_matrix, "w_out": w_out, "gain_in": gain_in, "gain_query": gain_query, "gain_key": gain_key, "gain_post": gain_post}


EPSILON = 1e-06
ROPE_BASE = 10000.0

def row_norm(values, scales):
    mean_square = lax.optimization_barrier(jnp.mean(values * values, axis=-1, keepdims=True))
    return values * lax.rsqrt(mean_square + EPSILON) * scales

def rotate(head_rows, offsets):
    half_dim = head_rows.shape[-1] // 2
    frequency = ROPE_BASE ** (-(jnp.arange(half_dim, dtype=jnp.float32) * 2.0) / head_rows.shape[-1])
    angles = offsets.astype(jnp.float32)[:, None] * frequency[None, :]
    cosine = jnp.cos(angles)[:, None, :]
    sine_wave = jnp.sin(angles)[:, None, :]
    first_half = head_rows[..., :half_dim]
    second_half = head_rows[..., half_dim:]
    return jnp.concatenate([first_half * cosine - second_half * sine_wave, second_half * cosine + first_half * sine_wave], axis=-1)

def attend(query_matrix, projected_keys, projected_values, query_offsets, key_offsets, key_valid):
    scores = jnp.einsum('qkgd,skd->kgqs', query_matrix.astype(jnp.float32), projected_keys.astype(jnp.float32)) * QS ** (-0.5)
    position_gap = query_offsets[:, None] - key_offsets[None, :]
    allowed = key_valid[None, :] & (position_gap >= 0) & (position_gap < LOOKBACK_WINDOW)
    scores = jnp.where(allowed[None, None], scores, -1e+30)
    row_max = lax.optimization_barrier(jnp.max(scores, axis=-1, keepdims=True))
    weights = jnp.where(allowed[None, None], jnp.exp(scores - row_max), 0.0)
    totals = lax.optimization_barrier(jnp.sum(weights, axis=-1, keepdims=True))
    rounded = weights.astype(jnp.bfloat16)
    mixed = jnp.einsum('kgqs,skd->qkgd', rounded.astype(jnp.float32), projected_values.astype(jnp.float32))
    mixed = mixed / jnp.transpose(totals, (2, 0, 1, 3))
    return mixed.astype(jnp.bfloat16).reshape(query_matrix.shape[0], -1)

def reference(tokens, positions, w_query, key_matrix, value_matrix, w_out, gain_in, gain_query, gain_key, gain_post):
    normalized_rows = row_norm(tokens.astype(jnp.float32), gain_in).astype(jnp.bfloat16)
    offsets = positions - positions[0]
    query_raw = jnp.dot(normalized_rows, w_query, preferred_element_type=jnp.float32).reshape(TOKEN_COUNT, QUERY_HEAD_COUNT, HEAD_SIZE)
    unnormed_keys = jnp.dot(normalized_rows, key_matrix, preferred_element_type=jnp.float32).reshape(TOKEN_COUNT, KEY_VALUE_HEADS, HEAD_SIZE)
    projected_values = jnp.dot(normalized_rows, value_matrix, preferred_element_type=jnp.float32).astype(jnp.bfloat16).reshape(TOKEN_COUNT, KEY_VALUE_HEADS, HEAD_SIZE)
    query_matrix = rotate(row_norm(query_raw, gain_query), offsets).astype(jnp.bfloat16)
    projected_keys = rotate(row_norm(unnormed_keys, gain_key), offsets).astype(jnp.bfloat16)
    query_matrix = query_matrix.reshape(TOKEN_COUNT, KEY_VALUE_HEADS, QUERY_HEAD_COUNT // KEY_VALUE_HEADS, HEAD_SIZE)
    keys_with_padding = jnp.concatenate([jnp.zeros((LOOKBACK_WINDOW, KEY_VALUE_HEADS, HEAD_SIZE), jnp.bfloat16), projected_keys], axis=0)
    values_with_padding = jnp.concatenate([jnp.zeros((LOOKBACK_WINDOW, KEY_VALUE_HEADS, HEAD_SIZE), jnp.bfloat16), projected_values], axis=0)
    padded_offsets = jnp.concatenate([jnp.zeros((LOOKBACK_WINDOW,), jnp.int32), offsets.astype(jnp.int32)], axis=0)

    def one_block(block_index):
        block_begin = (block_index * TOK_DEV).astype(jnp.int32)
        query_block = lax.dynamic_slice_in_dim(query_matrix, block_begin, TOK_DEV, 0)
        query_offsets = lax.dynamic_slice_in_dim(offsets.astype(jnp.int32), block_begin, TOK_DEV, 0)
        key_block = lax.dynamic_slice_in_dim(keys_with_padding, block_begin, LOOKBACK_WINDOW + TOK_DEV, 0)
        value_block = lax.dynamic_slice_in_dim(values_with_padding, block_begin, LOOKBACK_WINDOW + TOK_DEV, 0)
        key_offsets = lax.dynamic_slice_in_dim(padded_offsets, block_begin, LOOKBACK_WINDOW + TOK_DEV, 0)
        key_valid = block_begin + jnp.arange(LOOKBACK_WINDOW + TOK_DEV, dtype=jnp.int32) >= LOOKBACK_WINDOW
        return attend(query_block, key_block, value_block, query_offsets, key_offsets, key_valid)
    blocks = lax.map(one_block, jnp.arange(TOKEN_COUNT // TOK_DEV, dtype=jnp.int32))
    attended = blocks.reshape(TOKEN_COUNT, QUERY_HEAD_COUNT * HEAD_SIZE)
    projected = jnp.dot(attended, w_out, preferred_element_type=jnp.float32)
    return (tokens.astype(jnp.float32) + row_norm(projected, gain_post)).astype(jnp.bfloat16)
```

```python
import jax
import jax.numpy as jnp
from jax import lax
from jax.experimental import pallas as pl
from jax.experimental.pallas import tpu as pltpu
from jax.sharding import PartitionSpec as P

HEAD_SIZE = 128
QS = 168
LOOKBACK_WINDOW = 1024


EPSILON = 1e-06
ROPE_BASE = 10000.0


def shifted(value, axis, steps):
    count = lax.axis_size(axis)
    leading, last = (max(0, -steps), min(count, count - steps))
    return lax.ppermute(value, axis, [(source, source + steps) for source in range(leading, last)])


def row_norm(values, scales):
    mean_square = jnp.mean(values * values, axis=-1, keepdims=True)
    return values * lax.rsqrt(mean_square + EPSILON) * scales


def rotate(head_rows, offsets):
    half_dim = head_rows.shape[-1] // 2
    frequency = ROPE_BASE ** (
        -(jnp.arange(half_dim, dtype=jnp.float32) * 2.0) / head_rows.shape[-1]
    )
    angles = offsets.astype(jnp.float32)[:, None] * frequency[None, :]
    cosine = jnp.cos(angles)[:, None, :]
    sine_wave = jnp.sin(angles)[:, None, :]
    first_half = head_rows[..., :half_dim]
    second_half = head_rows[..., half_dim:]
    return jnp.concatenate(
        [
            first_half * cosine - second_half * sine_wave,
            second_half * cosine + first_half * sine_wave,
        ],
        axis=-1,
    )


Z_SIZE = 4
TILE = 16
W_PIECES = 4
O_PIECES = 2
MESH = pl.DeviceIdType.MESH
FAR_KEY = 1e9


def remote(source, target, send, recv, device):
    return pltpu.make_async_remote_copy(
        src_ref=source, dst_ref=target, send_sem=send, recv_sem=recv,
        device_id=device, device_id_type=MESH,
    )


def aligned(value, size, step=TILE):
    return pl.ds(pl.multiple_of(value, step), size)


class Places:
    def __init__(self):
        self.ctx = lax.axis_index("ctx")
        self.tp = lax.axis_index("tp")
        self.z, self.y = self.ctx // 2, self.ctx % 2
        self.x, self.c = self.tp // 2, self.tp % 2
        y_ctx = self.z * 2 + 1 - self.y
        core_tp = self.x * 2 + 1 - self.c
        self.core_id = (self.ctx, core_tp)
        self.x_id = (self.ctx, (1 - self.x) * 2 + self.c)
        self.y_id = (y_ctx, self.tp)
        self.diag_id = (y_ctx, core_tp)
        self.up_id = (self.ctx + 2, self.tp)
        self.down_id = (self.ctx - 2, self.tp)

    def greet(self):
        barrier = pltpu.get_barrier_semaphore()

        def signal(target):
            pl.semaphore_signal(barrier, inc=1, device_id=target, device_id_type=MESH)

        for target in (self.core_id, self.x_id, self.y_id, self.diag_id):
            signal(target)

        @pl.when(self.z < Z_SIZE - 1)
        def _():
            signal(self.up_id)

        @pl.when(self.z > 0)
        def _():
            signal(self.down_id)

    def meet(self):
        middle = ((self.z + 1) // 2) % 2
        pl.semaphore_wait(pltpu.get_barrier_semaphore(), 5 + middle)


class Line:
    def __init__(self, places, piece_ref, pieces, sems):
        self.at, self.piece_ref, self.pieces = places, piece_ref, pieces
        self.up_send, self.down_send, self.below, self.above = sems

    def copy(self, plane, distance, piece, upward):
        ref = self.piece_ref(plane, piece)
        slot = distance * self.pieces + piece
        if upward:
            return remote(ref, ref, self.up_send.at[slot], self.below.at[slot], self.at.up_id)
        return remote(ref, ref, self.down_send.at[slot], self.above.at[slot], self.at.down_id)

    def send_own(self, piece):
        z = self.at.z

        @pl.when(z < Z_SIZE - 1)
        def _():
            self.copy(z, 0, piece, True).start()

        @pl.when(z > 0)
        def _():
            self.copy(z, 0, piece, False).start()

    def forward(self, distance, piece):
        z = self.at.z
        if distance == Z_SIZE - 1:
            return

        @pl.when((z >= distance) & (z < Z_SIZE - 1))
        def _():
            self.copy(z - distance, distance - 1, piece, True).wait_recv()
            self.copy(z - distance, distance, piece, True).start()

        @pl.when((z + distance < Z_SIZE) & (z > 0))
        def _():
            self.copy(z + distance, distance - 1, piece, False).wait_recv()
            self.copy(z + distance, distance, piece, False).start()

    def arrive(self, distance, piece):
        z = self.at.z

        @pl.when(z == Z_SIZE - 1)
        def _():
            self.copy(z - distance, distance - 1, piece, True).wait_recv()

        @pl.when(z == 0)
        def _():
            self.copy(z + distance, distance - 1, piece, False).wait_recv()

    def drain(self):
        z = self.at.z
        for distance in range(Z_SIZE - 1):
            for piece in range(self.pieces):
                @pl.when((z < Z_SIZE - 1) & (z >= distance))
                def _():
                    self.copy(z - distance, distance, piece, True).wait_send()

                @pl.when((z > 0) & (z + distance < Z_SIZE))
                def _():
                    self.copy(z + distance, distance, piece, False).wait_send()


def line_semaphores(pieces):
    return [pltpu.SemaphoreType.DMA(((Z_SIZE - 1) * pieces,)) for _ in range(4)]


def layer_kernel(
    tok_ref, wq_ref, wk_ref, wv_ref, wo_ref, gin_ref, gpost_ref, gq_ref, gk_ref, pos_ref, freq_ref,
    out_ref,
    xs, x_all, ws, w_all, acc, queries, kv, att_own, att_all, wo_raw, wo_all,
    cos_t, sin_t, q_off, k_off,
    sent_core, got_core, kept, sent_x, got_x, sent_y, got_y, fin, outs,
    stage_sem, local_sem, w_send, w_recv, x_send, x_recv, halo_send, halo_recv, att_send, att_recv,
    core_send, core_recv, sx_send, sx_recv, sy_send, sy_recv,
    *line_sems,
):
    at = Places()
    z, y, x, c = at.z, at.y, at.x, at.c
    same = c == y
    depth = wq_ref.shape[0]
    own_tokens, model = xs.shape
    plane_tokens = x_all.shape[0]
    head = HEAD_SIZE
    f32, bf16 = jnp.float32, jnp.bfloat16
    at.greet()

    q_half, k_half = 2 * head, head
    loads = []
    for half in range(2):
        for ref, begin, width in ((wq_ref, 0, q_half), (wk_ref, q_half, k_half), (wv_ref, q_half + k_half, k_half)):
            loads.append(pltpu.make_async_copy(
                ref.at[:, pl.ds(half * width, width)],
                ws.at[half, :, pl.ds(begin, width)],
                stage_sem.at[len(loads)],
            ))
    tok_load = pltpu.make_async_copy(tok_ref, xs, stage_sem.at[6])
    wo_load = pltpu.make_async_copy(wo_ref, wo_raw, stage_sem.at[7])
    for copy in loads + [tok_load, wo_load]:
        copy.start()
    for copy in loads:
        copy.wait()
    at.meet()

    def block_rows(plane, row):
        return w_all.at[aligned((plane * 2 + row) * depth, depth)]

    def near_copy():
        return remote(ws.at[1 - c], block_rows(z, y), w_send.at[0], w_recv.at[0], at.core_id)

    def far_copy(target):
        block = block_rows(z, y) if target is not None else block_rows(z, 1 - y)
        device = at.y_id if target is None else target
        if target is at.diag_id:
            return remote(ws.at[1 - c], block, w_send.at[1], w_recv.at[1], device)
        return remote(ws.at[c], block, w_send.at[0], w_recv.at[1], device)

    own_block = pltpu.make_async_copy(ws.at[c], block_rows(z, y), local_sem.at[0])

    @pl.when(same)
    def _():
        near_copy().start()
        own_block.start()

    @pl.when(jnp.logical_not(same))
    def _():
        far_copy(at.y_id).start()
        far_copy(at.diag_id).start()

    half_rows = depth // 2

    def w_piece(plane, piece):
        row = at.y if piece < 2 else 1 - at.y
        return w_all.at[aligned((plane * 2 + row) * depth + (piece % 2) * half_rows, half_rows)]

    def o_piece(plane, piece):
        return wo_all.at[plane, pl.ds(piece * half_rows, half_rows)]

    w_line = Line(at, w_piece, W_PIECES, line_sems[:4])
    o_line = Line(at, o_piece, O_PIECES, line_sems[4:])

    @pl.when(same)
    def _():
        own_block.wait()

    @pl.when(jnp.logical_not(same))
    def _():
        near_copy().wait_recv()

    for piece in range(2):
        w_line.send_own(piece)

    def block_of(row, column, core):
        return (row * 4 + column * 2 + core) * own_tokens

    tok_load.wait()
    own_begin = block_of(y, x, c)

    @pl.loop(0, own_tokens // TILE)
    def _(step):
        v = xs[aligned(step * TILE, TILE), :].astype(f32)
        mean_square = jnp.mean(v * v, axis=-1, keepdims=True)
        x_all[aligned(own_begin + step * TILE, TILE), :] = (
            v * lax.rsqrt(mean_square + EPSILON) * gin_ref[...]
        ).astype(bf16)

    def x_copy(slot, block, device, begin=0, size=own_tokens):
        ref = x_all.at[aligned(block + begin, size)]
        return remote(ref, ref, x_send.at[slot], x_recv.at[slot], device)

    cut = own_tokens * 3 // 4
    x_block, y_block, far_block = block_of(y, 1 - x, c), block_of(1 - y, x, c), block_of(1 - y, 1 - x, c)
    sends = [
        x_copy(0, own_begin, at.x_id),
        x_copy(1, own_begin, at.y_id),
        x_copy(2, y_block, at.x_id, 0, cut),
        x_copy(3, x_block, at.y_id, cut, own_tokens - cut),
        x_copy(4, own_begin, at.core_id),
        x_copy(5, x_block, at.core_id),
        x_copy(6, y_block, at.core_id),
        x_copy(7, far_block, at.core_id),
    ]
    sends[0].start()
    sends[1].start()
    sends[4].start()

    far_copy(None).wait_recv()
    for piece in range(2, W_PIECES):
        w_line.send_own(piece)

    first = pos_ref[0:1, 0:1]
    blocks = plane_tokens // head

    @pl.loop(0, blocks)
    def _(block):
        row = (pos_ref[pl.ds(z * blocks + block, 1), :] - first).astype(f32)
        column = jnp.broadcast_to(row, (head, head)).T
        here = aligned(block * head, head)
        q_off[here, :] = column
        angles = column * freq_ref[...]
        cos_t[here, :] = jnp.cos(angles)
        lane = lax.broadcasted_iota(jnp.int32, (head, head), 1)
        sine = jnp.sin(angles)
        sin_t[here, :] = jnp.where(lane < head // 2, -sine, sine)

    for block in range(2 * blocks):
        index = jnp.maximum((z - 1) * blocks + block, 0)
        row = (pos_ref[pl.ds(index, 1), :] - first).astype(f32)
        if block < blocks:
            row = jnp.where(z > 0, row, FAR_KEY)
        k_off[:, block * head:(block + 1) * head] = row

    @pl.when(z == 0)
    def _():
        kv[:, pl.ds(0, plane_tokens), :] = jnp.zeros((2, plane_tokens, head), bf16)

    wo_load.wait()
    wo_all[z] = wo_raw[...].T

    for piece in range(W_PIECES):
        w_line.forward(1, piece)
    x_copy(0, x_block, at.x_id).wait_recv()
    sends[3].start()
    sends[5].start()
    x_copy(1, y_block, at.y_id).wait_recv()
    sends[2].start()
    sends[6].start()
    for piece in range(W_PIECES):
        w_line.forward(2, piece)
    for piece in range(O_PIECES):
        o_line.send_own(piece)
    x_copy(2, far_block, at.x_id, 0, cut).wait_recv()
    x_copy(3, far_block, at.y_id, cut, own_tokens - cut).wait_recv()
    sends[7].start()
    x_copy(4, block_of(y, x, 1 - c), at.core_id).wait_recv()
    x_copy(5, block_of(y, 1 - x, 1 - c), at.core_id).wait_recv()
    x_copy(6, block_of(1 - y, x, 1 - c), at.core_id).wait_recv()
    x_copy(7, block_of(1 - y, 1 - x, 1 - c), at.core_id).wait_recv()

    pair_depth = 4 * depth
    row_step = plane_tokens // 2

    def multiply(pair, add):
        @pl.loop(0, plane_tokens // row_step)
        def _(step):
            rows = aligned(step * row_step, row_step)
            product = jnp.dot(
                x_all[rows, aligned(pair * pair_depth, pair_depth, 128)],
                w_all[aligned(pair * pair_depth, pair_depth), :],
                preferred_element_type=f32,
            )
            acc[rows, :] = acc[rows, :] + product if add else product

    for piece in range(W_PIECES):
        w_line.arrive(1, piece)
    multiply(z // 2, False)
    for distance in range(2, Z_SIZE):
        for piece in range(W_PIECES):
            w_line.arrive(distance, piece)
    multiply(1 - z // 2, True)

    def turned(v, gain, cosine, sine):
        mean_square = jnp.mean(v * v, axis=-1, keepdims=True)
        v = v * lax.rsqrt(mean_square + EPSILON) * gain
        return (v * cosine + pltpu.roll(v, head // 2, 1) * sine).astype(bf16)

    @pl.loop(0, blocks)
    def _(block):
        here = aligned(block * head, head)
        own = aligned(plane_tokens + block * head, head)
        cosine, sine = cos_t[here, :], sin_t[here, :]
        for h in range(2):
            columns = slice(h * head, (h + 1) * head)
            queries[here, columns] = turned(acc[here, columns], gq_ref[...], cosine, sine)
        kv[0, own, :] = turned(acc[here, 2 * head:3 * head], gk_ref[...], cosine, sine)
        kv[1, own, :] = acc[here, 3 * head:4 * head].astype(bf16)

    halo = remote(
        kv.at[:, pl.ds(plane_tokens, plane_tokens)], kv.at[:, pl.ds(0, plane_tokens)],
        halo_send, halo_recv, at.up_id,
    )

    @pl.when(z < Z_SIZE - 1)
    def _():
        halo.start()

    for piece in range(O_PIECES):
        o_line.forward(1, piece)

    @pl.when(z > 0)
    def _():
        halo.wait_recv()

    for piece in range(O_PIECES):
        o_line.forward(2, piece)

    q_step = 2 * own_tokens
    span = LOOKBACK_WINDOW + q_step

    @pl.loop(0, plane_tokens // q_step)
    def _(block):
        rows = aligned(block * q_step, q_step)
        keys = aligned(block * q_step, span)
        gap = q_off[rows, 0:1] - k_off[:, aligned(block * q_step, span, 128)]
        allowed = (gap >= 0) & (gap < LOOKBACK_WINDOW)
        k_rows, v_rows = kv[0, keys, :], kv[1, keys, :]
        place = (block % 2) * 2 * own_tokens + (block // 2) * own_tokens
        for h in range(2):
            columns = slice(h * head, (h + 1) * head)
            scores = lax.dot_general(
                queries[rows, columns], k_rows, (((1,), (1,)), ((), ())), preferred_element_type=f32
            ) * QS ** (-0.5)
            scores = jnp.where(allowed, scores, -1e30)
            weights = jnp.exp(scores - jnp.max(scores, axis=-1, keepdims=True))
            totals = jnp.sum(weights, axis=-1, keepdims=True)
            mixed = jnp.dot(weights.astype(bf16), v_rows, preferred_element_type=f32) / totals
            mixed = mixed.astype(bf16)
            for core in range(2):
                att_own[aligned(core * 4 * own_tokens + place, own_tokens), columns] = (
                    mixed[core * own_tokens:(core + 1) * own_tokens]
                )

    def att_copy(slot, device, recv, half):
        return remote(att_own, att_all.at[half], att_send.at[slot], att_recv.at[recv], device)

    keep_att = pltpu.make_async_copy(att_own, att_all.at[c], local_sem.at[1])

    @pl.when(same)
    def _():
        att_copy(0, at.y_id, 0, c).start()
        keep_att.start()

    @pl.when(jnp.logical_not(same))
    def _():
        att_copy(0, at.diag_id, 1, c).start()
        att_copy(1, at.core_id, 1, c).start()

    @pl.when(same)
    def _():
        keep_att.wait()

    @pl.when(jnp.logical_not(same))
    def _():
        att_copy(0, at.y_id, 0, c).wait_recv()

    att_copy(1, at.core_id, 1, 1 - c).wait_recv()

    planes = [z, z + 1 - 2 * (z % 2), (z + 2) % 4, 3 - z]
    half_tokens = plane_tokens // 2
    x_other = aligned((1 - x) * 2 * own_tokens, 2 * own_tokens)

    def core_copy(step):
        return remote(
            sent_core.at[step], got_core.at[step], core_send.at[step], core_recv.at[step], at.core_id
        )

    def sums_x(step):
        return remote(sent_x.at[step], got_x.at[step], sx_send.at[step], sx_recv.at[step], at.x_id)

    def sums_y(step):
        return remote(sent_y.at[step], got_y.at[step], sy_send.at[step], sy_recv.at[step], at.y_id)

    def product(core, plane):
        rows = aligned(core * half_tokens, half_tokens)
        total = None
        for half in range(2):
            term = lax.dot_general(
                att_all[half, rows, :], wo_all[plane, :, half * 2 * head:(half + 1) * 2 * head],
                (((1,), (1,)), ((), ())), preferred_element_type=f32,
            )
            total = term if total is None else total + term
        return total

    def project(step):
        sent_core[step] = product(1 - c, planes[step]).astype(bf16)
        core_copy(step).start()
        kept[step] = product(c, planes[step])

    def pass_x(step):
        core_copy(step).wait_recv()
        sent_x[step] = (kept[step, x_other, :] + got_core[step, x_other, :].astype(f32)).astype(bf16)
        sums_x(step).start()

    def pass_y(step):
        sums_x(step).wait_recv()

        def total(row):
            mine = aligned(x * 2 * own_tokens + row * own_tokens, own_tokens)
            return (
                kept[step, mine, :] + got_core[step, mine, :].astype(f32)
                + got_x[step, aligned(row * own_tokens, own_tokens), :].astype(f32)
            )

        sent_y[step] = total(1 - y).astype(bf16)
        sums_y(step).start()
        fin[2 * planes[step] + y] = total(y)

    def finish(step):
        sums_y(step).wait_recv()
        fin[2 * planes[step] + 1 - y] = got_y[step].astype(f32)

    for step in range(Z_SIZE):
        if step > 0:
            for piece in range(O_PIECES):
                o_line.arrive(step, piece)
        project(step)
        pass_x(step)
        if step > 0:
            pass_y(step - 1)
    pass_y(Z_SIZE - 1)
    for step in range(Z_SIZE):
        finish(step)

    width = fin.shape[2]
    square = jnp.zeros((own_tokens, 1), f32)
    for block in range(2 * Z_SIZE):
        v = fin[block]
        square = square + jnp.sum(v * v, axis=-1, keepdims=True)
        outs[:, block * width:(block + 1) * width] = v
    scale = lax.rsqrt(square / model + EPSILON)
    q_off[pl.ds(0, own_tokens), :] = jnp.broadcast_to(scale, (own_tokens, head))

    @pl.loop(0, own_tokens // TILE)
    def _(step):
        rows = aligned(step * TILE, TILE)
        out_ref[rows, :] = (
            xs[rows, :].astype(f32) + outs[rows, :] * q_off[rows, 0:1] * gpost_ref[...]
        ).astype(bf16)

    @pl.when(same)
    def _():
        near_copy().wait_send()
        att_copy(0, at.y_id, 0, c).wait_send()

    @pl.when(jnp.logical_not(same))
    def _():
        far_copy(at.y_id).wait_send()
        far_copy(at.diag_id).wait_send()
        att_copy(0, at.diag_id, 1, c).wait_send()
        att_copy(1, at.core_id, 1, c).wait_send()

    for copy in sends:
        copy.wait_send()

    @pl.when(z < Z_SIZE - 1)
    def _():
        halo.wait_send()

    w_line.drain()
    o_line.drain()
    for step in range(Z_SIZE):
        core_copy(step).wait_send()
        sums_x(step).wait_send()
        sums_y(step).wait_send()


def layer(tokens, positions, w_query, key_matrix, value_matrix, w_out, gain_in, gain_query, gain_key, gain_post):
    own_tokens, model = tokens.shape
    depth = w_query.shape[0]
    heads, columns = w_out.shape
    head = HEAD_SIZE
    plane = 8 * own_tokens
    bf16, f32, dma = jnp.bfloat16, jnp.float32, pltpu.SemaphoreType.DMA
    lanes = jnp.arange(head, dtype=jnp.int32) % (head // 2)
    frequency = ROPE_BASE ** (-(lanes.astype(f32) * 2.0) / head)
    vmem, anywhere = pl.BlockSpec(memory_space=pltpu.VMEM), pl.BlockSpec(memory_space=pl.ANY)
    half = plane // 2
    return pl.pallas_call(
        layer_kernel,
        out_shape=jax.ShapeDtypeStruct((own_tokens, model), bf16),
        in_specs=[anywhere] * 5 + [vmem] * 6,
        out_specs=vmem,
        scratch_shapes=[
            pltpu.VMEM((own_tokens, model), bf16),
            pltpu.VMEM((plane, model), bf16),
            pltpu.VMEM((2, depth, 4 * head), bf16),
            pltpu.VMEM((model, 4 * head), bf16),
            pltpu.VMEM((plane, 4 * head), f32),
            pltpu.VMEM((plane, 2 * head), bf16),
            pltpu.VMEM((2, 2 * plane, head), bf16),
            pltpu.VMEM((plane, 2 * head), bf16),
            pltpu.VMEM((2, plane, 2 * head), bf16),
            pltpu.VMEM((heads, columns), bf16),
            pltpu.VMEM((Z_SIZE, columns, heads), bf16),
            pltpu.VMEM((plane, head), f32),
            pltpu.VMEM((plane, head), f32),
            pltpu.VMEM((plane, head), f32),
            pltpu.VMEM((1, 2 * plane), f32),
            pltpu.VMEM((Z_SIZE, half, columns), bf16),
            pltpu.VMEM((Z_SIZE, half, columns), bf16),
            pltpu.VMEM((Z_SIZE, half, columns), f32),
            pltpu.VMEM((Z_SIZE, half // 2, columns), bf16),
            pltpu.VMEM((Z_SIZE, half // 2, columns), bf16),
            pltpu.VMEM((Z_SIZE, half // 4, columns), bf16),
            pltpu.VMEM((Z_SIZE, half // 4, columns), bf16),
            pltpu.VMEM((2 * Z_SIZE, own_tokens, columns), f32),
            pltpu.VMEM((own_tokens, model), f32),
            dma((8,)), dma((2,)), dma((2,)), dma((2,)), dma((8,)), dma((8,)), dma, dma, dma((2,)), dma((2,)),
            *[dma((Z_SIZE,)) for _ in range(6)],
            *line_semaphores(W_PIECES), *line_semaphores(O_PIECES),
        ],
        compiler_params=pltpu.CompilerParams(
            collective_id=0, has_side_effects=True, vmem_limit_bytes=60 * 2**20
        ),
        name="layer",
    )(
        tokens, w_query, key_matrix, value_matrix, w_out,
        gain_in.reshape(1, -1), gain_post.reshape(1, -1),
        gain_query.reshape(1, -1), gain_key.reshape(1, -1),
        positions.reshape(-1, head), frequency.reshape(1, -1),
    )


def attend(query_matrix, projected_keys, projected_values, query_offsets, key_offsets, key_valid):
    scores = jnp.einsum(
        "qkgd,skd->kgqs", query_matrix, projected_keys, preferred_element_type=jnp.float32
    ) * QS ** (-0.5)
    position_gap = query_offsets[:, None] - key_offsets[None, :]
    allowed = key_valid[None, :] & (position_gap >= 0) & (position_gap < LOOKBACK_WINDOW)
    scores = jnp.where(allowed[None, None], scores, -1e30)
    row_max = jnp.max(scores, axis=-1, keepdims=True)
    weights = jnp.where(allowed[None, None], jnp.exp(scores - row_max), 0.0)
    totals = jnp.sum(weights, axis=-1, keepdims=True)
    rounded = weights.astype(jnp.bfloat16)
    mixed = jnp.einsum(
        "kgqs,skd->qkgd", rounded, projected_values, preferred_element_type=jnp.float32
    )
    mixed = mixed / jnp.transpose(totals, (2, 0, 1, 3))
    return mixed.astype(jnp.bfloat16).reshape(query_matrix.shape[0], -1)


def shards(
    tokens,
    positions,
    w_query,
    key_matrix,
    value_matrix,
    w_out,
    gain_in,
    gain_query,
    gain_key,
    gain_post,
):
    if lax.axis_size("ctx") == 2 * Z_SIZE and lax.axis_size("tp") == 4:
        return layer(
            tokens, positions, w_query, key_matrix, value_matrix, w_out,
            gain_in, gain_query, gain_key, gain_post,
        )
    normed = row_norm(tokens.astype(jnp.float32), gain_in).astype(jnp.bfloat16)
    normalized_rows = lax.all_gather(normed, "tp", axis=0, tiled=True)
    weights_in = lax.all_gather(
        jnp.concatenate([w_query, key_matrix, value_matrix], axis=1), "ctx", axis=0, tiled=True
    )
    row_count = normalized_rows.shape[0]
    block_start = lax.axis_index("ctx") * row_count
    offsets_all = positions - positions[0]
    query_offsets = lax.dynamic_slice_in_dim(offsets_all, block_start, row_count, 0)
    query_width, key_width = w_query.shape[1], key_matrix.shape[1]

    def add_rows(weights):
        return jnp.dot(normalized_rows, weights, preferred_element_type=jnp.float32)

    key_value_raw = add_rows(weights_in[:, query_width:])
    query_raw = add_rows(weights_in[:, :query_width])
    unnormed_keys = key_value_raw[:, :key_width]
    value_raw = key_value_raw[:, key_width:]
    key_heads = key_matrix.shape[1] // HEAD_SIZE
    projected_keys = rotate(
        row_norm(unnormed_keys.reshape(row_count, key_heads, HEAD_SIZE), gain_key), query_offsets
    ).astype(jnp.bfloat16)
    projected_values = value_raw.astype(jnp.bfloat16).reshape(row_count, key_heads, HEAD_SIZE)
    own_pair = jnp.stack([projected_keys, projected_values])
    window_blocks = LOOKBACK_WINDOW // row_count
    earlier = [shifted(own_pair, "ctx", steps) for steps in range(window_blocks, 0, -1)]
    window_pair = jnp.concatenate(earlier + [own_pair], axis=1)
    query_heads = w_query.shape[1] // HEAD_SIZE
    query_matrix = rotate(
        row_norm(query_raw.reshape(row_count, query_heads, HEAD_SIZE), gain_query), query_offsets
    ).astype(jnp.bfloat16)
    query_matrix = query_matrix.reshape(row_count, key_heads, query_heads // key_heads, HEAD_SIZE)
    padded_offsets = jnp.concatenate(
        [jnp.zeros((LOOKBACK_WINDOW,), jnp.int32), offsets_all], axis=0
    )
    key_offsets = lax.dynamic_slice_in_dim(
        padded_offsets, block_start, LOOKBACK_WINDOW + row_count, 0
    )
    key_valid = (
        block_start + jnp.arange(LOOKBACK_WINDOW + row_count, dtype=jnp.int32) >= LOOKBACK_WINDOW
    )
    attended = attend(
        query_matrix, window_pair[0], window_pair[1], query_offsets, key_offsets, key_valid
    )
    projected = jnp.dot(
        attended,
        lax.all_gather(w_out, "ctx", axis=1, tiled=True),
        preferred_element_type=jnp.float32,
    )
    summed = lax.psum_scatter(
        projected.astype(jnp.bfloat16), "tp", scatter_dimension=0, tiled=True
    ).astype(jnp.float32)
    return (tokens.astype(jnp.float32) + row_norm(summed, gain_post)).astype(jnp.bfloat16)


def solution(mesh):
    in_specs = (
        P(("ctx", "tp"), None),
        P(),
        P("ctx", "tp"),
        P("ctx", "tp"),
        P("ctx", "tp"),
        P("tp", "ctx"),
        P(),
        P(),
        P(),
        P(),
    )
    out_specs = P(("ctx", "tp"), None)
    return jax.shard_map(shards, mesh=mesh, in_specs=in_specs, out_specs=out_specs, check_vma=False)
```

```python
import jax
import jax.numpy as jnp
import numpy as np
from jax import lax
from jax.experimental import pallas as pl
from jax.experimental.pallas import tpu as pltpu
from jax.sharding import PartitionSpec as P

HEAD_SIZE = 128
QS = 168
LOOKBACK_WINDOW = 1024


EPSILON = 1e-06
ROPE_BASE = 10000.0


def shifted(value, axis, steps):
    count = lax.axis_size(axis)
    leading, last = (max(0, -steps), min(count, count - steps))
    return lax.ppermute(value, axis, [(source, source + steps) for source in range(leading, last)])


def row_norm(values, scales):
    mean_square = jnp.mean(values * values, axis=-1, keepdims=True)
    return values * lax.rsqrt(mean_square + EPSILON) * scales


def rotate(head_rows, offsets):
    half_dim = head_rows.shape[-1] // 2
    frequency = ROPE_BASE ** (
        -(jnp.arange(half_dim, dtype=jnp.float32) * 2.0) / head_rows.shape[-1]
    )
    angles = offsets.astype(jnp.float32)[:, None] * frequency[None, :]
    cosine = jnp.cos(angles)[:, None, :]
    sine_wave = jnp.sin(angles)[:, None, :]
    first_half = head_rows[..., :half_dim]
    second_half = head_rows[..., half_dim:]
    return jnp.concatenate(
        [
            first_half * cosine - second_half * sine_wave,
            second_half * cosine + first_half * sine_wave,
        ],
        axis=-1,
    )


Z_SIZE = 4
TILE = 16
W_PIECES = 4
O_PIECES = 3
O_CUTS = (0, 80, 160, 176)
MATES = [(i // 4, i // 2 % 2, i % 2) for i in range(1, 8)]
MESH = pl.DeviceIdType.MESH
FAR_KEY = 1e9


def remote(source, target, send, recv, device):
    return pltpu.make_async_remote_copy(
        src_ref=source, dst_ref=target, send_sem=send, recv_sem=recv,
        device_id=device, device_id_type=MESH,
    )


def aligned(value, size, step=TILE):
    return pl.ds(pl.multiple_of(value, step), size)


class Places:
    def __init__(self):
        self.ctx = lax.axis_index("ctx")
        self.tp = lax.axis_index("tp")
        self.z, self.y = self.ctx // 2, self.ctx % 2
        self.x, self.c = self.tp // 2, self.tp % 2
        self.core_id = self.mate(0, 0, 1)
        self.x_id = self.mate(0, 1, 0)
        self.y_id = self.mate(1, 0, 0)
        self.diag_id = self.mate(1, 0, 1)
        self.up_id = (self.ctx + 2, self.tp)
        self.down_id = (self.ctx - 2, self.tp)

    def mate(self, dy, dx, dc):
        row, column, core = ((v + d) % 2 for v, d in ((self.y, dy), (self.x, dx), (self.c, dc)))
        return (self.z * 2 + row, column * 2 + core)

    def greet(self):
        barrier = pltpu.get_barrier_semaphore()

        def signal(target):
            pl.semaphore_signal(barrier, inc=1, device_id=target, device_id_type=MESH)

        for dy, dx, dc in MATES:
            signal(self.mate(dy, dx, dc))

        @pl.when(self.z < Z_SIZE - 1)
        def _():
            signal(self.up_id)

        @pl.when(self.z > 0)
        def _():
            signal(self.down_id)

    def meet(self):
        middle = ((self.z + 1) // 2) % 2
        pl.semaphore_wait(pltpu.get_barrier_semaphore(), 8 + middle)


class Line:
    def __init__(self, places, piece_ref, pieces, sems, guard=None):
        self.at, self.piece_ref, self.pieces = places, piece_ref, pieces
        self.guard = guard or (lambda piece, condition: condition)
        self.up_send, self.down_send, self.below, self.above = sems

    def copy(self, plane, distance, piece, upward):
        ref = self.piece_ref(plane, piece)
        slot = distance * self.pieces + piece
        if upward:
            return remote(ref, ref, self.up_send.at[slot], self.below.at[slot], self.at.up_id)
        return remote(ref, ref, self.down_send.at[slot], self.above.at[slot], self.at.down_id)

    def send_own(self, piece):
        z = self.at.z

        @pl.when(self.guard(piece, z < Z_SIZE - 1))
        def _():
            self.copy(z, 0, piece, True).start()

        @pl.when(self.guard(piece, z > 0))
        def _():
            self.copy(z, 0, piece, False).start()

    def forward(self, distance, piece):
        z = self.at.z
        if distance == Z_SIZE - 1:
            return

        @pl.when(self.guard(piece, (z >= distance) & (z < Z_SIZE - 1)))
        def _():
            self.copy(z - distance, distance - 1, piece, True).wait_recv()
            self.copy(z - distance, distance, piece, True).start()

        @pl.when(self.guard(piece, (z + distance < Z_SIZE) & (z > 0)))
        def _():
            self.copy(z + distance, distance - 1, piece, False).wait_recv()
            self.copy(z + distance, distance, piece, False).start()

    def arrive(self, distance, piece):
        z = self.at.z

        @pl.when(self.guard(piece, z == Z_SIZE - 1))
        def _():
            self.copy(z - distance, distance - 1, piece, True).wait_recv()

        @pl.when(self.guard(piece, z == 0))
        def _():
            self.copy(z + distance, distance - 1, piece, False).wait_recv()

    def drain(self, upward):
        z = self.at.z
        for distance in range(Z_SIZE - 1):
            for piece in range(self.pieces):
                if upward:
                    plane, sent = z - distance, (z < Z_SIZE - 1) & (z >= distance)
                else:
                    plane, sent = z + distance, (z > 0) & (z + distance < Z_SIZE)

                @pl.when(self.guard(piece, sent))
                def _():
                    self.copy(plane, distance, piece, upward).wait_send()


class PlaneGather:
    def __init__(self, places, block_ref, send, recv):
        self.at, self.block_ref, self.send, self.recv = places, block_ref, send, recv

    def copy(self, slot):
        device, (dy, dx), part = (
            (self.at.x_id, (0, 0), None), (self.at.y_id, (0, 0), None),
            (self.at.x_id, (1, 0), 0), (self.at.y_id, (0, 1), 1),
            (self.at.core_id, (0, 0), None), (self.at.core_id, (0, 1), None),
            (self.at.core_id, (1, 0), None), (self.at.core_id, (1, 1), None),
        )[slot]
        ref = self.block_ref((self.at.y + dy) % 2, (self.at.x + dx) % 2, self.at.c, part)
        return remote(ref, ref, self.send.at[slot], self.recv.at[slot], device)

    def start(self, *slots):
        for slot in slots:
            self.copy(slot).start()

    def arrive(self, *slots):
        for slot in slots:
            (dy, dx, dc), part = (
                ((0, 1, 0), None), ((1, 0, 0), None), ((1, 1, 0), 0), ((1, 1, 0), 1),
                ((0, 0, 1), None), ((0, 1, 1), None), ((1, 0, 1), None), ((1, 1, 1), None),
            )[slot]
            ref = self.block_ref(
                (self.at.y + dy) % 2, (self.at.x + dx) % 2, (self.at.c + dc) % 2, part
            )
            remote(ref, ref, self.send.at[slot], self.recv.at[slot], self.at.core_id).wait_recv()

    def drain(self):
        for slot in range(8):
            self.copy(slot).wait_send()


def line_semaphores(pieces):
    return [pltpu.SemaphoreType.DMA(((Z_SIZE - 1) * pieces,)) for _ in range(4)]


def layer_kernel(
    tok_ref, wq_ref, wk_ref, wv_ref, wo_ref, gin_ref, gpost_ref, gq_ref, gk_ref, pos_ref, freq_ref,
    out_ref,
    xs, x_all, ws, w_all, acc, queries, kv, att_all, wo_own, wo_all, gin, gpost,
    cos_t, sin_t, q_off, k_off, result, got, turned_out,
    stage_sem, local_sem, w_send, w_recv, x_send, x_recv, halo_send, halo_recv, att_send, att_recv,
    o_send, o_recv, r_send, r_recv,
    *line_sems,
):
    at = Places()
    z, y, x, c = at.z, at.y, at.x, at.c
    same = c == y
    depth = wq_ref.shape[0]
    own_tokens, model = xs.shape
    plane_tokens = x_all.shape[0]
    head = HEAD_SIZE
    f32, bf16 = jnp.float32, jnp.bfloat16
    at.greet()

    q_half, k_half = 2 * head, head
    loads = []
    for half in range(2):
        for ref, begin, width in ((wq_ref, 0, q_half), (wk_ref, q_half, k_half), (wv_ref, q_half + k_half, k_half)):
            loads.append(pltpu.make_async_copy(
                ref.at[:, pl.ds(half * width, width)],
                ws.at[half, :, pl.ds(begin, width)],
                stage_sem.at[len(loads)],
            ))
    tok_load = pltpu.make_async_copy(tok_ref, xs, stage_sem.at[6])
    wo_load = pltpu.make_async_copy(wo_ref, wo_own, stage_sem.at[7])
    for copy in loads + [tok_load, wo_load]:
        copy.start()
    for copy in loads:
        copy.wait()
    at.meet()

    def block_rows(plane, row):
        return w_all.at[aligned((plane * 2 + row) * depth, depth)]

    def near_copy():
        return remote(ws.at[1 - c], block_rows(z, y), w_send.at[0], w_recv.at[0], at.core_id)

    def far_copy(target):
        block = block_rows(z, y) if target is not None else block_rows(z, 1 - y)
        device = at.y_id if target is None else target
        if target is at.diag_id:
            return remote(ws.at[1 - c], block, w_send.at[1], w_recv.at[1], device)
        return remote(ws.at[c], block, w_send.at[0], w_recv.at[1], device)

    own_block = pltpu.make_async_copy(ws.at[c], block_rows(z, y), local_sem.at[0])

    @pl.when(same)
    def _():
        near_copy().start()
        own_block.start()

    @pl.when(jnp.logical_not(same))
    def _():
        far_copy(at.y_id).start()
        far_copy(at.diag_id).start()

    half_rows = depth // 2

    def w_piece(plane, piece):
        row = at.y if piece < 2 else 1 - at.y
        return w_all.at[aligned((plane * 2 + row) * depth + (piece % 2) * half_rows, half_rows)]

    def o_piece(plane, piece):
        return wo_all.at[plane, pl.ds(O_CUTS[piece], O_CUTS[piece + 1] - O_CUTS[piece])]

    w_line = Line(at, w_piece, W_PIECES, line_sems[:4])
    o_line = Line(
        at, o_piece, O_PIECES, line_sems[4:],
        lambda piece, condition: condition & (c == 1) if piece == O_PIECES - 1 else condition,
    )

    @pl.when(same)
    def _():
        own_block.wait()

    @pl.when(jnp.logical_not(same))
    def _():
        near_copy().wait_recv()

    for piece in range(2):
        w_line.send_own(piece)

    def block_of(row, column, core):
        return (row * 4 + column * 2 + core) * own_tokens

    tok_load.wait()
    gin[...] = gin_ref[...].reshape(1, model)
    gpost[...] = gpost_ref[...].reshape(1, model)
    own_begin = block_of(y, x, c)

    @pl.loop(0, own_tokens // TILE)
    def _(step):
        v = xs[aligned(step * TILE, TILE), :].astype(f32)
        mean_square = jnp.mean(v * v, axis=-1, keepdims=True)
        x_all[aligned(own_begin + step * TILE, TILE), :] = (
            v * lax.rsqrt(mean_square + EPSILON) * gin[...]
        ).astype(bf16)

    cut = own_tokens * 3 // 4

    def x_block(row, column, core, part):
        begin, size = ((0, own_tokens), (0, cut), (cut, own_tokens - cut))[0 if part is None else part + 1]
        return x_all.at[aligned(block_of(row, column, core) + begin, size)]

    tokens = PlaneGather(at, x_block, x_send, x_recv)
    tokens.start(0, 1, 4)

    o_rows = O_CUTS[-1]
    o_width = wo_own.shape[1]

    def o_copy(slot):
        dx, dc = ((0, 1), (1, 0), (1, 1))[slot]
        part = (x + dx) % 2 * 2 + (c + dc) % 2
        begin = part * (depth // TILE) // 4 * TILE
        return remote(
            wo_own.at[aligned(begin, o_rows)],
            wo_all.at[z, :, aligned((x * 2 + c) * o_width, o_width, 128)],
            o_send.at[slot], o_recv.at[slot], at.mate(0, dx, dc),
        )

    def o_arrive(slot):
        dx, dc = ((0, 1), (1, 0), (1, 1))[slot]
        part = (x + dx) % 2 * 2 + (c + dc) % 2
        block = wo_all.at[z, :, aligned(part * o_width, o_width, 128)]
        remote(block, block, o_send.at[slot], o_recv.at[slot], at.mate(0, dx, dc)).wait_recv()

    wo_load.wait()
    for slot in range(3):
        o_copy(slot).start()
    own_part = x * 2 + c
    keep_o = pltpu.make_async_copy(
        wo_own.at[aligned(own_part * (depth // TILE) // 4 * TILE, o_rows)],
        wo_all.at[z, :, aligned(own_part * o_width, o_width, 128)],
        local_sem.at[1],
    )
    keep_o.start()

    far_copy(None).wait_recv()
    for piece in range(2, W_PIECES):
        w_line.send_own(piece)

    first = pos_ref[0:1, 0:1]
    blocks = plane_tokens // head

    @pl.loop(0, blocks)
    def _(block):
        row = (pos_ref[pl.ds(z * blocks + block, 1), :] - first).astype(f32)
        column = jnp.broadcast_to(row, (head, head)).T
        here = aligned(block * head, head)
        q_off[here, :] = column
        angles = column * freq_ref[...]
        cos_t[here, :] = jnp.cos(angles)
        lane = lax.broadcasted_iota(jnp.int32, (head, head), 1)
        sine = jnp.sin(angles)
        sin_t[here, :] = jnp.where(lane < head // 2, -sine, sine)

    for block in range(2 * blocks):
        index = jnp.maximum((z - 1) * blocks + block, 0)
        row = (pos_ref[pl.ds(index, 1), :] - first).astype(f32)
        if block < blocks:
            row = jnp.where(z > 0, row, FAR_KEY)
        k_off[:, block * head:(block + 1) * head] = row

    @pl.when(z == 0)
    def _():
        kv[:, pl.ds(0, plane_tokens), :] = jnp.zeros((2, plane_tokens, head), bf16)

    for piece in range(W_PIECES):
        w_line.forward(1, piece)
    tokens.arrive(0)
    tokens.start(3, 5)
    tokens.arrive(1)
    tokens.start(2, 6)
    for piece in range(W_PIECES):
        w_line.forward(2, piece)
    tokens.arrive(2, 3)
    tokens.start(7)
    tokens.arrive(4, 5, 6, 7)

    pair_depth = 4 * depth
    row_step = plane_tokens // 2

    def multiply(pair, add):
        @pl.loop(0, plane_tokens // row_step)
        def _(step):
            rows = aligned(step * row_step, row_step)
            product = jnp.dot(
                x_all[rows, aligned(pair * pair_depth, pair_depth, 128)],
                w_all[aligned(pair * pair_depth, pair_depth), :],
                preferred_element_type=f32,
            )
            acc[rows, :] = acc[rows, :] + product if add else product

    for piece in range(W_PIECES):
        w_line.arrive(1, piece)
    multiply(z // 2, False)
    for distance in range(2, Z_SIZE):
        for piece in range(W_PIECES):
            w_line.arrive(distance, piece)
    multiply(1 - z // 2, True)

    def turned(v, gain, cosine, sine):
        mean_square = jnp.mean(v * v, axis=-1, keepdims=True)
        v = v * lax.rsqrt(mean_square + EPSILON) * gain
        return (v * cosine + pltpu.roll(v, head // 2, 1) * sine).astype(bf16)

    @pl.loop(0, blocks)
    def _(block):
        here = aligned(block * head, head)
        own = aligned(plane_tokens + block * head, head)
        cosine, sine = cos_t[here, :], sin_t[here, :]
        for h in range(2):
            columns = slice(h * head, (h + 1) * head)
            queries[here, columns] = turned(acc[here, columns], gq_ref[...], cosine, sine)
        kv[0, own, :] = turned(acc[here, 2 * head:3 * head], gk_ref[...], cosine, sine)
        kv[1, own, :] = acc[here, 3 * head:4 * head].astype(bf16)

    halo = remote(
        kv.at[:, pl.ds(plane_tokens, plane_tokens)], kv.at[:, pl.ds(0, plane_tokens)],
        halo_send, halo_recv, at.up_id,
    )

    w_line.drain(True)

    @pl.when(z < Z_SIZE - 1)
    def _():
        halo.start()

    w_line.drain(False)
    keep_o.wait()
    for slot in range(3):
        o_arrive(slot)
    for piece in range(O_PIECES):
        o_line.send_own(piece)
    for piece in range(O_PIECES):
        o_line.forward(1, piece)

    @pl.when(z > 0)
    def _():
        halo.wait_recv()

    for piece in range(O_PIECES):
        o_line.forward(2, piece)

    width = 2 * head

    def att_block(row, column, core, part):
        half = plane_tokens // 2
        begin, size = ((0, plane_tokens), (0, half), (half, half))[0 if part is None else part + 1]
        return att_all.at[
            pl.ds(begin, size), aligned((column * 4 + row * 2 + core) * width, width, 128)
        ]

    attended = PlaneGather(at, att_block, att_send, att_recv)
    own_heads = (x * 4 + y * 2 + c) * width

    q_step = 2 * own_tokens
    span = LOOKBACK_WINDOW + q_step

    @pl.loop(0, plane_tokens // q_step)
    def _(block):
        rows = aligned(block * q_step, q_step)
        keys = aligned(block * q_step, span)
        gap = q_off[rows, 0:1] - k_off[:, aligned(block * q_step, span, 128)]
        allowed = (gap >= 0) & (gap < LOOKBACK_WINDOW)
        k_rows, v_rows = kv[0, keys, :], kv[1, keys, :]
        for h in range(2):
            columns = slice(h * head, (h + 1) * head)
            scores = lax.dot_general(
                queries[rows, columns], k_rows, (((1,), (1,)), ((), ())), preferred_element_type=f32
            ) * QS ** (-0.5)
            scores = jnp.where(allowed, scores, -1e30)
            weights = jnp.exp(scores - jnp.max(scores, axis=-1, keepdims=True))
            totals = jnp.sum(weights, axis=-1, keepdims=True)
            mixed = jnp.dot(weights.astype(bf16), v_rows, preferred_element_type=f32) / totals
            att_all[rows, aligned(own_heads + h * head, head, 128)] = mixed.astype(bf16)

    attended.start(0, 1, 4)
    attended.arrive(0)
    attended.start(3, 5)
    attended.arrive(1)
    attended.start(2, 6)
    attended.arrive(2, 3)
    attended.start(7)
    attended.arrive(4, 5, 6, 7)

    planes = [z, z + 1 - 2 * (z % 2), (z + 2) % 4, 3 - z]
    own_index = y * 4 + x * 2 + c

    def r_copy(step, mate):
        dy, dx, dc = MATES[mate]
        owner = (y + dy) % 2 * 4 + (x + dx) % 2 * 2 + (c + dc) % 2
        slot = step * len(MATES) + mate
        return remote(
            result.at[step, owner], got.at[step, own_index], r_send.at[slot], r_recv.at[slot],
            at.mate(dy, dx, dc),
        )

    def r_arrive(step, mate):
        dy, dx, dc = MATES[mate]
        owner = (y + dy) % 2 * 4 + (x + dx) % 2 * 2 + (c + dc) % 2
        slot = step * len(MATES) + mate
        block = got.at[step, owner]
        remote(block, block, r_send.at[slot], r_recv.at[slot], at.core_id).wait_recv()

    def project(step):
        sums = lax.dot_general(
            wo_all[planes[step]], att_all[...], (((1,), (1,)), ((), ())), preferred_element_type=f32
        ).astype(bf16)
        for owner in range(2 * blocks // 2):
            result[step, owner] = sums[:, owner * own_tokens:(owner + 1) * own_tokens]
        for mate in range(len(MATES)):
            r_copy(step, mate).start()
        got[step, own_index] = result[step, own_index]

    def finish(step, square):
        for mate in range(len(MATES)):
            r_arrive(step, mate)
        for owner in range(8):
            row, part = owner // 4, owner % 4
            begin = part * (depth // TILE) // 4 * TILE
            size = (part + 1) * (depth // TILE) // 4 * TILE - begin
            v = got[step, owner, :size].astype(f32)
            turned_out[aligned((planes[step] * 2 + row) * depth + begin, size), :] = v
            square = square + jnp.sum(v * v, axis=0, keepdims=True)
        return square

    square = jnp.zeros((1, own_tokens), f32)
    for step in range(Z_SIZE):
        if step > 0:
            for piece in range(O_PIECES):
                o_line.arrive(step, piece)
        project(step)
        if step > 0:
            square = finish(step - 1, square)
    square = finish(Z_SIZE - 1, square)

    scale = lax.rsqrt(square / model + EPSILON)
    for begin in range(0, model, head):
        columns = slice(begin, begin + head)
        normed = (turned_out[columns, :] * scale).T * gpost[:, columns]
        out_ref[:, columns] = (xs[:, columns].astype(f32) + normed).astype(bf16)

    @pl.when(same)
    def _():
        near_copy().wait_send()

    @pl.when(jnp.logical_not(same))
    def _():
        far_copy(at.y_id).wait_send()
        far_copy(at.diag_id).wait_send()

    tokens.drain()
    attended.drain()
    for slot in range(3):
        o_copy(slot).wait_send()

    @pl.when(z < Z_SIZE - 1)
    def _():
        halo.wait_send()

    o_line.drain(True)
    o_line.drain(False)
    for step in range(Z_SIZE):
        for mate in range(len(MATES)):
            r_copy(step, mate).wait_send()


def layer(tokens, positions, w_query, key_matrix, value_matrix, w_out_t, gain_in, gain_query, gain_key, gain_post):
    own_tokens, model = tokens.shape
    depth = w_query.shape[0]
    columns, heads = w_out_t.shape
    head = HEAD_SIZE
    plane = 8 * own_tokens
    bf16, f32, dma = jnp.bfloat16, jnp.float32, pltpu.SemaphoreType.DMA
    frequency = jnp.asarray(ROPE_BASE ** (-2.0 * (np.arange(head) % (head // 2)) / head), f32)
    vmem, anywhere = pl.BlockSpec(memory_space=pltpu.VMEM), pl.BlockSpec(memory_space=pl.ANY)
    o_rows = O_CUTS[-1]
    return pl.pallas_call(
        layer_kernel,
        out_shape=jax.ShapeDtypeStruct((own_tokens, model), bf16),
        in_specs=[anywhere] * 5 + [vmem] * 6,
        out_specs=vmem,
        scratch_shapes=[
            pltpu.VMEM((own_tokens, model), bf16),
            pltpu.VMEM((plane, model), bf16),
            pltpu.VMEM((2, depth, 4 * head), bf16),
            pltpu.VMEM((model, 4 * head), bf16),
            pltpu.VMEM((plane, 4 * head), f32),
            pltpu.VMEM((plane, 2 * head), bf16),
            pltpu.VMEM((2, 2 * plane, head), bf16),
            pltpu.VMEM((plane, 4 * heads), bf16),
            pltpu.VMEM((columns, heads), bf16),
            pltpu.VMEM((Z_SIZE, o_rows, 4 * heads), bf16),
            pltpu.VMEM((1, model), f32),
            pltpu.VMEM((1, model), f32),
            pltpu.VMEM((plane, head), f32),
            pltpu.VMEM((plane, head), f32),
            pltpu.VMEM((plane, head), f32),
            pltpu.VMEM((1, 2 * plane), f32),
            pltpu.VMEM((Z_SIZE, 8, o_rows, own_tokens), bf16),
            pltpu.VMEM((Z_SIZE, 8, o_rows, own_tokens), bf16),
            pltpu.VMEM((model, own_tokens), f32),
            dma((8,)), dma((2,)), dma((2,)), dma((2,)), dma((8,)), dma((8,)), dma, dma, dma((8,)), dma((8,)),
            dma((3,)), dma((3,)), dma((7 * Z_SIZE,)), dma((7 * Z_SIZE,)),
            *line_semaphores(W_PIECES), *line_semaphores(O_PIECES),
        ],
        compiler_params=pltpu.CompilerParams(
            collective_id=0, has_side_effects=True, vmem_limit_bytes=60 * 2**20
        ),
        name="layer",
    )(
        tokens, w_query, key_matrix, value_matrix, w_out_t,
        gain_in, gain_post,
        gain_query.reshape(1, -1), gain_key.reshape(1, -1),
        positions.reshape(-1, head), frequency.reshape(1, -1),
    )


def attend(query_matrix, projected_keys, projected_values, query_offsets, key_offsets, key_valid):
    scores = jnp.einsum(
        "qkgd,skd->kgqs", query_matrix, projected_keys, preferred_element_type=jnp.float32
    ) * QS ** (-0.5)
    position_gap = query_offsets[:, None] - key_offsets[None, :]
    allowed = key_valid[None, :] & (position_gap >= 0) & (position_gap < LOOKBACK_WINDOW)
    scores = jnp.where(allowed[None, None], scores, -1e30)
    row_max = jnp.max(scores, axis=-1, keepdims=True)
    weights = jnp.where(allowed[None, None], jnp.exp(scores - row_max), 0.0)
    totals = jnp.sum(weights, axis=-1, keepdims=True)
    rounded = weights.astype(jnp.bfloat16)
    mixed = jnp.einsum(
        "kgqs,skd->qkgd", rounded, projected_values, preferred_element_type=jnp.float32
    )
    mixed = mixed / jnp.transpose(totals, (2, 0, 1, 3))
    return mixed.astype(jnp.bfloat16).reshape(query_matrix.shape[0], -1)


def shards(
    tokens,
    positions,
    w_query,
    key_matrix,
    value_matrix,
    w_out,
    gain_in,
    gain_query,
    gain_key,
    gain_post,
):
    if lax.axis_size("ctx") == 2 * Z_SIZE and lax.axis_size("tp") == 4:
        return layer(
            tokens, positions, w_query, key_matrix, value_matrix, w_out.T,
            gain_in, gain_query, gain_key, gain_post,
        )
    normed = row_norm(tokens.astype(jnp.float32), gain_in).astype(jnp.bfloat16)
    normalized_rows = lax.all_gather(normed, "tp", axis=0, tiled=True)
    weights_in = lax.all_gather(
        jnp.concatenate([w_query, key_matrix, value_matrix], axis=1), "ctx", axis=0, tiled=True
    )
    row_count = normalized_rows.shape[0]
    block_start = lax.axis_index("ctx") * row_count
    offsets_all = positions - positions[0]
    query_offsets = lax.dynamic_slice_in_dim(offsets_all, block_start, row_count, 0)
    query_width, key_width = w_query.shape[1], key_matrix.shape[1]

    def add_rows(weights):
        return jnp.dot(normalized_rows, weights, preferred_element_type=jnp.float32)

    key_value_raw = add_rows(weights_in[:, query_width:])
    query_raw = add_rows(weights_in[:, :query_width])
    unnormed_keys = key_value_raw[:, :key_width]
    value_raw = key_value_raw[:, key_width:]
    key_heads = key_matrix.shape[1] // HEAD_SIZE
    projected_keys = rotate(
        row_norm(unnormed_keys.reshape(row_count, key_heads, HEAD_SIZE), gain_key), query_offsets
    ).astype(jnp.bfloat16)
    projected_values = value_raw.astype(jnp.bfloat16).reshape(row_count, key_heads, HEAD_SIZE)
    own_pair = jnp.stack([projected_keys, projected_values])
    window_blocks = LOOKBACK_WINDOW // row_count
    earlier = [shifted(own_pair, "ctx", steps) for steps in range(window_blocks, 0, -1)]
    window_pair = jnp.concatenate(earlier + [own_pair], axis=1)
    query_heads = w_query.shape[1] // HEAD_SIZE
    query_matrix = rotate(
        row_norm(query_raw.reshape(row_count, query_heads, HEAD_SIZE), gain_query), query_offsets
    ).astype(jnp.bfloat16)
    query_matrix = query_matrix.reshape(row_count, key_heads, query_heads // key_heads, HEAD_SIZE)
    padded_offsets = jnp.concatenate(
        [jnp.zeros((LOOKBACK_WINDOW,), jnp.int32), offsets_all], axis=0
    )
    key_offsets = lax.dynamic_slice_in_dim(
        padded_offsets, block_start, LOOKBACK_WINDOW + row_count, 0
    )
    key_valid = (
        block_start + jnp.arange(LOOKBACK_WINDOW + row_count, dtype=jnp.int32) >= LOOKBACK_WINDOW
    )
    attended = attend(
        query_matrix, window_pair[0], window_pair[1], query_offsets, key_offsets, key_valid
    )
    projected = jnp.dot(
        attended,
        lax.all_gather(w_out, "ctx", axis=1, tiled=True),
        preferred_element_type=jnp.float32,
    )
    summed = lax.psum_scatter(
        projected.astype(jnp.bfloat16), "tp", scatter_dimension=0, tiled=True
    ).astype(jnp.float32)
    return (tokens.astype(jnp.float32) + row_norm(summed, gain_post)).astype(jnp.bfloat16)


def solution(mesh):
    in_specs = (
        P(("ctx", "tp"), None),
        P(),
        P("ctx", "tp"),
        P("ctx", "tp"),
        P("ctx", "tp"),
        P("tp", "ctx"),
        P(),
        P(),
        P(),
        P(),
    )
    out_specs = P(("ctx", "tp"), None)
    return jax.shard_map(shards, mesh=mesh, in_specs=in_specs, out_specs=out_specs, check_vma=False)
```

```python
import jax
import jax.numpy as jnp
import numpy as np
from jax import lax
from jax.experimental import pallas as pl
from jax.experimental.pallas import tpu as pltpu
from jax.sharding import PartitionSpec as P

HEAD_SIZE = 128
QS = 168
LOOKBACK_WINDOW = 1024


EPSILON = 1e-06
ROPE_BASE = 10000.0


def shifted(value, axis, steps):
    count = lax.axis_size(axis)
    leading, last = (max(0, -steps), min(count, count - steps))
    return lax.ppermute(value, axis, [(source, source + steps) for source in range(leading, last)])


def row_norm(values, scales):
    mean_square = jnp.mean(values * values, axis=-1, keepdims=True)
    return values * lax.rsqrt(mean_square + EPSILON) * scales


def rotate(head_rows, offsets):
    half_dim = head_rows.shape[-1] // 2
    frequency = ROPE_BASE ** (
        -(jnp.arange(half_dim, dtype=jnp.float32) * 2.0) / head_rows.shape[-1]
    )
    angles = offsets.astype(jnp.float32)[:, None] * frequency[None, :]
    cosine = jnp.cos(angles)[:, None, :]
    sine_wave = jnp.sin(angles)[:, None, :]
    first_half = head_rows[..., :half_dim]
    second_half = head_rows[..., half_dim:]
    return jnp.concatenate(
        [
            first_half * cosine - second_half * sine_wave,
            second_half * cosine + first_half * sine_wave,
        ],
        axis=-1,
    )


Z_SIZE = 4
TILE = 16
W_PIECES = 4
O_PIECES = 3
O_CUTS = (0, 80, 160, 176)
MATES = [(i // 4, i // 2 % 2, i % 2) for i in range(1, 8)]
MESH = pl.DeviceIdType.MESH
FAR_KEY = 1e9


def remote(source, target, send, recv, device):
    return pltpu.make_async_remote_copy(
        src_ref=source, dst_ref=target, send_sem=send, recv_sem=recv,
        device_id=device, device_id_type=MESH,
    )


def aligned(value, size, step=TILE):
    return pl.ds(pl.multiple_of(value, step), size)


class Places:
    def __init__(self):
        self.ctx = lax.axis_index("ctx")
        self.tp = lax.axis_index("tp")
        self.z, self.y = self.ctx // 2, self.ctx % 2
        self.x, self.c = self.tp // 2, self.tp % 2
        self.core_id = self.mate(0, 0, 1)
        self.x_id = self.mate(0, 1, 0)
        self.y_id = self.mate(1, 0, 0)
        self.diag_id = self.mate(1, 0, 1)
        self.up_id = (self.ctx + 2, self.tp)
        self.down_id = (self.ctx - 2, self.tp)

    def mate(self, dy, dx, dc):
        row, column, core = ((v + d) % 2 for v, d in ((self.y, dy), (self.x, dx), (self.c, dc)))
        return (self.z * 2 + row, column * 2 + core)

    def greet(self):
        barrier = pltpu.get_barrier_semaphore()

        def signal(target):
            pl.semaphore_signal(barrier, inc=1, device_id=target, device_id_type=MESH)

        for dy, dx, dc in MATES:
            signal(self.mate(dy, dx, dc))

        @pl.when(self.z < Z_SIZE - 1)
        def _():
            signal(self.up_id)

        @pl.when(self.z > 0)
        def _():
            signal(self.down_id)

    def meet(self):
        middle = ((self.z + 1) // 2) % 2
        pl.semaphore_wait(pltpu.get_barrier_semaphore(), 8 + middle)


class Line:
    def __init__(self, places, piece_ref, pieces, sems, guard=None):
        self.at, self.piece_ref, self.pieces = places, piece_ref, pieces
        self.guard = guard or (lambda piece, condition: condition)
        self.up_send, self.down_send, self.below, self.above = sems

    def copy(self, plane, distance, piece, upward):
        ref = self.piece_ref(plane, piece)
        slot = distance * self.pieces + piece
        if upward:
            return remote(ref, ref, self.up_send.at[slot], self.below.at[slot], self.at.up_id)
        return remote(ref, ref, self.down_send.at[slot], self.above.at[slot], self.at.down_id)

    def send_own(self, piece, upward=True, downward=True):
        z = self.at.z
        if upward:
            @pl.when(self.guard(piece, z < Z_SIZE - 1))
            def _():
                self.copy(z, 0, piece, True).start()

        if downward:
            @pl.when(self.guard(piece, z > 0))
            def _():
                self.copy(z, 0, piece, False).start()

    def forward(self, distance, piece):
        z = self.at.z
        if distance == Z_SIZE - 1:
            return

        @pl.when(self.guard(piece, (z >= distance) & (z < Z_SIZE - 1)))
        def _():
            self.copy(z - distance, distance - 1, piece, True).wait_recv()
            self.copy(z - distance, distance, piece, True).start()

        @pl.when(self.guard(piece, (z + distance < Z_SIZE) & (z > 0)))
        def _():
            self.copy(z + distance, distance - 1, piece, False).wait_recv()
            self.copy(z + distance, distance, piece, False).start()

    def arrive(self, distance, piece):
        z = self.at.z

        @pl.when(self.guard(piece, z == Z_SIZE - 1))
        def _():
            self.copy(z - distance, distance - 1, piece, True).wait_recv()

        @pl.when(self.guard(piece, z == 0))
        def _():
            self.copy(z + distance, distance - 1, piece, False).wait_recv()

    def drain(self, upward):
        z = self.at.z
        for distance in range(Z_SIZE - 1):
            for piece in range(self.pieces):
                if upward:
                    plane, sent = z - distance, (z < Z_SIZE - 1) & (z >= distance)
                else:
                    plane, sent = z + distance, (z > 0) & (z + distance < Z_SIZE)

                @pl.when(self.guard(piece, sent))
                def _():
                    self.copy(plane, distance, piece, upward).wait_send()


class PlaneGather:
    def __init__(self, places, block_ref, send, recv):
        self.at, self.block_ref, self.send, self.recv = places, block_ref, send, recv

    def copy(self, slot):
        device, (dy, dx), part = (
            (self.at.x_id, (0, 0), None), (self.at.y_id, (0, 0), None),
            (self.at.x_id, (1, 0), 0), (self.at.y_id, (0, 1), 1),
            (self.at.core_id, (0, 0), None), (self.at.core_id, (0, 1), None),
            (self.at.core_id, (1, 0), None), (self.at.core_id, (1, 1), None),
        )[slot]
        ref = self.block_ref((self.at.y + dy) % 2, (self.at.x + dx) % 2, self.at.c, part)
        return remote(ref, ref, self.send.at[slot], self.recv.at[slot], device)

    def start(self, *slots):
        for slot in slots:
            self.copy(slot).start()

    def arrive(self, *slots):
        for slot in slots:
            (dy, dx, dc), part = (
                ((0, 1, 0), None), ((1, 0, 0), None), ((1, 1, 0), 0), ((1, 1, 0), 1),
                ((0, 0, 1), None), ((0, 1, 1), None), ((1, 0, 1), None), ((1, 1, 1), None),
            )[slot]
            ref = self.block_ref(
                (self.at.y + dy) % 2, (self.at.x + dx) % 2, (self.at.c + dc) % 2, part
            )
            remote(ref, ref, self.send.at[slot], self.recv.at[slot], self.at.core_id).wait_recv()

    def drain(self):
        for slot in range(8):
            self.copy(slot).wait_send()


def line_semaphores(pieces):
    return [pltpu.SemaphoreType.DMA(((Z_SIZE - 1) * pieces,)) for _ in range(4)]


def layer_kernel(
    tok_ref, wq_ref, wk_ref, wv_ref, wo_ref, gin_ref, gpost_ref, gq_ref, gk_ref, pos_ref, freq_ref,
    out_ref,
    xs, x_all, ws, w_all, acc, queries, kv, att_all, wo_own, wo_all, gin, gpost,
    cos_t, sin_t, q_off, k_off, result, got, turned_out,
    stage_sem, local_sem, w_send, w_recv, x_send, x_recv, halo_send, halo_recv, att_send, att_recv,
    o_send, o_recv, r_send, r_recv,
    *line_sems,
):
    at = Places()
    z, y, x, c = at.z, at.y, at.x, at.c
    same = c == y
    depth = wq_ref.shape[0]
    own_tokens, model = xs.shape
    plane_tokens = x_all.shape[0]
    head = HEAD_SIZE
    f32, bf16 = jnp.float32, jnp.bfloat16
    at.greet()

    q_half, k_half = 2 * head, head
    loads = []
    for half in range(2):
        for ref, begin, width in ((wq_ref, 0, q_half), (wk_ref, q_half, k_half), (wv_ref, q_half + k_half, k_half)):
            loads.append(pltpu.make_async_copy(
                ref.at[:, pl.ds(half * width, width)],
                ws.at[half, :, pl.ds(begin, width)],
                stage_sem.at[len(loads)],
            ))
    tok_load = pltpu.make_async_copy(tok_ref, xs, stage_sem.at[6])
    wo_load = pltpu.make_async_copy(wo_ref, wo_own, stage_sem.at[7])
    for copy in loads + [tok_load, wo_load]:
        copy.start()
    for copy in loads:
        copy.wait()
    at.meet()

    def block_rows(plane, row):
        return w_all.at[aligned((plane * 2 + row) * depth, depth)]

    def near_copy():
        return remote(ws.at[1 - c], block_rows(z, y), w_send.at[0], w_recv.at[0], at.core_id)

    def far_copy(target):
        block = block_rows(z, y) if target is not None else block_rows(z, 1 - y)
        device = at.y_id if target is None else target
        if target is at.diag_id:
            return remote(ws.at[1 - c], block, w_send.at[1], w_recv.at[1], device)
        return remote(ws.at[c], block, w_send.at[0], w_recv.at[1], device)

    own_block = pltpu.make_async_copy(ws.at[c], block_rows(z, y), local_sem.at[0])

    @pl.when(same)
    def _():
        near_copy().start()
        own_block.start()

    @pl.when(jnp.logical_not(same))
    def _():
        far_copy(at.y_id).start()
        far_copy(at.diag_id).start()

    half_rows = depth // 2

    def w_piece(plane, piece):
        row = at.y if piece < 2 else 1 - at.y
        return w_all.at[aligned((plane * 2 + row) * depth + (piece % 2) * half_rows, half_rows)]

    def o_piece(plane, piece):
        return wo_all.at[plane, pl.ds(O_CUTS[piece], O_CUTS[piece + 1] - O_CUTS[piece])]

    w_line = Line(at, w_piece, W_PIECES, line_sems[:4])
    o_line = Line(
        at, o_piece, O_PIECES, line_sems[4:],
        lambda piece, condition: condition & (c == 1) if piece == O_PIECES - 1 else condition,
    )

    @pl.when(same)
    def _():
        own_block.wait()

    @pl.when(jnp.logical_not(same))
    def _():
        near_copy().wait_recv()

    for piece in range(2):
        w_line.send_own(piece)

    def block_of(row, column, core):
        return (row * 4 + column * 2 + core) * own_tokens

    tok_load.wait()
    gin[...] = gin_ref[...].reshape(1, model)
    gpost[...] = gpost_ref[...].reshape(1, model)
    own_begin = block_of(y, x, c)

    @pl.loop(0, own_tokens // TILE)
    def _(step):
        v = xs[aligned(step * TILE, TILE), :].astype(f32)
        mean_square = jnp.mean(v * v, axis=-1, keepdims=True)
        x_all[aligned(own_begin + step * TILE, TILE), :] = (
            v * lax.rsqrt(mean_square + EPSILON) * gin[...]
        ).astype(bf16)

    cut = own_tokens * 3 // 4

    def x_block(row, column, core, part):
        begin, size = ((0, own_tokens), (0, cut), (cut, own_tokens - cut))[0 if part is None else part + 1]
        return x_all.at[aligned(block_of(row, column, core) + begin, size)]

    tokens = PlaneGather(at, x_block, x_send, x_recv)
    tokens.start(0, 1, 4)

    o_rows = O_CUTS[-1]
    o_width = wo_own.shape[1]

    def o_copy(slot):
        dx, dc = ((0, 1), (1, 0), (1, 1))[slot]
        part = (x + dx) % 2 * 2 + (c + dc) % 2
        begin = part * (depth // TILE) // 4 * TILE
        return remote(
            wo_own.at[aligned(begin, o_rows)],
            wo_all.at[z, :, aligned((x * 2 + c) * o_width, o_width, 128)],
            o_send.at[slot], o_recv.at[slot], at.mate(0, dx, dc),
        )

    def o_arrive(slot):
        dx, dc = ((0, 1), (1, 0), (1, 1))[slot]
        part = (x + dx) % 2 * 2 + (c + dc) % 2
        block = wo_all.at[z, :, aligned(part * o_width, o_width, 128)]
        remote(block, block, o_send.at[slot], o_recv.at[slot], at.mate(0, dx, dc)).wait_recv()

    wo_load.wait()
    for slot in range(3):
        o_copy(slot).start()
    own_part = x * 2 + c
    keep_o = pltpu.make_async_copy(
        wo_own.at[aligned(own_part * (depth // TILE) // 4 * TILE, o_rows)],
        wo_all.at[z, :, aligned(own_part * o_width, o_width, 128)],
        local_sem.at[1],
    )
    keep_o.start()

    far_copy(None).wait_recv()
    for piece in range(2, W_PIECES):
        w_line.send_own(piece)

    first = pos_ref[0:1, 0:1]
    blocks = plane_tokens // head

    @pl.loop(0, blocks)
    def _(block):
        row = (pos_ref[pl.ds(z * blocks + block, 1), :] - first).astype(f32)
        column = jnp.broadcast_to(row, (head, head)).T
        here = aligned(block * head, head)
        q_off[here, :] = column
        angles = column * freq_ref[...]
        cos_t[here, :] = jnp.cos(angles)
        lane = lax.broadcasted_iota(jnp.int32, (head, head), 1)
        sine = jnp.sin(angles)
        sin_t[here, :] = jnp.where(lane < head // 2, -sine, sine)

    for block in range(2 * blocks):
        index = jnp.maximum((z - 1) * blocks + block, 0)
        row = (pos_ref[pl.ds(index, 1), :] - first).astype(f32)
        if block < blocks:
            row = jnp.where(z > 0, row, FAR_KEY)
        k_off[:, block * head:(block + 1) * head] = row

    @pl.when(z == 0)
    def _():
        kv[:, pl.ds(0, plane_tokens), :] = jnp.zeros((2, plane_tokens, head), bf16)

    for piece in range(W_PIECES):
        w_line.forward(1, piece)
    tokens.arrive(0)
    tokens.start(3, 5)
    tokens.arrive(1)
    tokens.start(2, 6)
    for piece in range(W_PIECES):
        w_line.forward(2, piece)
    keep_o.wait()
    for slot in range(3):
        o_arrive(slot)

    @pl.when((z == 0) | (z == Z_SIZE - 1))
    def _():
        for piece in range(O_PIECES):
            o_line.send_own(piece)

    tokens.arrive(2, 3)
    tokens.start(7)
    tokens.arrive(4, 5, 6, 7)

    pair_depth = 4 * depth
    row_step = plane_tokens // 2

    def multiply(pair, add):
        @pl.loop(0, plane_tokens // row_step)
        def _(step):
            rows = aligned(step * row_step, row_step)
            product = jnp.dot(
                x_all[rows, aligned(pair * pair_depth, pair_depth, 128)],
                w_all[aligned(pair * pair_depth, pair_depth), :],
                preferred_element_type=f32,
            )
            acc[rows, :] = acc[rows, :] + product if add else product

    for piece in range(W_PIECES):
        w_line.arrive(1, piece)
    multiply(z // 2, False)
    for distance in range(2, Z_SIZE):
        for piece in range(W_PIECES):
            w_line.arrive(distance, piece)
    multiply(1 - z // 2, True)

    def turned(v, gain, cosine, sine):
        mean_square = jnp.mean(v * v, axis=-1, keepdims=True)
        v = v * lax.rsqrt(mean_square + EPSILON) * gain
        return (v * cosine + pltpu.roll(v, head // 2, 1) * sine).astype(bf16)

    @pl.loop(0, blocks)
    def _(block):
        here = aligned(block * head, head)
        own = aligned(plane_tokens + block * head, head)
        kv[0, own, :] = turned(
            acc[here, 2 * head:3 * head], gk_ref[...], cos_t[here, :], sin_t[here, :]
        )
        kv[1, own, :] = acc[here, 3 * head:4 * head].astype(bf16)

    q_step = 2 * own_tokens
    q_blocks = plane_tokens // q_step
    span = LOOKBACK_WINDOW + q_step

    def halo(block):
        return remote(
            kv.at[:, pl.ds(plane_tokens + block * q_step, q_step)],
            kv.at[:, pl.ds(block * q_step, q_step)],
            halo_send.at[block], halo_recv.at[block], at.up_id,
        )

    @pl.when(z < Z_SIZE - 1)
    def _():
        for block in reversed(range(q_blocks)):
            halo(block).start()

    @pl.loop(0, blocks)
    def _(block):
        here = aligned(block * head, head)
        for h in range(2):
            columns = slice(h * head, (h + 1) * head)
            queries[here, columns] = turned(
                acc[here, columns], gq_ref[...], cos_t[here, :], sin_t[here, :]
            )

    def pass_o(upward):
        w_line.drain(upward)
        for piece in range(O_PIECES):
            o_line.send_own(piece, upward, not upward)

    @pl.when(z == 1)
    def _():
        pass_o(True)
        pass_o(False)
        for distance in (1, 2):
            for piece in range(O_PIECES):
                o_line.forward(distance, piece)

    @pl.when(z == 2)
    def _():
        pass_o(False)

    width = 2 * head

    def att_block(block):
        def ref(row, column, core, part):
            half = q_step // 2
            begin, size = ((0, q_step), (0, half), (half, half))[0 if part is None else part + 1]
            return att_all.at[
                pl.ds(block * q_step + begin, size),
                aligned((column * 4 + row * 2 + core) * width, width, 128),
            ]

        return ref

    attended = [
        PlaneGather(at, att_block(block), att_send.at[block], att_recv.at[block])
        for block in range(q_blocks)
    ]
    own_heads = (x * 4 + y * 2 + c) * width

    def attend_block(block):
        rows, keys = pl.ds(block * q_step, q_step), pl.ds(block * q_step, span)
        gap = q_off[rows, 0:1] - k_off[:, keys]
        allowed = (gap >= 0) & (gap < LOOKBACK_WINDOW)
        k_rows, v_rows = kv[0, keys, :], kv[1, keys, :]
        for h in range(2):
            scores = lax.dot_general(
                queries[rows, h * head:(h + 1) * head], k_rows, (((1,), (1,)), ((), ())),
                preferred_element_type=f32,
            ) * QS ** (-0.5)
            scores = jnp.where(allowed, scores, -1e30)
            weights = jnp.exp(scores - jnp.max(scores, axis=-1, keepdims=True))
            totals = jnp.sum(weights, axis=-1, keepdims=True)
            mixed = jnp.dot(weights.astype(bf16), v_rows, preferred_element_type=f32) / totals
            att_all[rows, aligned(own_heads + h * head, head, 128)] = mixed.astype(bf16)

    def hand_on(block):
        attended[block].arrive(0)
        attended[block].start(3, 5)
        attended[block].arrive(1)
        attended[block].start(2, 6)

    def hand_across(block):
        attended[block].arrive(2, 3)
        attended[block].start(7)

    for block in reversed(range(q_blocks)):
        @pl.when(z > 0)
        def _():
            halo(block).wait_recv()

        attend_block(block)
        attended[block].start(0, 1, 4)
        if block + 1 < q_blocks:
            hand_on(block + 1)
        if block + 2 < q_blocks:
            hand_across(block + 2)

    @pl.when(z == 2)
    def _():
        pass_o(True)
        for distance in (1, 2):
            for piece in range(O_PIECES):
                o_line.forward(distance, piece)

    @pl.when((z == 0) | (z == Z_SIZE - 1))
    def _():
        w_line.drain(True)
        w_line.drain(False)

    hand_on(0)
    hand_across(1)
    hand_across(0)
    for gather in attended:
        gather.arrive(4, 5, 6, 7)

    planes = [z, z + 1 - 2 * (z % 2), (z + 2) % 4, 3 - z]
    own_index = y * 4 + x * 2 + c

    def r_copy(step, mate):
        dy, dx, dc = MATES[mate]
        owner = (y + dy) % 2 * 4 + (x + dx) % 2 * 2 + (c + dc) % 2
        slot = step * len(MATES) + mate
        return remote(
            result.at[step, owner], got.at[step, own_index], r_send.at[slot], r_recv.at[slot],
            at.mate(dy, dx, dc),
        )

    def r_arrive(step, mate):
        dy, dx, dc = MATES[mate]
        owner = (y + dy) % 2 * 4 + (x + dx) % 2 * 2 + (c + dc) % 2
        slot = step * len(MATES) + mate
        block = got.at[step, owner]
        remote(block, block, r_send.at[slot], r_recv.at[slot], at.core_id).wait_recv()

    def project(step):
        sums = lax.dot_general(
            wo_all[planes[step]], att_all[...], (((1,), (1,)), ((), ())), preferred_element_type=f32
        ).astype(bf16)
        for owner in range(2 * blocks // 2):
            result[step, owner] = sums[:, owner * own_tokens:(owner + 1) * own_tokens]
        for mate in range(len(MATES)):
            r_copy(step, mate).start()
        got[step, own_index] = result[step, own_index]

    def finish(step, square):
        for mate in range(len(MATES)):
            r_arrive(step, mate)
        for owner in range(8):
            row, part = owner // 4, owner % 4
            begin = part * (depth // TILE) // 4 * TILE
            size = (part + 1) * (depth // TILE) // 4 * TILE - begin
            v = got[step, owner, :size].astype(f32)
            turned_out[aligned((planes[step] * 2 + row) * depth + begin, size), :] = v
            square = square + jnp.sum(v * v, axis=0, keepdims=True)
        return square

    square = jnp.zeros((1, own_tokens), f32)
    for step in range(Z_SIZE):
        if step > 0:
            for piece in range(O_PIECES):
                o_line.arrive(step, piece)
        project(step)
        if step > 0:
            square = finish(step - 1, square)
    square = finish(Z_SIZE - 1, square)

    scale = lax.rsqrt(square / model + EPSILON)
    for begin in range(0, model, head):
        columns = slice(begin, begin + head)
        normed = (turned_out[columns, :] * scale).T * gpost[:, columns]
        out_ref[:, columns] = (xs[:, columns].astype(f32) + normed).astype(bf16)

    @pl.when(same)
    def _():
        near_copy().wait_send()

    @pl.when(jnp.logical_not(same))
    def _():
        far_copy(at.y_id).wait_send()
        far_copy(at.diag_id).wait_send()

    tokens.drain()
    for gather in attended:
        gather.drain()
    for slot in range(3):
        o_copy(slot).wait_send()

    @pl.when(z < Z_SIZE - 1)
    def _():
        for block in range(q_blocks):
            halo(block).wait_send()

    o_line.drain(True)
    o_line.drain(False)
    for step in range(Z_SIZE):
        for mate in range(len(MATES)):
            r_copy(step, mate).wait_send()


def layer(tokens, positions, w_query, key_matrix, value_matrix, w_out_t, gain_in, gain_query, gain_key, gain_post):
    own_tokens, model = tokens.shape
    depth = w_query.shape[0]
    columns, heads = w_out_t.shape
    head = HEAD_SIZE
    plane = 8 * own_tokens
    bf16, f32, dma = jnp.bfloat16, jnp.float32, pltpu.SemaphoreType.DMA
    frequency = jnp.asarray(ROPE_BASE ** (-2.0 * (np.arange(head) % (head // 2)) / head), f32)
    vmem, anywhere = pl.BlockSpec(memory_space=pltpu.VMEM), pl.BlockSpec(memory_space=pl.ANY)
    o_rows = O_CUTS[-1]
    return pl.pallas_call(
        layer_kernel,
        out_shape=jax.ShapeDtypeStruct((own_tokens, model), bf16),
        in_specs=[anywhere] * 5 + [vmem] * 6,
        out_specs=vmem,
        scratch_shapes=[
            pltpu.VMEM((own_tokens, model), bf16),
            pltpu.VMEM((plane, model), bf16),
            pltpu.VMEM((2, depth, 4 * head), bf16),
            pltpu.VMEM((model, 4 * head), bf16),
            pltpu.VMEM((plane, 4 * head), f32),
            pltpu.VMEM((plane, 2 * head), bf16),
            pltpu.VMEM((2, 2 * plane, head), bf16),
            pltpu.VMEM((plane, 4 * heads), bf16),
            pltpu.VMEM((columns, heads), bf16),
            pltpu.VMEM((Z_SIZE, o_rows, 4 * heads), bf16),
            pltpu.VMEM((1, model), f32),
            pltpu.VMEM((1, model), f32),
            pltpu.VMEM((plane, head), f32),
            pltpu.VMEM((plane, head), f32),
            pltpu.VMEM((plane, head), f32),
            pltpu.VMEM((1, 2 * plane), f32),
            pltpu.VMEM((Z_SIZE, 8, o_rows, own_tokens), bf16),
            pltpu.VMEM((Z_SIZE, 8, o_rows, own_tokens), bf16),
            pltpu.VMEM((model, own_tokens), f32),
            dma((8,)), dma((2,)), dma((2,)), dma((2,)), dma((8,)), dma((8,)), dma((4,)), dma((4,)), dma((4, 8)), dma((4, 8)),
            dma((3,)), dma((3,)), dma((7 * Z_SIZE,)), dma((7 * Z_SIZE,)),
            *line_semaphores(W_PIECES), *line_semaphores(O_PIECES),
        ],
        compiler_params=pltpu.CompilerParams(
            collective_id=0, has_side_effects=True, vmem_limit_bytes=60 * 2**20
        ),
        name="layer",
    )(
        tokens, w_query, key_matrix, value_matrix, w_out_t,
        gain_in, gain_post,
        gain_query.reshape(1, -1), gain_key.reshape(1, -1),
        positions.reshape(-1, head), frequency.reshape(1, -1),
    )


def attend(query_matrix, projected_keys, projected_values, query_offsets, key_offsets, key_valid):
    scores = jnp.einsum(
        "qkgd,skd->kgqs", query_matrix, projected_keys, preferred_element_type=jnp.float32
    ) * QS ** (-0.5)
    position_gap = query_offsets[:, None] - key_offsets[None, :]
    allowed = key_valid[None, :] & (position_gap >= 0) & (position_gap < LOOKBACK_WINDOW)
    scores = jnp.where(allowed[None, None], scores, -1e30)
    row_max = jnp.max(scores, axis=-1, keepdims=True)
    weights = jnp.where(allowed[None, None], jnp.exp(scores - row_max), 0.0)
    totals = jnp.sum(weights, axis=-1, keepdims=True)
    rounded = weights.astype(jnp.bfloat16)
    mixed = jnp.einsum(
        "kgqs,skd->qkgd", rounded, projected_values, preferred_element_type=jnp.float32
    )
    mixed = mixed / jnp.transpose(totals, (2, 0, 1, 3))
    return mixed.astype(jnp.bfloat16).reshape(query_matrix.shape[0], -1)


def shards(
    tokens,
    positions,
    w_query,
    key_matrix,
    value_matrix,
    w_out,
    gain_in,
    gain_query,
    gain_key,
    gain_post,
):
    if lax.axis_size("ctx") == 2 * Z_SIZE and lax.axis_size("tp") == 4:
        return layer(
            tokens, positions, w_query, key_matrix, value_matrix, w_out.T,
            gain_in, gain_query, gain_key, gain_post,
        )
    normed = row_norm(tokens.astype(jnp.float32), gain_in).astype(jnp.bfloat16)
    normalized_rows = lax.all_gather(normed, "tp", axis=0, tiled=True)
    weights_in = lax.all_gather(
        jnp.concatenate([w_query, key_matrix, value_matrix], axis=1), "ctx", axis=0, tiled=True
    )
    row_count = normalized_rows.shape[0]
    block_start = lax.axis_index("ctx") * row_count
    offsets_all = positions - positions[0]
    query_offsets = lax.dynamic_slice_in_dim(offsets_all, block_start, row_count, 0)
    query_width, key_width = w_query.shape[1], key_matrix.shape[1]

    def add_rows(weights):
        return jnp.dot(normalized_rows, weights, preferred_element_type=jnp.float32)

    key_value_raw = add_rows(weights_in[:, query_width:])
    query_raw = add_rows(weights_in[:, :query_width])
    unnormed_keys = key_value_raw[:, :key_width]
    value_raw = key_value_raw[:, key_width:]
    key_heads = key_matrix.shape[1] // HEAD_SIZE
    projected_keys = rotate(
        row_norm(unnormed_keys.reshape(row_count, key_heads, HEAD_SIZE), gain_key), query_offsets
    ).astype(jnp.bfloat16)
    projected_values = value_raw.astype(jnp.bfloat16).reshape(row_count, key_heads, HEAD_SIZE)
    own_pair = jnp.stack([projected_keys, projected_values])
    window_blocks = LOOKBACK_WINDOW // row_count
    earlier = [shifted(own_pair, "ctx", steps) for steps in range(window_blocks, 0, -1)]
    window_pair = jnp.concatenate(earlier + [own_pair], axis=1)
    query_heads = w_query.shape[1] // HEAD_SIZE
    query_matrix = rotate(
        row_norm(query_raw.reshape(row_count, query_heads, HEAD_SIZE), gain_query), query_offsets
    ).astype(jnp.bfloat16)
    query_matrix = query_matrix.reshape(row_count, key_heads, query_heads // key_heads, HEAD_SIZE)
    padded_offsets = jnp.concatenate(
        [jnp.zeros((LOOKBACK_WINDOW,), jnp.int32), offsets_all], axis=0
    )
    key_offsets = lax.dynamic_slice_in_dim(
        padded_offsets, block_start, LOOKBACK_WINDOW + row_count, 0
    )
    key_valid = (
        block_start + jnp.arange(LOOKBACK_WINDOW + row_count, dtype=jnp.int32) >= LOOKBACK_WINDOW
    )
    attended = attend(
        query_matrix, window_pair[0], window_pair[1], query_offsets, key_offsets, key_valid
    )
    projected = jnp.dot(
        attended,
        lax.all_gather(w_out, "ctx", axis=1, tiled=True),
        preferred_element_type=jnp.float32,
    )
    summed = lax.psum_scatter(
        projected.astype(jnp.bfloat16), "tp", scatter_dimension=0, tiled=True
    ).astype(jnp.float32)
    return (tokens.astype(jnp.float32) + row_norm(summed, gain_post)).astype(jnp.bfloat16)


def solution(mesh):
    in_specs = (
        P(("ctx", "tp"), None),
        P(),
        P("ctx", "tp"),
        P("ctx", "tp"),
        P("ctx", "tp"),
        P("tp", "ctx"),
        P(),
        P(),
        P(),
        P(),
    )
    out_specs = P(("ctx", "tp"), None)
    return jax.shard_map(shards, mesh=mesh, in_specs=in_specs, out_specs=out_specs, check_vma=False)
```

```python
import jax
import jax.numpy as jnp
import numpy as np
from jax import lax
from jax.experimental import pallas as pl
from jax.experimental.pallas import tpu as pltpu
from jax.sharding import PartitionSpec as P

HEAD_SIZE = 128
QS = 168
LOOKBACK_WINDOW = 1024


EPSILON = 1e-06
ROPE_BASE = 10000.0


def shifted(value, axis, steps):
    count = lax.axis_size(axis)
    leading, last = (max(0, -steps), min(count, count - steps))
    return lax.ppermute(value, axis, [(source, source + steps) for source in range(leading, last)])


def row_norm(values, scales):
    mean_square = jnp.mean(values * values, axis=-1, keepdims=True)
    return values * lax.rsqrt(mean_square + EPSILON) * scales


def rotate(head_rows, offsets):
    half_dim = head_rows.shape[-1] // 2
    frequency = ROPE_BASE ** (
        -(jnp.arange(half_dim, dtype=jnp.float32) * 2.0) / head_rows.shape[-1]
    )
    angles = offsets.astype(jnp.float32)[:, None] * frequency[None, :]
    cosine = jnp.cos(angles)[:, None, :]
    sine_wave = jnp.sin(angles)[:, None, :]
    first_half = head_rows[..., :half_dim]
    second_half = head_rows[..., half_dim:]
    return jnp.concatenate(
        [
            first_half * cosine - second_half * sine_wave,
            second_half * cosine + first_half * sine_wave,
        ],
        axis=-1,
    )


Z_SIZE = 4
TILE = 16
W_PIECES = 4
O_PIECES = 3
O_CUTS = (0, 80, 160, 176)
MATES = [(i // 4, i // 2 % 2, i % 2) for i in range(1, 8)]
MESH = pl.DeviceIdType.MESH
FAR_KEY = 1e9


def remote(source, target, send, recv, device):
    return pltpu.make_async_remote_copy(
        src_ref=source, dst_ref=target, send_sem=send, recv_sem=recv,
        device_id=device, device_id_type=MESH,
    )


def aligned(value, size, step=TILE):
    return pl.ds(pl.multiple_of(value, step), size)


class Places:
    def __init__(self):
        self.ctx = lax.axis_index("ctx")
        self.tp = lax.axis_index("tp")
        self.z, self.y = self.ctx // 2, self.ctx % 2
        self.x, self.c = self.tp // 2, self.tp % 2
        self.core_id = self.mate(0, 0, 1)
        self.x_id = self.mate(0, 1, 0)
        self.y_id = self.mate(1, 0, 0)
        self.diag_id = self.mate(1, 0, 1)
        self.up_id = (self.ctx + 2, self.tp)
        self.down_id = (self.ctx - 2, self.tp)

    def mate(self, dy, dx, dc):
        row, column, core = ((v + d) % 2 for v, d in ((self.y, dy), (self.x, dx), (self.c, dc)))
        return (self.z * 2 + row, column * 2 + core)

    def greet(self):
        barrier = pltpu.get_barrier_semaphore()

        def signal(target):
            pl.semaphore_signal(barrier, inc=1, device_id=target, device_id_type=MESH)

        for dy, dx, dc in MATES:
            signal(self.mate(dy, dx, dc))

        @pl.when(self.z < Z_SIZE - 1)
        def _():
            signal(self.up_id)

        @pl.when(self.z > 0)
        def _():
            signal(self.down_id)

    def meet(self):
        middle = ((self.z + 1) // 2) % 2
        pl.semaphore_wait(pltpu.get_barrier_semaphore(), 8 + middle)


class Line:
    def __init__(self, places, piece_ref, pieces, sems, guard=None):
        self.at, self.piece_ref, self.pieces = places, piece_ref, pieces
        self.guard = guard or (lambda piece, condition: condition)
        self.up_send, self.down_send, self.below, self.above = sems

    def copy(self, plane, distance, piece, upward):
        ref = self.piece_ref(plane, piece)
        slot = distance * self.pieces + piece
        if upward:
            return remote(ref, ref, self.up_send.at[slot], self.below.at[slot], self.at.up_id)
        return remote(ref, ref, self.down_send.at[slot], self.above.at[slot], self.at.down_id)

    def send_own(self, piece, upward=True, downward=True):
        z = self.at.z
        if upward:
            @pl.when(self.guard(piece, z < Z_SIZE - 1))
            def _():
                self.copy(z, 0, piece, True).start()

        if downward:
            @pl.when(self.guard(piece, z > 0))
            def _():
                self.copy(z, 0, piece, False).start()

    def forward(self, distance, piece):
        z = self.at.z
        if distance == Z_SIZE - 1:
            return

        @pl.when(self.guard(piece, (z >= distance) & (z < Z_SIZE - 1)))
        def _():
            self.copy(z - distance, distance - 1, piece, True).wait_recv()
            self.copy(z - distance, distance, piece, True).start()

        @pl.when(self.guard(piece, (z + distance < Z_SIZE) & (z > 0)))
        def _():
            self.copy(z + distance, distance - 1, piece, False).wait_recv()
            self.copy(z + distance, distance, piece, False).start()

    def arrive(self, distance, piece):
        z = self.at.z

        @pl.when(self.guard(piece, z == Z_SIZE - 1))
        def _():
            self.copy(z - distance, distance - 1, piece, True).wait_recv()

        @pl.when(self.guard(piece, z == 0))
        def _():
            self.copy(z + distance, distance - 1, piece, False).wait_recv()

    def drain(self, upward, last=None):
        z = self.at.z
        final = (Z_SIZE - 2, self.pieces - 1)
        for distance in range(Z_SIZE - 1):
            for piece in range(self.pieces):
                if last is not None and last != ((distance, piece) == final):
                    continue
                if upward:
                    plane, sent = z - distance, (z < Z_SIZE - 1) & (z >= distance)
                else:
                    plane, sent = z + distance, (z > 0) & (z + distance < Z_SIZE)

                @pl.when(self.guard(piece, sent))
                def _():
                    self.copy(plane, distance, piece, upward).wait_send()


class PlaneGather:
    def __init__(self, places, block_ref, send, recv):
        self.at, self.block_ref, self.send, self.recv = places, block_ref, send, recv

    def copy(self, slot):
        device, (dy, dx), part = (
            (self.at.x_id, (0, 0), None), (self.at.y_id, (0, 0), None),
            (self.at.x_id, (1, 0), 0), (self.at.y_id, (0, 1), 1),
            (self.at.core_id, (0, 0), None), (self.at.core_id, (0, 1), None),
            (self.at.core_id, (1, 0), None), (self.at.core_id, (1, 1), None),
        )[slot]
        ref = self.block_ref((self.at.y + dy) % 2, (self.at.x + dx) % 2, self.at.c, part)
        return remote(ref, ref, self.send.at[slot], self.recv.at[slot], device)

    def start(self, *slots):
        for slot in slots:
            self.copy(slot).start()

    def arrive(self, *slots):
        for slot in slots:
            (dy, dx, dc), part = (
                ((0, 1, 0), None), ((1, 0, 0), None), ((1, 1, 0), 0), ((1, 1, 0), 1),
                ((0, 0, 1), None), ((0, 1, 1), None), ((1, 0, 1), None), ((1, 1, 1), None),
            )[slot]
            ref = self.block_ref(
                (self.at.y + dy) % 2, (self.at.x + dx) % 2, (self.at.c + dc) % 2, part
            )
            remote(ref, ref, self.send.at[slot], self.recv.at[slot], self.at.core_id).wait_recv()

    def drain(self):
        for slot in range(8):
            self.copy(slot).wait_send()


def line_semaphores(pieces):
    return [pltpu.SemaphoreType.DMA(((Z_SIZE - 1) * pieces,)) for _ in range(4)]


def layer_kernel(
    tok_ref, wq_ref, wk_ref, wv_ref, wo_ref, gin_ref, gpost_ref, gq_ref, gk_ref, pos_ref, freq_ref,
    out_ref,
    xs, x_all, ws, w_all, acc, queries, kv, att_all, wo_own, wo_all, gin, gpost,
    cos_t, sin_t, q_off, k_off, result, got, turned_out,
    stage_sem, local_sem, w_send, w_recv, x_send, x_recv, halo_send, halo_recv, att_send, att_recv,
    o_send, o_recv, r_send, r_recv,
    *line_sems,
):
    at = Places()
    z, y, x, c = at.z, at.y, at.x, at.c
    same = c == y
    depth = wq_ref.shape[0]
    own_tokens, model = xs.shape
    plane_tokens = x_all.shape[0]
    head = HEAD_SIZE
    f32, bf16 = jnp.float32, jnp.bfloat16
    at.greet()

    loads = []
    for half in range(2):
        for ref, part, begin, width in (
            (wk_ref, 0, 0, head), (wv_ref, 0, head, head), (wq_ref, 1, 0, 2 * head)
        ):
            loads.append(pltpu.make_async_copy(
                ref.at[:, pl.ds(half * width, width)],
                ws.at[half, part, :, pl.ds(begin, width)],
                stage_sem.at[len(loads)],
            ))
    tok_load = pltpu.make_async_copy(tok_ref, xs, stage_sem.at[6])
    wo_load = pltpu.make_async_copy(wo_ref, wo_own, stage_sem.at[7])
    for copy in loads + [tok_load, wo_load]:
        copy.start()
    for copy in loads:
        copy.wait()
    at.meet()

    def block_rows(plane, row):
        return w_all.at[:, aligned((plane * 2 + row) * depth, depth)]

    def near_copy():
        return remote(ws.at[1 - c], block_rows(z, y), w_send.at[0], w_recv.at[0], at.core_id)

    def far_copy(target):
        block = block_rows(z, y) if target is not None else block_rows(z, 1 - y)
        device = at.y_id if target is None else target
        if target is at.diag_id:
            return remote(ws.at[1 - c], block, w_send.at[1], w_recv.at[1], device)
        return remote(ws.at[c], block, w_send.at[0], w_recv.at[1], device)

    own_block = pltpu.make_async_copy(ws.at[c], block_rows(z, y), local_sem.at[0])

    @pl.when(same)
    def _():
        near_copy().start()
        own_block.start()

    @pl.when(jnp.logical_not(same))
    def _():
        far_copy(at.y_id).start()
        far_copy(at.diag_id).start()


    def w_piece(plane, piece):
        row = (at.y + piece % 2) % 2
        return w_all.at[piece // 2, aligned((plane * 2 + row) * depth, depth)]

    def o_piece(plane, piece):
        return wo_all.at[plane, pl.ds(O_CUTS[piece], O_CUTS[piece + 1] - O_CUTS[piece])]

    w_line = Line(at, w_piece, W_PIECES, line_sems[:4])
    o_line = Line(
        at, o_piece, O_PIECES, line_sems[4:],
        lambda piece, condition: condition & (c == 1) if piece == O_PIECES - 1 else condition,
    )

    @pl.when(same)
    def _():
        own_block.wait()

    @pl.when(jnp.logical_not(same))
    def _():
        near_copy().wait_recv()

    w_line.send_own(0)
    w_line.send_own(2)

    def block_of(row, column, core):
        return (row * 4 + column * 2 + core) * own_tokens

    tok_load.wait()
    gin[...] = gin_ref[...].reshape(1, model)
    gpost[...] = gpost_ref[...].reshape(1, model)
    own_begin = block_of(y, x, c)

    @pl.loop(0, own_tokens // TILE)
    def _(step):
        v = xs[aligned(step * TILE, TILE), :].astype(f32)
        mean_square = jnp.mean(v * v, axis=-1, keepdims=True)
        x_all[aligned(own_begin + step * TILE, TILE), :] = (
            v * lax.rsqrt(mean_square + EPSILON) * gin[...]
        ).astype(bf16)

    cut = own_tokens * 3 // 4

    def x_block(row, column, core, part):
        begin, size = ((0, own_tokens), (0, cut), (cut, own_tokens - cut))[0 if part is None else part + 1]
        return x_all.at[aligned(block_of(row, column, core) + begin, size)]

    tokens = PlaneGather(at, x_block, x_send, x_recv)
    tokens.start(0, 1, 4)

    o_rows = O_CUTS[-1]
    o_width = wo_own.shape[1]

    def o_copy(slot):
        dx, dc = ((0, 1), (1, 0), (1, 1))[slot]
        part = (x + dx) % 2 * 2 + (c + dc) % 2
        begin = part * (depth // TILE) // 4 * TILE
        return remote(
            wo_own.at[aligned(begin, o_rows)],
            wo_all.at[z, :, aligned((x * 2 + c) * o_width, o_width, 128)],
            o_send.at[slot], o_recv.at[slot], at.mate(0, dx, dc),
        )

    def o_arrive(slot):
        dx, dc = ((0, 1), (1, 0), (1, 1))[slot]
        part = (x + dx) % 2 * 2 + (c + dc) % 2
        block = wo_all.at[z, :, aligned(part * o_width, o_width, 128)]
        remote(block, block, o_send.at[slot], o_recv.at[slot], at.mate(0, dx, dc)).wait_recv()

    wo_load.wait()
    for slot in range(3):
        o_copy(slot).start()
    own_part = x * 2 + c
    keep_o = pltpu.make_async_copy(
        wo_own.at[aligned(own_part * (depth // TILE) // 4 * TILE, o_rows)],
        wo_all.at[z, :, aligned(own_part * o_width, o_width, 128)],
        local_sem.at[1],
    )
    keep_o.start()

    far_copy(None).wait_recv()
    w_line.send_own(1)
    w_line.send_own(3)
    middle = (z == 1) | (z == 2)

    first = pos_ref[0:1, 0:1]
    blocks = plane_tokens // head

    @pl.loop(0, blocks)
    def _(block):
        row = (pos_ref[pl.ds(z * blocks + block, 1), :] - first).astype(f32)
        column = jnp.broadcast_to(row, (head, head)).T
        here = aligned(block * head, head)
        q_off[here, :] = column
        angles = column * freq_ref[...]
        cos_t[here, :] = jnp.cos(angles)
        lane = lax.broadcasted_iota(jnp.int32, (head, head), 1)
        sine = jnp.sin(angles)
        sin_t[here, :] = jnp.where(lane < head // 2, -sine, sine)

    for block in range(2 * blocks):
        index = jnp.maximum((z - 1) * blocks + block, 0)
        row = (pos_ref[pl.ds(index, 1), :] - first).astype(f32)
        if block < blocks:
            row = jnp.where(z > 0, row, FAR_KEY)
        k_off[:, block * head:(block + 1) * head] = row

    @pl.when(z == 0)
    def _():
        kv[:, pl.ds(0, plane_tokens), :] = jnp.zeros((2, plane_tokens, head), bf16)

    for piece in range(2):
        w_line.forward(1, piece)

    tokens.arrive(0)
    tokens.start(3, 5)
    for piece in range(2):
        w_line.forward(2, piece)
    tokens.arrive(1)
    tokens.start(2, 6)
    for distance in (1, 2):
        for piece in range(2, W_PIECES):
            w_line.forward(distance, piece)
    keep_o.wait()
    for slot in range(3):
        o_arrive(slot)

    @pl.when(jnp.logical_not(middle))
    def _():
        for piece in range(O_PIECES):
            o_line.send_own(piece)

    tokens.arrive(2, 3)
    tokens.start(7)
    tokens.arrive(4, 5, 6, 7)

    pair_depth = 4 * depth
    row_step = plane_tokens // 2

    def multiply(part, pair, add):
        @pl.loop(0, plane_tokens // row_step)
        def _(step):
            rows = aligned(step * row_step, row_step)
            product = jnp.dot(
                x_all[rows, aligned(pair * pair_depth, pair_depth, 128)],
                w_all[part, aligned(pair * pair_depth, pair_depth), :],
                preferred_element_type=f32,
            )
            columns = slice(part * 2 * head, (part + 1) * 2 * head)
            acc[rows, columns] = acc[rows, columns] + product if add else product

    def turned(v, gain, cosine, sine):
        mean_square = jnp.mean(v * v, axis=-1, keepdims=True)
        v = v * lax.rsqrt(mean_square + EPSILON) * gain
        return (v * cosine + pltpu.roll(v, head // 2, 1) * sine).astype(bf16)

    for distance in range(1, Z_SIZE):
        for piece in range(2):
            w_line.arrive(distance, piece)
    multiply(0, z // 2, False)
    multiply(0, 1 - z // 2, True)

    @pl.loop(0, blocks)
    def _(block):
        here = aligned(block * head, head)
        own = aligned(plane_tokens + block * head, head)
        kv[0, own, :] = turned(acc[here, 0:head], gk_ref[...], cos_t[here, :], sin_t[here, :])
        kv[1, own, :] = acc[here, head:2 * head].astype(bf16)

    q_step = 2 * own_tokens
    q_blocks = plane_tokens // q_step
    span = LOOKBACK_WINDOW + q_step

    def halo(block):
        return remote(
            kv.at[:, pl.ds(plane_tokens + block * q_step, q_step)],
            kv.at[:, pl.ds(block * q_step, q_step)],
            halo_send.at[block], halo_recv.at[block], at.up_id,
        )

    @pl.when(z < Z_SIZE - 1)
    def _():
        for block in reversed(range(q_blocks)):
            halo(block).start()

    def pass_o(upward):
        w_line.drain(upward, False)
        for piece in range(O_PIECES):
            o_line.send_own(piece, upward, not upward)

    @pl.when(z == 1)
    def _():
        pass_o(True)

    @pl.when(z == 2)
    def _():
        pass_o(False)

    for piece in range(2, W_PIECES):
        w_line.arrive(1, piece)
    multiply(1, z // 2, False)
    for distance in range(2, Z_SIZE):
        for piece in range(2, W_PIECES):
            w_line.arrive(distance, piece)
    multiply(1, 1 - z // 2, True)

    @pl.loop(0, blocks)
    def _(block):
        here = aligned(block * head, head)
        for h in range(2):
            raw = acc[here, (h + 2) * head:(h + 3) * head]
            queries[here, h * head:(h + 1) * head] = turned(
                raw, gq_ref[...], cos_t[here, :], sin_t[here, :]
            )

    width = 2 * head

    def att_block(block):
        def ref(row, column, core, part):
            half = q_step // 2
            begin, size = ((0, q_step), (0, half), (half, half))[0 if part is None else part + 1]
            return att_all.at[
                pl.ds(block * q_step + begin, size),
                aligned((column * 4 + row * 2 + core) * width, width, 128),
            ]

        return ref

    attended = [
        PlaneGather(at, att_block(block), att_send.at[block], att_recv.at[block])
        for block in range(q_blocks)
    ]
    own_heads = (x * 4 + y * 2 + c) * width

    def attend_block(block):
        rows, keys = pl.ds(block * q_step, q_step), pl.ds(block * q_step, span)
        gap = q_off[rows, 0:1] - k_off[:, keys]
        allowed = (gap >= 0) & (gap < LOOKBACK_WINDOW)
        k_rows, v_rows = kv[0, keys, :], kv[1, keys, :]
        for h in range(2):
            scores = lax.dot_general(
                queries[rows, h * head:(h + 1) * head], k_rows, (((1,), (1,)), ((), ())),
                preferred_element_type=f32,
            ) * QS ** (-0.5)
            scores = jnp.where(allowed, scores, -1e30)
            weights = jnp.exp(scores - jnp.max(scores, axis=-1, keepdims=True))
            totals = jnp.sum(weights, axis=-1, keepdims=True)
            mixed = jnp.dot(weights.astype(bf16), v_rows, preferred_element_type=f32) / totals
            att_all[rows, aligned(own_heads + h * head, head, 128)] = mixed.astype(bf16)

    def hand_on(block):
        attended[block].arrive(0)
        attended[block].start(3, 5)
        attended[block].arrive(1)
        attended[block].start(2, 6)

    def hand_across(block):
        attended[block].arrive(2, 3)
        attended[block].start(7)

    for block in reversed(range(q_blocks)):
        @pl.when(z > 0)
        def _():
            halo(block).wait_recv()

        attend_block(block)
        attended[block].start(0, 1, 4)
        if block + 1 < q_blocks:
            hand_on(block + 1)
        if block + 2 < q_blocks:
            hand_across(block + 2)

    @pl.when(z == 1)
    def _():
        pass_o(False)

    @pl.when(z == 2)
    def _():
        pass_o(True)

    @pl.when(middle)
    def _():
        for distance in (1, 2):
            for piece in range(O_PIECES):
                o_line.forward(distance, piece)

    @pl.when(jnp.logical_not(middle))
    def _():
        w_line.drain(True, False)
        w_line.drain(False, False)

    hand_on(0)
    hand_across(1)
    hand_across(0)
    for gather in attended:
        gather.arrive(4, 5, 6, 7)

    planes = [z, z + 1 - 2 * (z % 2), (z + 2) % 4, 3 - z]
    own_index = y * 4 + x * 2 + c

    def r_copy(step, mate):
        dy, dx, dc = MATES[mate]
        owner = (y + dy) % 2 * 4 + (x + dx) % 2 * 2 + (c + dc) % 2
        slot = step * len(MATES) + mate
        return remote(
            result.at[step, owner], got.at[step, own_index], r_send.at[slot], r_recv.at[slot],
            at.mate(dy, dx, dc),
        )

    def r_arrive(step, mate):
        dy, dx, dc = MATES[mate]
        owner = (y + dy) % 2 * 4 + (x + dx) % 2 * 2 + (c + dc) % 2
        slot = step * len(MATES) + mate
        block = got.at[step, owner]
        remote(block, block, r_send.at[slot], r_recv.at[slot], at.core_id).wait_recv()

    def project(step):
        sums = lax.dot_general(
            wo_all[planes[step]], att_all[...], (((1,), (1,)), ((), ())), preferred_element_type=f32
        ).astype(bf16)
        for owner in range(2 * blocks // 2):
            result[step, owner] = sums[:, owner * own_tokens:(owner + 1) * own_tokens]
        for mate in range(len(MATES)):
            r_copy(step, mate).start()
        got[step, own_index] = result[step, own_index]

    def finish(step, square):
        for mate in range(len(MATES)):
            r_arrive(step, mate)
        for owner in range(8):
            row, part = owner // 4, owner % 4
            begin = part * (depth // TILE) // 4 * TILE
            size = (part + 1) * (depth // TILE) // 4 * TILE - begin
            v = got[step, owner, :size].astype(f32)
            turned_out[aligned((planes[step] * 2 + row) * depth + begin, size), :] = v
            square = square + jnp.sum(v * v, axis=0, keepdims=True)
        return square

    square = jnp.zeros((1, own_tokens), f32)
    for step in range(Z_SIZE):
        if step > 0:
            for piece in range(O_PIECES):
                o_line.arrive(step, piece)
        project(step)
        if step > 0:
            square = finish(step - 1, square)
    square = finish(Z_SIZE - 1, square)

    scale = lax.rsqrt(square / model + EPSILON)
    for begin in range(0, model, head):
        columns = slice(begin, begin + head)
        normed = (turned_out[columns, :] * scale).T * gpost[:, columns]
        out_ref[:, columns] = (xs[:, columns].astype(f32) + normed).astype(bf16)

    @pl.when(same)
    def _():
        near_copy().wait_send()

    @pl.when(jnp.logical_not(same))
    def _():
        far_copy(at.y_id).wait_send()
        far_copy(at.diag_id).wait_send()

    tokens.drain()
    for gather in attended:
        gather.drain()
    for slot in range(3):
        o_copy(slot).wait_send()

    @pl.when(z < Z_SIZE - 1)
    def _():
        for block in range(q_blocks):
            halo(block).wait_send()

    w_line.drain(True, True)
    w_line.drain(False, True)
    o_line.drain(True)
    o_line.drain(False)
    for step in range(Z_SIZE):
        for mate in range(len(MATES)):
            r_copy(step, mate).wait_send()


def layer(tokens, positions, w_query, key_matrix, value_matrix, w_out_t, gain_in, gain_query, gain_key, gain_post):
    own_tokens, model = tokens.shape
    depth = w_query.shape[0]
    columns, heads = w_out_t.shape
    head = HEAD_SIZE
    plane = 8 * own_tokens
    bf16, f32, dma = jnp.bfloat16, jnp.float32, pltpu.SemaphoreType.DMA
    frequency = jnp.asarray(ROPE_BASE ** (-2.0 * (np.arange(head) % (head // 2)) / head), f32)
    vmem, anywhere = pl.BlockSpec(memory_space=pltpu.VMEM), pl.BlockSpec(memory_space=pl.ANY)
    o_rows = O_CUTS[-1]
    return pl.pallas_call(
        layer_kernel,
        out_shape=jax.ShapeDtypeStruct((own_tokens, model), bf16),
        in_specs=[anywhere] * 5 + [vmem] * 6,
        out_specs=vmem,
        scratch_shapes=[
            pltpu.VMEM((own_tokens, model), bf16),
            pltpu.VMEM((plane, model), bf16),
            pltpu.VMEM((2, 2, depth, 2 * head), bf16),
            pltpu.VMEM((2, model, 2 * head), bf16),
            pltpu.VMEM((plane, 4 * head), f32),
            pltpu.VMEM((plane, 2 * head), bf16),
            pltpu.VMEM((2, 2 * plane, head), bf16),
            pltpu.VMEM((plane, 4 * heads), bf16),
            pltpu.VMEM((columns, heads), bf16),
            pltpu.VMEM((Z_SIZE, o_rows, 4 * heads), bf16),
            pltpu.VMEM((1, model), f32),
            pltpu.VMEM((1, model), f32),
            pltpu.VMEM((plane, head), f32),
            pltpu.VMEM((plane, head), f32),
            pltpu.VMEM((plane, head), f32),
            pltpu.VMEM((1, 2 * plane), f32),
            pltpu.VMEM((Z_SIZE, 8, o_rows, own_tokens), bf16),
            pltpu.VMEM((Z_SIZE, 8, o_rows, own_tokens), bf16),
            pltpu.VMEM((model, own_tokens), f32),
            dma((8,)), dma((2,)), dma((2,)), dma((2,)), dma((8,)), dma((8,)), dma((4,)), dma((4,)), dma((4, 8)), dma((4, 8)),
            dma((3,)), dma((3,)), dma((7 * Z_SIZE,)), dma((7 * Z_SIZE,)),
            *line_semaphores(W_PIECES), *line_semaphores(O_PIECES),
        ],
        compiler_params=pltpu.CompilerParams(
            collective_id=0, has_side_effects=True, vmem_limit_bytes=60 * 2**20
        ),
        name="layer",
    )(
        tokens, w_query, key_matrix, value_matrix, w_out_t,
        gain_in, gain_post,
        gain_query.reshape(1, -1), gain_key.reshape(1, -1),
        positions.reshape(-1, head), frequency.reshape(1, -1),
    )


def attend(query_matrix, projected_keys, projected_values, query_offsets, key_offsets, key_valid):
    scores = jnp.einsum(
        "qkgd,skd->kgqs", query_matrix, projected_keys, preferred_element_type=jnp.float32
    ) * QS ** (-0.5)
    position_gap = query_offsets[:, None] - key_offsets[None, :]
    allowed = key_valid[None, :] & (position_gap >= 0) & (position_gap < LOOKBACK_WINDOW)
    scores = jnp.where(allowed[None, None], scores, -1e30)
    row_max = jnp.max(scores, axis=-1, keepdims=True)
    weights = jnp.where(allowed[None, None], jnp.exp(scores - row_max), 0.0)
    totals = jnp.sum(weights, axis=-1, keepdims=True)
    rounded = weights.astype(jnp.bfloat16)
    mixed = jnp.einsum(
        "kgqs,skd->qkgd", rounded, projected_values, preferred_element_type=jnp.float32
    )
    mixed = mixed / jnp.transpose(totals, (2, 0, 1, 3))
    return mixed.astype(jnp.bfloat16).reshape(query_matrix.shape[0], -1)


def shards(
    tokens,
    positions,
    w_query,
    key_matrix,
    value_matrix,
    w_out,
    gain_in,
    gain_query,
    gain_key,
    gain_post,
):
    if lax.axis_size("ctx") == 2 * Z_SIZE and lax.axis_size("tp") == 4:
        return layer(
            tokens, positions, w_query, key_matrix, value_matrix, w_out.T,
            gain_in, gain_query, gain_key, gain_post,
        )
    normed = row_norm(tokens.astype(jnp.float32), gain_in).astype(jnp.bfloat16)
    normalized_rows = lax.all_gather(normed, "tp", axis=0, tiled=True)
    weights_in = lax.all_gather(
        jnp.concatenate([w_query, key_matrix, value_matrix], axis=1), "ctx", axis=0, tiled=True
    )
    row_count = normalized_rows.shape[0]
    block_start = lax.axis_index("ctx") * row_count
    offsets_all = positions - positions[0]
    query_offsets = lax.dynamic_slice_in_dim(offsets_all, block_start, row_count, 0)
    query_width, key_width = w_query.shape[1], key_matrix.shape[1]

    def add_rows(weights):
        return jnp.dot(normalized_rows, weights, preferred_element_type=jnp.float32)

    key_value_raw = add_rows(weights_in[:, query_width:])
    query_raw = add_rows(weights_in[:, :query_width])
    unnormed_keys = key_value_raw[:, :key_width]
    value_raw = key_value_raw[:, key_width:]
    key_heads = key_matrix.shape[1] // HEAD_SIZE
    projected_keys = rotate(
        row_norm(unnormed_keys.reshape(row_count, key_heads, HEAD_SIZE), gain_key), query_offsets
    ).astype(jnp.bfloat16)
    projected_values = value_raw.astype(jnp.bfloat16).reshape(row_count, key_heads, HEAD_SIZE)
    own_pair = jnp.stack([projected_keys, projected_values])
    window_blocks = LOOKBACK_WINDOW // row_count
    earlier = [shifted(own_pair, "ctx", steps) for steps in range(window_blocks, 0, -1)]
    window_pair = jnp.concatenate(earlier + [own_pair], axis=1)
    query_heads = w_query.shape[1] // HEAD_SIZE
    query_matrix = rotate(
        row_norm(query_raw.reshape(row_count, query_heads, HEAD_SIZE), gain_query), query_offsets
    ).astype(jnp.bfloat16)
    query_matrix = query_matrix.reshape(row_count, key_heads, query_heads // key_heads, HEAD_SIZE)
    padded_offsets = jnp.concatenate(
        [jnp.zeros((LOOKBACK_WINDOW,), jnp.int32), offsets_all], axis=0
    )
    key_offsets = lax.dynamic_slice_in_dim(
        padded_offsets, block_start, LOOKBACK_WINDOW + row_count, 0
    )
    key_valid = (
        block_start + jnp.arange(LOOKBACK_WINDOW + row_count, dtype=jnp.int32) >= LOOKBACK_WINDOW
    )
    attended = attend(
        query_matrix, window_pair[0], window_pair[1], query_offsets, key_offsets, key_valid
    )
    projected = jnp.dot(
        attended,
        lax.all_gather(w_out, "ctx", axis=1, tiled=True),
        preferred_element_type=jnp.float32,
    )
    summed = lax.psum_scatter(
        projected.astype(jnp.bfloat16), "tp", scatter_dimension=0, tiled=True
    ).astype(jnp.float32)
    return (tokens.astype(jnp.float32) + row_norm(summed, gain_post)).astype(jnp.bfloat16)


def solution(mesh):
    in_specs = (
        P(("ctx", "tp"), None),
        P(),
        P("ctx", "tp"),
        P("ctx", "tp"),
        P("ctx", "tp"),
        P("tp", "ctx"),
        P(),
        P(),
        P(),
        P(),
    )
    out_specs = P(("ctx", "tp"), None)
    return jax.shard_map(shards, mesh=mesh, in_specs=in_specs, out_specs=out_specs, check_vma=False)
```

```python
import jax
import jax.numpy as jnp
import numpy as np
from jax import lax
from jax.experimental import pallas as pl
from jax.experimental.pallas import tpu as pltpu
from jax.sharding import PartitionSpec as P

HEAD_SIZE = 128
QS = 168
LOOKBACK_WINDOW = 1024


EPSILON = 1e-06
ROPE_BASE = 10000.0


def shifted(value, axis, steps):
    count = lax.axis_size(axis)
    leading, last = (max(0, -steps), min(count, count - steps))
    return lax.ppermute(value, axis, [(source, source + steps) for source in range(leading, last)])


def row_norm(values, scales):
    mean_square = jnp.mean(values * values, axis=-1, keepdims=True)
    return values * lax.rsqrt(mean_square + EPSILON) * scales


def rotate(head_rows, offsets):
    half_dim = head_rows.shape[-1] // 2
    frequency = ROPE_BASE ** (
        -(jnp.arange(half_dim, dtype=jnp.float32) * 2.0) / head_rows.shape[-1]
    )
    angles = offsets.astype(jnp.float32)[:, None] * frequency[None, :]
    cosine = jnp.cos(angles)[:, None, :]
    sine_wave = jnp.sin(angles)[:, None, :]
    first_half = head_rows[..., :half_dim]
    second_half = head_rows[..., half_dim:]
    return jnp.concatenate(
        [
            first_half * cosine - second_half * sine_wave,
            second_half * cosine + first_half * sine_wave,
        ],
        axis=-1,
    )


Z_SIZE = 4
TILE = 16
W_PIECES = 4
O_PIECES = 3
O_CUTS = (0, 112, 160, 176)
MATES = [(i // 4, i // 2 % 2, i % 2) for i in range(1, 8)]
MESH = pl.DeviceIdType.MESH
FAR_KEY = 1e9


def remote(source, target, send, recv, device):
    return pltpu.make_async_remote_copy(
        src_ref=source, dst_ref=target, send_sem=send, recv_sem=recv,
        device_id=device, device_id_type=MESH,
    )


def aligned(value, size, step=TILE):
    return pl.ds(pl.multiple_of(value, step), size)


class Places:
    def __init__(self):
        self.ctx = lax.axis_index("ctx")
        self.tp = lax.axis_index("tp")
        self.z, self.y = self.ctx // 2, self.ctx % 2
        self.x, self.c = self.tp // 2, self.tp % 2
        self.core_id = self.mate(0, 0, 1)
        self.x_id = self.mate(0, 1, 0)
        self.y_id = self.mate(1, 0, 0)
        self.diag_id = self.mate(1, 0, 1)
        self.up_id = (self.ctx + 2, self.tp)
        self.down_id = (self.ctx - 2, self.tp)

    def mate(self, dy, dx, dc):
        row, column, core = ((v + d) % 2 for v, d in ((self.y, dy), (self.x, dx), (self.c, dc)))
        return (self.z * 2 + row, column * 2 + core)

    def greet(self):
        barrier = pltpu.get_barrier_semaphore()

        def signal(target):
            pl.semaphore_signal(barrier, inc=1, device_id=target, device_id_type=MESH)

        for dy, dx, dc in MATES:
            signal(self.mate(dy, dx, dc))

        @pl.when(self.z < Z_SIZE - 1)
        def _():
            signal(self.up_id)

        @pl.when(self.z > 0)
        def _():
            signal(self.down_id)

    def meet(self):
        middle = ((self.z + 1) // 2) % 2
        pl.semaphore_wait(pltpu.get_barrier_semaphore(), 8 + middle)


class Line:
    def __init__(self, places, piece_ref, pieces, sems, guard=None):
        self.at, self.piece_ref, self.pieces = places, piece_ref, pieces
        self.guard = guard or (lambda piece, condition: condition)
        self.up_send, self.down_send, self.below, self.above = sems

    def copy(self, plane, distance, piece, upward):
        ref = self.piece_ref(plane, piece)
        slot = distance * self.pieces + piece
        if upward:
            return remote(ref, ref, self.up_send.at[slot], self.below.at[slot], self.at.up_id)
        return remote(ref, ref, self.down_send.at[slot], self.above.at[slot], self.at.down_id)

    def send_own(self, piece, upward=True, downward=True):
        z = self.at.z
        if upward:
            @pl.when(self.guard(piece, z < Z_SIZE - 1))
            def _():
                self.copy(z, 0, piece, True).start()

        if downward:
            @pl.when(self.guard(piece, z > 0))
            def _():
                self.copy(z, 0, piece, False).start()

    def forward(self, distance, piece):
        z = self.at.z
        if distance == Z_SIZE - 1:
            return

        @pl.when(self.guard(piece, (z >= distance) & (z < Z_SIZE - 1)))
        def _():
            self.copy(z - distance, distance - 1, piece, True).wait_recv()
            self.copy(z - distance, distance, piece, True).start()

        @pl.when(self.guard(piece, (z + distance < Z_SIZE) & (z > 0)))
        def _():
            self.copy(z + distance, distance - 1, piece, False).wait_recv()
            self.copy(z + distance, distance, piece, False).start()

    def arrive(self, distance, piece):
        z = self.at.z

        @pl.when(self.guard(piece, z == Z_SIZE - 1))
        def _():
            self.copy(z - distance, distance - 1, piece, True).wait_recv()

        @pl.when(self.guard(piece, z == 0))
        def _():
            self.copy(z + distance, distance - 1, piece, False).wait_recv()

    def drain(self, upward, last=None):
        z = self.at.z
        final = (Z_SIZE - 2, self.pieces - 1)
        for distance in range(Z_SIZE - 1):
            for piece in range(self.pieces):
                if last is not None and last != ((distance, piece) == final):
                    continue
                if upward:
                    plane, sent = z - distance, (z < Z_SIZE - 1) & (z >= distance)
                else:
                    plane, sent = z + distance, (z > 0) & (z + distance < Z_SIZE)

                @pl.when(self.guard(piece, sent))
                def _():
                    self.copy(plane, distance, piece, upward).wait_send()


class PlaneGather:
    def __init__(self, places, block_ref, send, recv):
        self.at, self.block_ref, self.send, self.recv = places, block_ref, send, recv

    def copy(self, slot):
        device, (dy, dx), part = (
            (self.at.x_id, (0, 0), None), (self.at.y_id, (0, 0), None),
            (self.at.x_id, (1, 0), 0), (self.at.y_id, (0, 1), 1),
            (self.at.core_id, (0, 0), None), (self.at.core_id, (0, 1), None),
            (self.at.core_id, (1, 0), None), (self.at.core_id, (1, 1), None),
        )[slot]
        ref = self.block_ref((self.at.y + dy) % 2, (self.at.x + dx) % 2, self.at.c, part)
        return remote(ref, ref, self.send.at[slot], self.recv.at[slot], device)

    def start(self, *slots):
        for slot in slots:
            self.copy(slot).start()

    def arrive(self, *slots):
        for slot in slots:
            (dy, dx, dc), part = (
                ((0, 1, 0), None), ((1, 0, 0), None), ((1, 1, 0), 0), ((1, 1, 0), 1),
                ((0, 0, 1), None), ((0, 1, 1), None), ((1, 0, 1), None), ((1, 1, 1), None),
            )[slot]
            ref = self.block_ref(
                (self.at.y + dy) % 2, (self.at.x + dx) % 2, (self.at.c + dc) % 2, part
            )
            remote(ref, ref, self.send.at[slot], self.recv.at[slot], self.at.core_id).wait_recv()

    def drain(self):
        for slot in range(8):
            self.copy(slot).wait_send()


def line_semaphores(pieces):
    return [pltpu.SemaphoreType.DMA(((Z_SIZE - 1) * pieces,)) for _ in range(4)]


def layer_kernel(
    tok_ref, wq_ref, wk_ref, wv_ref, wo_ref, gin_ref, gpost_ref, gq_ref, gk_ref, pos_ref, freq_ref,
    out_ref,
    xs, x_all, ws, w_all, acc, queries, kv, att_all, wo_own, wo_all, gin, gpost,
    cos_t, sin_t, q_off, k_off, result, got, turned_out,
    stage_sem, local_sem, w_send, w_recv, x_send, x_recv, halo_send, halo_recv, att_send, att_recv,
    o_send, o_recv, r_send, r_recv,
    *line_sems,
):
    at = Places()
    z, y, x, c = at.z, at.y, at.x, at.c
    same = c == y
    depth = wq_ref.shape[0]
    own_tokens, model = xs.shape
    plane_tokens = x_all.shape[0]
    head = HEAD_SIZE
    f32, bf16 = jnp.float32, jnp.bfloat16
    at.greet()

    loads = []
    for half in range(2):
        for ref, part, begin, width in (
            (wk_ref, 0, 0, head), (wv_ref, 0, head, head), (wq_ref, 1, 0, 2 * head)
        ):
            loads.append(pltpu.make_async_copy(
                ref.at[:, pl.ds(half * width, width)],
                ws.at[half, part, :, pl.ds(begin, width)],
                stage_sem.at[len(loads)],
            ))
    tok_load = pltpu.make_async_copy(tok_ref, xs, stage_sem.at[6])
    wo_load = pltpu.make_async_copy(wo_ref, wo_own, stage_sem.at[7])
    for copy in loads + [tok_load, wo_load]:
        copy.start()
    for copy in loads:
        copy.wait()
    at.meet()

    def block_rows(plane, row):
        return w_all.at[:, aligned((plane * 2 + row) * depth, depth)]

    def near_copy():
        return remote(ws.at[1 - c], block_rows(z, y), w_send.at[0], w_recv.at[0], at.core_id)

    def far_copy(target):
        block = block_rows(z, y) if target is not None else block_rows(z, 1 - y)
        device = at.y_id if target is None else target
        if target is at.diag_id:
            return remote(ws.at[1 - c], block, w_send.at[1], w_recv.at[1], device)
        return remote(ws.at[c], block, w_send.at[0], w_recv.at[1], device)

    own_block = pltpu.make_async_copy(ws.at[c], block_rows(z, y), local_sem.at[0])

    @pl.when(same)
    def _():
        near_copy().start()
        own_block.start()

    @pl.when(jnp.logical_not(same))
    def _():
        far_copy(at.y_id).start()
        far_copy(at.diag_id).start()


    def w_piece(plane, piece):
        row = (at.y + piece % 2) % 2
        return w_all.at[piece // 2, aligned((plane * 2 + row) * depth, depth)]

    def o_piece(plane, piece):
        return wo_all.at[plane, pl.ds(O_CUTS[piece], O_CUTS[piece + 1] - O_CUTS[piece])]

    w_line = Line(at, w_piece, W_PIECES, line_sems[:4])
    o_line = Line(
        at, o_piece, O_PIECES, line_sems[4:],
        lambda piece, condition: condition & (c == 1) if piece == O_PIECES - 1 else condition,
    )

    @pl.when(same)
    def _():
        own_block.wait()

    @pl.when(jnp.logical_not(same))
    def _():
        near_copy().wait_recv()

    w_line.send_own(0)
    w_line.send_own(2)

    def block_of(row, column, core):
        return (row * 4 + column * 2 + core) * own_tokens

    tok_load.wait()
    gin[...] = gin_ref[...].reshape(1, model)
    gpost[...] = gpost_ref[...].reshape(1, model)
    own_begin = block_of(y, x, c)

    @pl.loop(0, own_tokens // TILE)
    def _(step):
        v = xs[aligned(step * TILE, TILE), :].astype(f32)
        mean_square = jnp.mean(v * v, axis=-1, keepdims=True)
        x_all[aligned(own_begin + step * TILE, TILE), :] = (
            v * lax.rsqrt(mean_square + EPSILON) * gin[...]
        ).astype(bf16)

    cut = own_tokens * 3 // 4

    def x_block(row, column, core, part):
        begin, size = ((0, own_tokens), (0, cut), (cut, own_tokens - cut))[0 if part is None else part + 1]
        return x_all.at[aligned(block_of(row, column, core) + begin, size)]

    tokens = PlaneGather(at, x_block, x_send, x_recv)
    tokens.start(0, 1, 4)

    o_rows = O_CUTS[-1]
    o_width = wo_own.shape[1]

    def o_copy(slot):
        dx, dc = ((0, 1), (1, 0), (1, 1))[slot]
        part = (x + dx) % 2 * 2 + (c + dc) % 2
        begin = part * (depth // TILE) // 4 * TILE
        return remote(
            wo_own.at[aligned(begin, o_rows)],
            wo_all.at[z, :, aligned((x * 2 + c) * o_width, o_width, 128)],
            o_send.at[slot], o_recv.at[slot], at.mate(0, dx, dc),
        )

    def o_arrive(slot):
        dx, dc = ((0, 1), (1, 0), (1, 1))[slot]
        part = (x + dx) % 2 * 2 + (c + dc) % 2
        block = wo_all.at[z, :, aligned(part * o_width, o_width, 128)]
        remote(block, block, o_send.at[slot], o_recv.at[slot], at.mate(0, dx, dc)).wait_recv()

    wo_load.wait()
    for slot in range(3):
        o_copy(slot).start()
    own_part = x * 2 + c
    keep_o = pltpu.make_async_copy(
        wo_own.at[aligned(own_part * (depth // TILE) // 4 * TILE, o_rows)],
        wo_all.at[z, :, aligned(own_part * o_width, o_width, 128)],
        local_sem.at[1],
    )
    keep_o.start()

    far_copy(None).wait_recv()
    w_line.send_own(1)
    w_line.send_own(3)
    middle = (z == 1) | (z == 2)

    first = pos_ref[0:1, 0:1]
    blocks = plane_tokens // head

    @pl.loop(0, blocks)
    def _(block):
        row = (pos_ref[pl.ds(z * blocks + block, 1), :] - first).astype(f32)
        column = jnp.broadcast_to(row, (head, head)).T
        here = aligned(block * head, head)
        q_off[here, :] = column
        angles = column * freq_ref[...]
        cos_t[here, :] = jnp.cos(angles)
        lane = lax.broadcasted_iota(jnp.int32, (head, head), 1)
        sine = jnp.sin(angles)
        sin_t[here, :] = jnp.where(lane < head // 2, -sine, sine)

    for block in range(2 * blocks):
        index = jnp.maximum((z - 1) * blocks + block, 0)
        row = (pos_ref[pl.ds(index, 1), :] - first).astype(f32)
        if block < blocks:
            row = jnp.where(z > 0, row, FAR_KEY)
        k_off[:, block * head:(block + 1) * head] = row

    @pl.when(z == 0)
    def _():
        kv[:, pl.ds(0, plane_tokens), :] = jnp.zeros((2, plane_tokens, head), bf16)

    for piece in range(2):
        w_line.forward(1, piece)

    tokens.arrive(0)
    tokens.start(3, 5)
    for piece in range(2):
        w_line.forward(2, piece)
    tokens.arrive(1)
    tokens.start(2, 6)
    for distance in (1, 2):
        for piece in range(2, W_PIECES):
            w_line.forward(distance, piece)
    keep_o.wait()
    for slot in range(3):
        o_arrive(slot)

    @pl.when(jnp.logical_not(middle))
    def _():
        for piece in range(O_PIECES):
            o_line.send_own(piece)

    tokens.arrive(2, 3)
    tokens.start(7)
    tokens.arrive(4, 5, 6, 7)

    pair_depth = 4 * depth
    row_step = plane_tokens // 2

    def multiply(part, pair, add):
        @pl.loop(0, plane_tokens // row_step)
        def _(step):
            rows = aligned(step * row_step, row_step)
            product = jnp.dot(
                x_all[rows, aligned(pair * pair_depth, pair_depth, 128)],
                w_all[part, aligned(pair * pair_depth, pair_depth), :],
                preferred_element_type=f32,
            )
            columns = slice(part * 2 * head, (part + 1) * 2 * head)
            acc[rows, columns] = acc[rows, columns] + product if add else product

    def turned(v, gain, cosine, sine):
        mean_square = jnp.mean(v * v, axis=-1, keepdims=True)
        v = v * lax.rsqrt(mean_square + EPSILON) * gain
        return (v * cosine + pltpu.roll(v, head // 2, 1) * sine).astype(bf16)

    for distance in range(1, Z_SIZE):
        for piece in range(2):
            w_line.arrive(distance, piece)
    multiply(0, z // 2, False)
    multiply(0, 1 - z // 2, True)

    @pl.loop(0, blocks)
    def _(block):
        here = aligned(block * head, head)
        own = aligned(plane_tokens + block * head, head)
        kv[0, own, :] = turned(acc[here, 0:head], gk_ref[...], cos_t[here, :], sin_t[here, :])
        kv[1, own, :] = acc[here, head:2 * head].astype(bf16)

    q_step = 2 * own_tokens
    q_blocks = plane_tokens // q_step
    span = LOOKBACK_WINDOW + q_step

    def halo(block):
        return remote(
            kv.at[:, pl.ds(plane_tokens + block * q_step, q_step)],
            kv.at[:, pl.ds(block * q_step, q_step)],
            halo_send.at[block], halo_recv.at[block], at.up_id,
        )

    @pl.when(z < Z_SIZE - 1)
    def _():
        for block in reversed(range(q_blocks)):
            halo(block).start()

    def pass_o(upward):
        w_line.drain(upward, False)
        for piece in range(O_PIECES):
            o_line.send_own(piece, upward, not upward)

    @pl.when(z == 1)
    def _():
        pass_o(True)

    @pl.when(z == 2)
    def _():
        pass_o(False)

    for piece in range(2, W_PIECES):
        w_line.arrive(1, piece)
    multiply(1, z // 2, False)
    for distance in range(2, Z_SIZE):
        for piece in range(2, W_PIECES):
            w_line.arrive(distance, piece)
    multiply(1, 1 - z // 2, True)

    @pl.loop(0, blocks)
    def _(block):
        here = aligned(block * head, head)
        for h in range(2):
            raw = acc[here, (h + 2) * head:(h + 3) * head]
            queries[here, h * head:(h + 1) * head] = turned(
                raw, gq_ref[...], cos_t[here, :], sin_t[here, :]
            )

    width = 2 * head

    def att_block(block):
        def ref(row, column, core, part):
            half = q_step // 2
            begin, size = ((0, q_step), (0, half), (half, half))[0 if part is None else part + 1]
            return att_all.at[
                pl.ds(block * q_step + begin, size),
                aligned((column * 4 + row * 2 + core) * width, width, 128),
            ]

        return ref

    attended = [
        PlaneGather(at, att_block(block), att_send.at[block], att_recv.at[block])
        for block in range(q_blocks)
    ]
    own_heads = (x * 4 + y * 2 + c) * width

    def attend_block(block):
        rows, keys = pl.ds(block * q_step, q_step), pl.ds(block * q_step, span)
        gap = q_off[rows, 0:1] - k_off[:, keys]
        allowed = (gap >= 0) & (gap < LOOKBACK_WINDOW)
        k_rows, v_rows = kv[0, keys, :], kv[1, keys, :]
        for h in range(2):
            scores = lax.dot_general(
                queries[rows, h * head:(h + 1) * head], k_rows, (((1,), (1,)), ((), ())),
                preferred_element_type=f32,
            ) * QS ** (-0.5)
            scores = jnp.where(allowed, scores, -1e30)
            weights = jnp.exp(scores - jnp.max(scores, axis=-1, keepdims=True))
            totals = jnp.sum(weights, axis=-1, keepdims=True)
            mixed = jnp.dot(weights.astype(bf16), v_rows, preferred_element_type=f32) / totals
            att_all[rows, aligned(own_heads + h * head, head, 128)] = mixed.astype(bf16)

    def hand_on(block):
        attended[block].arrive(0)
        attended[block].start(3, 5)
        attended[block].arrive(1)
        attended[block].start(2, 6)

    def hand_across(block):
        attended[block].arrive(2, 3)
        attended[block].start(7)

    @pl.when(z == 1)
    def _():
        pass_o(False)

    for block in reversed(range(q_blocks)):
        @pl.when(z > 0)
        def _():
            halo(block).wait_recv()

        attend_block(block)
        attended[block].start(0, 1, 4)
        if block + 1 < q_blocks:
            hand_on(block + 1)
        if block + 2 < q_blocks:
            hand_across(block + 2)

    @pl.when(z == 2)
    def _():
        pass_o(True)

    @pl.when(middle)
    def _():
        for distance in (1, 2):
            for piece in range(O_PIECES):
                o_line.forward(distance, piece)

    @pl.when(jnp.logical_not(middle))
    def _():
        w_line.drain(True, False)
        w_line.drain(False, False)

    hand_on(0)
    hand_across(1)
    hand_across(0)
    for gather in attended:
        gather.arrive(4, 5, 6, 7)

    planes = [z, z + 1 - 2 * (z % 2), (z + 2) % 4, 3 - z]
    own_index = y * 4 + x * 2 + c

    def part_rows(part):
        return ((0, o_rows), (0, O_CUTS[1]), (O_CUTS[1], o_rows))[part]

    def r_refs(step, part, mate):
        dy, dx, dc = MATES[mate]
        owner = (y + dy) % 2 * 4 + (x + dx) % 2 * 2 + (c + dc) % 2
        begin, end = part_rows(part)
        rows = pl.ds(begin, end - begin)
        slot = (step + part // 2) * len(MATES) + mate
        return owner, rows, r_send.at[slot], r_recv.at[slot]

    def r_copy(step, part, mate):
        owner, rows, send, recv = r_refs(step, part, mate)
        return remote(
            result.at[step, owner, rows], got.at[step, own_index, rows], send, recv,
            at.mate(*MATES[mate]),
        )

    def r_arrive(step, part, mate):
        owner, rows, send, recv = r_refs(step, part, mate)
        block = got.at[step, owner, rows]
        remote(block, block, send, recv, at.core_id).wait_recv()

    def project(step, part=0):
        begin, end = part_rows(part)
        sums = lax.dot_general(
            wo_all[planes[step], begin:end], att_all[...], (((1,), (1,)), ((), ())),
            preferred_element_type=f32,
        ).astype(bf16)
        for owner in range(8):
            result[step, owner, begin:end] = sums[:, owner * own_tokens:(owner + 1) * own_tokens]
        for mate in range(len(MATES)):
            r_copy(step, part, mate).start()
        got[step, own_index, begin:end] = result[step, own_index, begin:end]

    def finish(step, square, part=0):
        for mate in range(len(MATES)):
            r_arrive(step, part, mate)
        for owner in range(8):
            row, quarter = owner // 4, owner % 4
            start = quarter * (depth // TILE) // 4 * TILE
            size = (quarter + 1) * (depth // TILE) // 4 * TILE - start
            begin, end = part_rows(part)
            end = min(end, size)
            v = got[step, owner, begin:end].astype(f32)
            there = (planes[step] * 2 + row) * depth + start + begin
            turned_out[aligned(there, end - begin), :] = v
            square = square + jnp.sum(v * v, axis=0, keepdims=True)
        return square

    square = jnp.zeros((1, own_tokens), f32)
    last = Z_SIZE - 1
    for step in range(last):
        if step > 0:
            for piece in range(O_PIECES):
                o_line.arrive(step, piece)
        project(step)
        if step > 0:
            square = finish(step - 1, square)
    o_line.arrive(last, 0)
    project(last, 1)
    square = finish(last - 1, square)
    for piece in range(1, O_PIECES):
        o_line.arrive(last, piece)
    project(last, 2)
    square = finish(last, square, 1)
    square = finish(last, square, 2)

    scale = lax.rsqrt(square / model + EPSILON)
    for begin in range(0, model, head):
        columns = slice(begin, begin + head)
        normed = (turned_out[columns, :] * scale).T * gpost[:, columns]
        out_ref[:, columns] = (xs[:, columns].astype(f32) + normed).astype(bf16)

    @pl.when(same)
    def _():
        near_copy().wait_send()

    @pl.when(jnp.logical_not(same))
    def _():
        far_copy(at.y_id).wait_send()
        far_copy(at.diag_id).wait_send()

    tokens.drain()
    for gather in attended:
        gather.drain()
    for slot in range(3):
        o_copy(slot).wait_send()

    @pl.when(z < Z_SIZE - 1)
    def _():
        for block in range(q_blocks):
            halo(block).wait_send()

    w_line.drain(True, True)
    w_line.drain(False, True)
    o_line.drain(True)
    o_line.drain(False)
    for step, part in [(step, 0) for step in range(last)] + [(last, 1), (last, 2)]:
        for mate in range(len(MATES)):
            r_copy(step, part, mate).wait_send()


def layer(tokens, positions, w_query, key_matrix, value_matrix, w_out_t, gain_in, gain_query, gain_key, gain_post):
    own_tokens, model = tokens.shape
    depth = w_query.shape[0]
    columns, heads = w_out_t.shape
    head = HEAD_SIZE
    plane = 8 * own_tokens
    bf16, f32, dma = jnp.bfloat16, jnp.float32, pltpu.SemaphoreType.DMA
    frequency = jnp.asarray(ROPE_BASE ** (-2.0 * (np.arange(head) % (head // 2)) / head), f32)
    vmem, anywhere = pl.BlockSpec(memory_space=pltpu.VMEM), pl.BlockSpec(memory_space=pl.ANY)
    o_rows = O_CUTS[-1]
    return pl.pallas_call(
        layer_kernel,
        out_shape=jax.ShapeDtypeStruct((own_tokens, model), bf16),
        in_specs=[anywhere] * 5 + [vmem] * 6,
        out_specs=vmem,
        scratch_shapes=[
            pltpu.VMEM((own_tokens, model), bf16),
            pltpu.VMEM((plane, model), bf16),
            pltpu.VMEM((2, 2, depth, 2 * head), bf16),
            pltpu.VMEM((2, model, 2 * head), bf16),
            pltpu.VMEM((plane, 4 * head), f32),
            pltpu.VMEM((plane, 2 * head), bf16),
            pltpu.VMEM((2, 2 * plane, head), bf16),
            pltpu.VMEM((plane, 4 * heads), bf16),
            pltpu.VMEM((columns, heads), bf16),
            pltpu.VMEM((Z_SIZE, o_rows, 4 * heads), bf16),
            pltpu.VMEM((1, model), f32),
            pltpu.VMEM((1, model), f32),
            pltpu.VMEM((plane, head), f32),
            pltpu.VMEM((plane, head), f32),
            pltpu.VMEM((plane, head), f32),
            pltpu.VMEM((1, 2 * plane), f32),
            pltpu.VMEM((Z_SIZE, 8, o_rows, own_tokens), bf16),
            pltpu.VMEM((Z_SIZE, 8, o_rows, own_tokens), bf16),
            pltpu.VMEM((model, own_tokens), f32),
            dma((8,)), dma((2,)), dma((2,)), dma((2,)), dma((8,)), dma((8,)), dma((4,)), dma((4,)), dma((4, 8)), dma((4, 8)),
            dma((3,)), dma((3,)), dma((7 * Z_SIZE + 7,)), dma((7 * Z_SIZE + 7,)),
            *line_semaphores(W_PIECES), *line_semaphores(O_PIECES),
        ],
        compiler_params=pltpu.CompilerParams(
            collective_id=0, has_side_effects=True, vmem_limit_bytes=60 * 2**20
        ),
        name="layer",
    )(
        tokens, w_query, key_matrix, value_matrix, w_out_t,
        gain_in, gain_post,
        gain_query.reshape(1, -1), gain_key.reshape(1, -1),
        positions.reshape(-1, head), frequency.reshape(1, -1),
    )


def attend(query_matrix, projected_keys, projected_values, query_offsets, key_offsets, key_valid):
    scores = jnp.einsum(
        "qkgd,skd->kgqs", query_matrix, projected_keys, preferred_element_type=jnp.float32
    ) * QS ** (-0.5)
    position_gap = query_offsets[:, None] - key_offsets[None, :]
    allowed = key_valid[None, :] & (position_gap >= 0) & (position_gap < LOOKBACK_WINDOW)
    scores = jnp.where(allowed[None, None], scores, -1e30)
    row_max = jnp.max(scores, axis=-1, keepdims=True)
    weights = jnp.where(allowed[None, None], jnp.exp(scores - row_max), 0.0)
    totals = jnp.sum(weights, axis=-1, keepdims=True)
    rounded = weights.astype(jnp.bfloat16)
    mixed = jnp.einsum(
        "kgqs,skd->qkgd", rounded, projected_values, preferred_element_type=jnp.float32
    )
    mixed = mixed / jnp.transpose(totals, (2, 0, 1, 3))
    return mixed.astype(jnp.bfloat16).reshape(query_matrix.shape[0], -1)


def shards(
    tokens,
    positions,
    w_query,
    key_matrix,
    value_matrix,
    w_out,
    gain_in,
    gain_query,
    gain_key,
    gain_post,
):
    if lax.axis_size("ctx") == 2 * Z_SIZE and lax.axis_size("tp") == 4:
        return layer(
            tokens, positions, w_query, key_matrix, value_matrix, w_out.T,
            gain_in, gain_query, gain_key, gain_post,
        )
    normed = row_norm(tokens.astype(jnp.float32), gain_in).astype(jnp.bfloat16)
    normalized_rows = lax.all_gather(normed, "tp", axis=0, tiled=True)
    weights_in = lax.all_gather(
        jnp.concatenate([w_query, key_matrix, value_matrix], axis=1), "ctx", axis=0, tiled=True
    )
    row_count = normalized_rows.shape[0]
    block_start = lax.axis_index("ctx") * row_count
    offsets_all = positions - positions[0]
    query_offsets = lax.dynamic_slice_in_dim(offsets_all, block_start, row_count, 0)
    query_width, key_width = w_query.shape[1], key_matrix.shape[1]

    def add_rows(weights):
        return jnp.dot(normalized_rows, weights, preferred_element_type=jnp.float32)

    key_value_raw = add_rows(weights_in[:, query_width:])
    query_raw = add_rows(weights_in[:, :query_width])
    unnormed_keys = key_value_raw[:, :key_width]
    value_raw = key_value_raw[:, key_width:]
    key_heads = key_matrix.shape[1] // HEAD_SIZE
    projected_keys = rotate(
        row_norm(unnormed_keys.reshape(row_count, key_heads, HEAD_SIZE), gain_key), query_offsets
    ).astype(jnp.bfloat16)
    projected_values = value_raw.astype(jnp.bfloat16).reshape(row_count, key_heads, HEAD_SIZE)
    own_pair = jnp.stack([projected_keys, projected_values])
    window_blocks = LOOKBACK_WINDOW // row_count
    earlier = [shifted(own_pair, "ctx", steps) for steps in range(window_blocks, 0, -1)]
    window_pair = jnp.concatenate(earlier + [own_pair], axis=1)
    query_heads = w_query.shape[1] // HEAD_SIZE
    query_matrix = rotate(
        row_norm(query_raw.reshape(row_count, query_heads, HEAD_SIZE), gain_query), query_offsets
    ).astype(jnp.bfloat16)
    query_matrix = query_matrix.reshape(row_count, key_heads, query_heads // key_heads, HEAD_SIZE)
    padded_offsets = jnp.concatenate(
        [jnp.zeros((LOOKBACK_WINDOW,), jnp.int32), offsets_all], axis=0
    )
    key_offsets = lax.dynamic_slice_in_dim(
        padded_offsets, block_start, LOOKBACK_WINDOW + row_count, 0
    )
    key_valid = (
        block_start + jnp.arange(LOOKBACK_WINDOW + row_count, dtype=jnp.int32) >= LOOKBACK_WINDOW
    )
    attended = attend(
        query_matrix, window_pair[0], window_pair[1], query_offsets, key_offsets, key_valid
    )
    projected = jnp.dot(
        attended,
        lax.all_gather(w_out, "ctx", axis=1, tiled=True),
        preferred_element_type=jnp.float32,
    )
    summed = lax.psum_scatter(
        projected.astype(jnp.bfloat16), "tp", scatter_dimension=0, tiled=True
    ).astype(jnp.float32)
    return (tokens.astype(jnp.float32) + row_norm(summed, gain_post)).astype(jnp.bfloat16)


def solution(mesh):
    in_specs = (
        P(("ctx", "tp"), None),
        P(),
        P("ctx", "tp"),
        P("ctx", "tp"),
        P("ctx", "tp"),
        P("tp", "ctx"),
        P(),
        P(),
        P(),
        P(),
    )
    out_specs = P(("ctx", "tp"), None)
    return jax.shard_map(shards, mesh=mesh, in_specs=in_specs, out_specs=out_specs, check_vma=False)
```

```python
import jax
import jax.numpy as jnp
import numpy as np
from jax import lax
from jax.experimental import pallas as pl
from jax.experimental.pallas import tpu as pltpu
from jax.sharding import PartitionSpec as P

HEAD_SIZE = 128
QS = 168
LOOKBACK_WINDOW = 1024


EPSILON = 1e-06
ROPE_BASE = 10000.0


def shifted(value, axis, steps):
    count = lax.axis_size(axis)
    leading, last = (max(0, -steps), min(count, count - steps))
    return lax.ppermute(value, axis, [(source, source + steps) for source in range(leading, last)])


def row_norm(values, scales):
    mean_square = jnp.mean(values * values, axis=-1, keepdims=True)
    return values * lax.rsqrt(mean_square + EPSILON) * scales


def rotate(head_rows, offsets):
    half_dim = head_rows.shape[-1] // 2
    frequency = ROPE_BASE ** (
        -(jnp.arange(half_dim, dtype=jnp.float32) * 2.0) / head_rows.shape[-1]
    )
    angles = offsets.astype(jnp.float32)[:, None] * frequency[None, :]
    cosine = jnp.cos(angles)[:, None, :]
    sine_wave = jnp.sin(angles)[:, None, :]
    first_half = head_rows[..., :half_dim]
    second_half = head_rows[..., half_dim:]
    return jnp.concatenate(
        [
            first_half * cosine - second_half * sine_wave,
            second_half * cosine + first_half * sine_wave,
        ],
        axis=-1,
    )


Z_SIZE = 4
TILE = 16
W_PIECES = 4
O_PIECES = 3
O_CUTS = (0, 112, 160, 176)
MATES = [(i // 4, i // 2 % 2, i % 2) for i in range(1, 8)]
MESH = pl.DeviceIdType.MESH
FAR_KEY = 1e9


def remote(source, target, send, recv, device):
    return pltpu.make_async_remote_copy(
        src_ref=source, dst_ref=target, send_sem=send, recv_sem=recv,
        device_id=device, device_id_type=MESH,
    )


def aligned(value, size, step=TILE):
    return pl.ds(pl.multiple_of(value, step), size)


class Places:
    def __init__(self):
        self.ctx = lax.axis_index("ctx")
        self.tp = lax.axis_index("tp")
        self.z, self.y = self.ctx // 2, self.ctx % 2
        self.x, self.c = self.tp // 2, self.tp % 2
        self.core_id = self.mate(0, 0, 1)
        self.x_id = self.mate(0, 1, 0)
        self.y_id = self.mate(1, 0, 0)
        self.diag_id = self.mate(1, 0, 1)
        self.up_id = (self.ctx + 2, self.tp)
        self.down_id = (self.ctx - 2, self.tp)

    def mate(self, dy, dx, dc):
        row, column, core = ((v + d) % 2 for v, d in ((self.y, dy), (self.x, dx), (self.c, dc)))
        return (self.z * 2 + row, column * 2 + core)

    def greet(self):
        barrier = pltpu.get_barrier_semaphore()

        def signal(target):
            pl.semaphore_signal(barrier, inc=1, device_id=target, device_id_type=MESH)

        for dy, dx, dc in MATES:
            signal(self.mate(dy, dx, dc))

        @pl.when(self.z < Z_SIZE - 1)
        def _():
            signal(self.up_id)

        @pl.when(self.z > 0)
        def _():
            signal(self.down_id)

    def meet(self):
        middle = ((self.z + 1) // 2) % 2
        pl.semaphore_wait(pltpu.get_barrier_semaphore(), 8 + middle)


class Line:
    def __init__(self, places, piece_ref, pieces, sems, guard=None):
        self.at, self.piece_ref, self.pieces = places, piece_ref, pieces
        self.guard = guard or (lambda piece, condition: condition)
        self.up_send, self.down_send, self.below, self.above = sems

    def copy(self, plane, distance, piece, upward):
        ref = self.piece_ref(plane, piece)
        slot = distance * self.pieces + piece
        if upward:
            return remote(ref, ref, self.up_send.at[slot], self.below.at[slot], self.at.up_id)
        return remote(ref, ref, self.down_send.at[slot], self.above.at[slot], self.at.down_id)

    def send_own(self, piece, upward=True, downward=True):
        z = self.at.z
        if upward:
            @pl.when(self.guard(piece, z < Z_SIZE - 1))
            def _():
                self.copy(z, 0, piece, True).start()

        if downward:
            @pl.when(self.guard(piece, z > 0))
            def _():
                self.copy(z, 0, piece, False).start()

    def forward(self, distance, piece):
        z = self.at.z
        if distance == Z_SIZE - 1:
            return

        @pl.when(self.guard(piece, (z >= distance) & (z < Z_SIZE - 1)))
        def _():
            self.copy(z - distance, distance - 1, piece, True).wait_recv()
            self.copy(z - distance, distance, piece, True).start()

        @pl.when(self.guard(piece, (z + distance < Z_SIZE) & (z > 0)))
        def _():
            self.copy(z + distance, distance - 1, piece, False).wait_recv()
            self.copy(z + distance, distance, piece, False).start()

    def arrive(self, distance, piece):
        z = self.at.z

        @pl.when(self.guard(piece, z == Z_SIZE - 1))
        def _():
            self.copy(z - distance, distance - 1, piece, True).wait_recv()

        @pl.when(self.guard(piece, z == 0))
        def _():
            self.copy(z + distance, distance - 1, piece, False).wait_recv()

    def drain(self, upward, last=None):
        z = self.at.z
        final = (Z_SIZE - 2, self.pieces - 1)
        for distance in range(Z_SIZE - 1):
            for piece in range(self.pieces):
                if last is not None and last != ((distance, piece) == final):
                    continue
                if upward:
                    plane, sent = z - distance, (z < Z_SIZE - 1) & (z >= distance)
                else:
                    plane, sent = z + distance, (z > 0) & (z + distance < Z_SIZE)

                @pl.when(self.guard(piece, sent))
                def _():
                    self.copy(plane, distance, piece, upward).wait_send()


class PlaneGather:
    def __init__(self, places, block_ref, send, recv):
        self.at, self.block_ref, self.send, self.recv = places, block_ref, send, recv

    def copy(self, slot):
        device, (dy, dx), part = (
            (self.at.x_id, (0, 0), None), (self.at.y_id, (0, 0), None),
            (self.at.x_id, (1, 0), 0), (self.at.y_id, (0, 1), 1),
            (self.at.core_id, (0, 0), None), (self.at.core_id, (0, 1), None),
            (self.at.core_id, (1, 0), None), (self.at.core_id, (1, 1), None),
        )[slot]
        ref = self.block_ref((self.at.y + dy) % 2, (self.at.x + dx) % 2, self.at.c, part)
        return remote(ref, ref, self.send.at[slot], self.recv.at[slot], device)

    def start(self, *slots):
        for slot in slots:
            self.copy(slot).start()

    def arrive(self, *slots):
        for slot in slots:
            (dy, dx, dc), part = (
                ((0, 1, 0), None), ((1, 0, 0), None), ((1, 1, 0), 0), ((1, 1, 0), 1),
                ((0, 0, 1), None), ((0, 1, 1), None), ((1, 0, 1), None), ((1, 1, 1), None),
            )[slot]
            ref = self.block_ref(
                (self.at.y + dy) % 2, (self.at.x + dx) % 2, (self.at.c + dc) % 2, part
            )
            remote(ref, ref, self.send.at[slot], self.recv.at[slot], self.at.core_id).wait_recv()

    def drain(self):
        for slot in range(8):
            self.copy(slot).wait_send()


def line_semaphores(pieces):
    return [pltpu.SemaphoreType.DMA(((Z_SIZE - 1) * pieces,)) for _ in range(4)]


def layer_kernel(
    tok_ref, wq_ref, wk_ref, wv_ref, wo_ref, gin_ref, gpost_ref, gq_ref, gk_ref, pos_ref, freq_ref,
    out_ref,
    xs, x_all, ws, w_all, acc, queries, kv, att_all, wo_own, wo_all, gin, gpost,
    cos_t, sin_t, q_off, k_off, result, got, turned_out,
    stage_sem, local_sem, w_send, w_recv, x_send, x_recv, halo_send, halo_recv, att_send, att_recv,
    o_send, o_recv, r_send, r_recv,
    *line_sems,
):
    at = Places()
    z, y, x, c = at.z, at.y, at.x, at.c
    same = c == y
    depth = wq_ref.shape[0]
    own_tokens, model = xs.shape
    plane_tokens = x_all.shape[0]
    head = HEAD_SIZE
    f32, bf16 = jnp.float32, jnp.bfloat16
    at.greet()

    loads = []
    for half in range(2):
        for ref, part, begin, width in (
            (wk_ref, 0, 0, head), (wv_ref, 0, head, head), (wq_ref, 1, 0, 2 * head)
        ):
            loads.append(pltpu.make_async_copy(
                ref.at[:, pl.ds(half * width, width)],
                ws.at[half, part, :, pl.ds(begin, width)],
                stage_sem.at[len(loads)],
            ))
    tok_load = pltpu.make_async_copy(tok_ref, xs, stage_sem.at[6])
    wo_load = pltpu.make_async_copy(wo_ref, wo_own, stage_sem.at[7])
    for copy in loads + [tok_load, wo_load]:
        copy.start()
    for copy in loads:
        copy.wait()
    at.meet()

    def block_rows(plane, row):
        return w_all.at[:, aligned((plane * 2 + row) * depth, depth)]

    def near_copy():
        return remote(ws.at[1 - c], block_rows(z, y), w_send.at[0], w_recv.at[0], at.core_id)

    def far_copy(target):
        block = block_rows(z, y) if target is not None else block_rows(z, 1 - y)
        device = at.y_id if target is None else target
        if target is at.diag_id:
            return remote(ws.at[1 - c], block, w_send.at[1], w_recv.at[1], device)
        return remote(ws.at[c], block, w_send.at[0], w_recv.at[1], device)

    own_block = pltpu.make_async_copy(ws.at[c], block_rows(z, y), local_sem.at[0])

    @pl.when(same)
    def _():
        near_copy().start()
        own_block.start()

    @pl.when(jnp.logical_not(same))
    def _():
        far_copy(at.y_id).start()
        far_copy(at.diag_id).start()


    def w_piece(plane, piece):
        row = (at.y + piece % 2) % 2
        return w_all.at[piece // 2, aligned((plane * 2 + row) * depth, depth)]

    def o_piece(plane, piece):
        return wo_all.at[plane, pl.ds(O_CUTS[piece], O_CUTS[piece + 1] - O_CUTS[piece])]

    w_line = Line(at, w_piece, W_PIECES, line_sems[:4])
    o_line = Line(
        at, o_piece, O_PIECES, line_sems[4:],
        lambda piece, condition: condition & (c == 1) if piece == O_PIECES - 1 else condition,
    )

    @pl.when(same)
    def _():
        own_block.wait()

    @pl.when(jnp.logical_not(same))
    def _():
        near_copy().wait_recv()

    w_line.send_own(0)
    w_line.send_own(2)

    def block_of(row, column, core):
        return (row * 4 + column * 2 + core) * own_tokens

    tok_load.wait()
    gin[...] = gin_ref[...].reshape(1, model)
    gpost[...] = gpost_ref[...].reshape(1, model)
    own_begin = block_of(y, x, c)

    @pl.loop(0, own_tokens // TILE)
    def _(step):
        v = xs[aligned(step * TILE, TILE), :].astype(f32)
        mean_square = jnp.mean(v * v, axis=-1, keepdims=True)
        x_all[aligned(own_begin + step * TILE, TILE), :] = (
            v * lax.rsqrt(mean_square + EPSILON) * gin[...]
        ).astype(bf16)

    cut = own_tokens * 3 // 4

    def x_block(row, column, core, part):
        begin, size = ((0, own_tokens), (0, cut), (cut, own_tokens - cut))[0 if part is None else part + 1]
        return x_all.at[aligned(block_of(row, column, core) + begin, size)]

    tokens = PlaneGather(at, x_block, x_send, x_recv)
    tokens.start(0, 4)

    o_rows = O_CUTS[-1]
    o_width = wo_own.shape[1]

    def o_copy(slot):
        dx, dc = ((0, 1), (1, 0), (1, 1))[slot]
        part = (x + dx) % 2 * 2 + (c + dc) % 2
        begin = part * (depth // TILE) // 4 * TILE
        return remote(
            wo_own.at[aligned(begin, o_rows)],
            wo_all.at[z, :, aligned((x * 2 + c) * o_width, o_width, 128)],
            o_send.at[slot], o_recv.at[slot], at.mate(0, dx, dc),
        )

    def o_arrive(slot):
        dx, dc = ((0, 1), (1, 0), (1, 1))[slot]
        part = (x + dx) % 2 * 2 + (c + dc) % 2
        block = wo_all.at[z, :, aligned(part * o_width, o_width, 128)]
        remote(block, block, o_send.at[slot], o_recv.at[slot], at.mate(0, dx, dc)).wait_recv()

    wo_load.wait()
    for slot in range(3):
        o_copy(slot).start()
    own_part = x * 2 + c
    keep_o = pltpu.make_async_copy(
        wo_own.at[aligned(own_part * (depth // TILE) // 4 * TILE, o_rows)],
        wo_all.at[z, :, aligned(own_part * o_width, o_width, 128)],
        local_sem.at[1],
    )
    keep_o.start()

    far_copy(None).wait_recv()
    w_line.send_own(1)
    w_line.send_own(3)
    tokens.start(1)
    middle = (z == 1) | (z == 2)

    first = pos_ref[0:1, 0:1]
    blocks = plane_tokens // head

    @pl.loop(0, blocks)
    def _(block):
        row = (pos_ref[pl.ds(z * blocks + block, 1), :] - first).astype(f32)
        column = jnp.broadcast_to(row, (head, head)).T
        here = aligned(block * head, head)
        q_off[here, :] = column
        angles = column * freq_ref[...]
        cos_t[here, :] = jnp.cos(angles)
        lane = lax.broadcasted_iota(jnp.int32, (head, head), 1)
        sine = jnp.sin(angles)
        sin_t[here, :] = jnp.where(lane < head // 2, -sine, sine)

    for block in range(2 * blocks):
        index = jnp.maximum((z - 1) * blocks + block, 0)
        row = (pos_ref[pl.ds(index, 1), :] - first).astype(f32)
        if block < blocks:
            row = jnp.where(z > 0, row, FAR_KEY)
        k_off[:, block * head:(block + 1) * head] = row

    @pl.when(z == 0)
    def _():
        kv[:, pl.ds(0, plane_tokens), :] = jnp.zeros((2, plane_tokens, head), bf16)

    for piece in range(2):
        w_line.forward(1, piece)

    tokens.arrive(0)
    tokens.start(3, 5)
    for piece in range(2):
        w_line.forward(2, piece)
    tokens.arrive(1)
    tokens.start(2, 6)
    for distance in (1, 2):
        for piece in range(2, W_PIECES):
            w_line.forward(distance, piece)
    keep_o.wait()
    for slot in range(3):
        o_arrive(slot)

    @pl.when(jnp.logical_not(middle))
    def _():
        for piece in range(O_PIECES):
            o_line.send_own(piece)

    tokens.arrive(2, 3)
    tokens.start(7)
    tokens.arrive(4, 5, 6, 7)

    pair_depth = 4 * depth
    row_step = plane_tokens // 2

    def multiply(part, pair, add):
        @pl.loop(0, plane_tokens // row_step)
        def _(step):
            rows = aligned(step * row_step, row_step)
            product = jnp.dot(
                x_all[rows, aligned(pair * pair_depth, pair_depth, 128)],
                w_all[part, aligned(pair * pair_depth, pair_depth), :],
                preferred_element_type=f32,
            )
            columns = slice(part * 2 * head, (part + 1) * 2 * head)
            acc[rows, columns] = acc[rows, columns] + product if add else product

    def turned(v, gain, cosine, sine):
        mean_square = jnp.mean(v * v, axis=-1, keepdims=True)
        v = v * lax.rsqrt(mean_square + EPSILON) * gain
        return (v * cosine + pltpu.roll(v, head // 2, 1) * sine).astype(bf16)

    for distance in range(1, Z_SIZE):
        for piece in range(2):
            w_line.arrive(distance, piece)
    multiply(0, z // 2, False)
    multiply(0, 1 - z // 2, True)

    @pl.loop(0, blocks)
    def _(block):
        here = aligned(block * head, head)
        own = aligned(plane_tokens + block * head, head)
        kv[0, own, :] = turned(acc[here, 0:head], gk_ref[...], cos_t[here, :], sin_t[here, :])
        kv[1, own, :] = acc[here, head:2 * head].astype(bf16)

    q_step = 2 * own_tokens
    q_blocks = plane_tokens // q_step
    span = LOOKBACK_WINDOW + q_step

    def halo(block):
        return remote(
            kv.at[:, pl.ds(plane_tokens + block * q_step, q_step)],
            kv.at[:, pl.ds(block * q_step, q_step)],
            halo_send.at[block], halo_recv.at[block], at.up_id,
        )

    @pl.when(z < Z_SIZE - 1)
    def _():
        for block in reversed(range(q_blocks)):
            halo(block).start()

    def pass_o(upward):
        w_line.drain(upward, False)
        for piece in range(O_PIECES):
            o_line.send_own(piece, upward, not upward)

    @pl.when(z == 1)
    def _():
        pass_o(True)

    @pl.when(z == 2)
    def _():
        pass_o(False)

    for piece in range(2, W_PIECES):
        w_line.arrive(1, piece)
    multiply(1, z // 2, False)
    for distance in range(2, Z_SIZE):
        for piece in range(2, W_PIECES):
            w_line.arrive(distance, piece)
    multiply(1, 1 - z // 2, True)

    @pl.loop(0, blocks)
    def _(block):
        here = aligned(block * head, head)
        for h in range(2):
            raw = acc[here, (h + 2) * head:(h + 3) * head]
            queries[here, h * head:(h + 1) * head] = turned(
                raw, gq_ref[...], cos_t[here, :], sin_t[here, :]
            )

    width = 2 * head

    def att_block(block):
        def ref(row, column, core, part):
            half = q_step // 2
            begin, size = ((0, q_step), (0, half), (half, half))[0 if part is None else part + 1]
            return att_all.at[
                pl.ds(block * q_step + begin, size),
                aligned((column * 4 + row * 2 + core) * width, width, 128),
            ]

        return ref

    attended = [
        PlaneGather(at, att_block(block), att_send.at[block], att_recv.at[block])
        for block in range(q_blocks)
    ]
    own_heads = (x * 4 + y * 2 + c) * width

    def attend_block(block):
        rows, keys = pl.ds(block * q_step, q_step), pl.ds(block * q_step, span)
        gap = q_off[rows, 0:1] - k_off[:, keys]
        allowed = (gap >= 0) & (gap < LOOKBACK_WINDOW)
        k_rows, v_rows = kv[0, keys, :], kv[1, keys, :]
        for h in range(2):
            scores = lax.dot_general(
                queries[rows, h * head:(h + 1) * head], k_rows, (((1,), (1,)), ((), ())),
                preferred_element_type=f32,
            ) * QS ** (-0.5)
            scores = jnp.where(allowed, scores, -1e30)
            weights = jnp.exp(scores - jnp.max(scores, axis=-1, keepdims=True))
            totals = jnp.sum(weights, axis=-1, keepdims=True)
            mixed = jnp.dot(weights.astype(bf16), v_rows, preferred_element_type=f32) / totals
            att_all[rows, aligned(own_heads + h * head, head, 128)] = mixed.astype(bf16)

    def hand_on(block):
        attended[block].arrive(0)
        attended[block].start(3, 5)
        attended[block].arrive(1)
        attended[block].start(2, 6)

    def hand_across(block):
        attended[block].arrive(2, 3)
        attended[block].start(7)

    @pl.when(z == 1)
    def _():
        pass_o(False)

    for block in reversed(range(q_blocks)):
        @pl.when(z > 0)
        def _():
            halo(block).wait_recv()

        attend_block(block)
        attended[block].start(0, 1, 4)
        if block + 1 < q_blocks:
            hand_on(block + 1)
        if block + 2 < q_blocks:
            hand_across(block + 2)

    @pl.when(z == 2)
    def _():
        pass_o(True)

    @pl.when(middle)
    def _():
        for distance in (1, 2):
            for piece in range(O_PIECES):
                o_line.forward(distance, piece)

    @pl.when(jnp.logical_not(middle))
    def _():
        w_line.drain(True, False)
        w_line.drain(False, False)

    hand_on(0)
    hand_across(1)
    hand_across(0)
    for gather in attended:
        gather.arrive(4, 5, 6, 7)

    planes = [z, z + 1 - 2 * (z % 2), (z + 2) % 4, 3 - z]
    own_index = y * 4 + x * 2 + c

    def part_rows(part):
        return ((0, o_rows), (0, O_CUTS[1]), (O_CUTS[1], o_rows))[part]

    def r_refs(step, part, mate):
        dy, dx, dc = MATES[mate]
        owner = (y + dy) % 2 * 4 + (x + dx) % 2 * 2 + (c + dc) % 2
        begin, end = part_rows(part)
        rows = pl.ds(begin, end - begin)
        slot = (step + part // 2) * len(MATES) + mate
        return owner, rows, r_send.at[slot], r_recv.at[slot]

    def r_copy(step, part, mate):
        owner, rows, send, recv = r_refs(step, part, mate)
        return remote(
            result.at[step, owner, rows], got.at[step, own_index, rows], send, recv,
            at.mate(*MATES[mate]),
        )

    def r_arrive(step, part, mate):
        owner, rows, send, recv = r_refs(step, part, mate)
        block = got.at[step, owner, rows]
        remote(block, block, send, recv, at.core_id).wait_recv()

    def project(step, part=0):
        begin, end = part_rows(part)
        sums = lax.dot_general(
            wo_all[planes[step], begin:end], att_all[...], (((1,), (1,)), ((), ())),
            preferred_element_type=f32,
        ).astype(bf16)
        for owner in range(8):
            result[step, owner, begin:end] = sums[:, owner * own_tokens:(owner + 1) * own_tokens]
        for mate in range(len(MATES)):
            r_copy(step, part, mate).start()
        got[step, own_index, begin:end] = result[step, own_index, begin:end]

    def finish(step, square, part=0):
        for mate in range(len(MATES)):
            r_arrive(step, part, mate)
        for owner in range(8):
            row, quarter = owner // 4, owner % 4
            start = quarter * (depth // TILE) // 4 * TILE
            size = (quarter + 1) * (depth // TILE) // 4 * TILE - start
            begin, end = part_rows(part)
            end = min(end, size)
            v = got[step, owner, begin:end].astype(f32)
            there = (planes[step] * 2 + row) * depth + start + begin
            turned_out[aligned(there, end - begin), :] = v
            square = square + jnp.sum(v * v, axis=0, keepdims=True)
        return square

    square = jnp.zeros((1, own_tokens), f32)
    last = Z_SIZE - 1
    for step in range(last):
        if step > 0:
            for piece in range(O_PIECES):
                o_line.arrive(step, piece)
        project(step)
        if step > 0:
            square = finish(step - 1, square)
    o_line.arrive(last, 0)
    project(last, 1)
    square = finish(last - 1, square)
    for piece in range(1, O_PIECES):
        o_line.arrive(last, piece)
    project(last, 2)
    square = finish(last, square, 1)
    square = finish(last, square, 2)

    scale = lax.rsqrt(square / model + EPSILON)
    for begin in range(0, model, head):
        columns = slice(begin, begin + head)
        normed = (turned_out[columns, :] * scale).T * gpost[:, columns]
        out_ref[:, columns] = (xs[:, columns].astype(f32) + normed).astype(bf16)

    @pl.when(same)
    def _():
        near_copy().wait_send()

    @pl.when(jnp.logical_not(same))
    def _():
        far_copy(at.y_id).wait_send()
        far_copy(at.diag_id).wait_send()

    tokens.drain()
    for gather in attended:
        gather.drain()
    for slot in range(3):
        o_copy(slot).wait_send()

    @pl.when(z < Z_SIZE - 1)
    def _():
        for block in range(q_blocks):
            halo(block).wait_send()

    w_line.drain(True, True)
    w_line.drain(False, True)
    o_line.drain(True)
    o_line.drain(False)
    for step, part in [(step, 0) for step in range(last)] + [(last, 1), (last, 2)]:
        for mate in range(len(MATES)):
            r_copy(step, part, mate).wait_send()


def layer(tokens, positions, w_query, key_matrix, value_matrix, w_out_t, gain_in, gain_query, gain_key, gain_post):
    own_tokens, model = tokens.shape
    depth = w_query.shape[0]
    columns, heads = w_out_t.shape
    head = HEAD_SIZE
    plane = 8 * own_tokens
    bf16, f32, dma = jnp.bfloat16, jnp.float32, pltpu.SemaphoreType.DMA
    frequency = jnp.asarray(ROPE_BASE ** (-2.0 * (np.arange(head) % (head // 2)) / head), f32)
    vmem, anywhere = pl.BlockSpec(memory_space=pltpu.VMEM), pl.BlockSpec(memory_space=pl.ANY)
    o_rows = O_CUTS[-1]
    return pl.pallas_call(
        layer_kernel,
        out_shape=jax.ShapeDtypeStruct((own_tokens, model), bf16),
        in_specs=[anywhere] * 5 + [vmem] * 6,
        out_specs=vmem,
        scratch_shapes=[
            pltpu.VMEM((own_tokens, model), bf16),
            pltpu.VMEM((plane, model), bf16),
            pltpu.VMEM((2, 2, depth, 2 * head), bf16),
            pltpu.VMEM((2, model, 2 * head), bf16),
            pltpu.VMEM((plane, 4 * head), f32),
            pltpu.VMEM((plane, 2 * head), bf16),
            pltpu.VMEM((2, 2 * plane, head), bf16),
            pltpu.VMEM((plane, 4 * heads), bf16),
            pltpu.VMEM((columns, heads), bf16),
            pltpu.VMEM((Z_SIZE, o_rows, 4 * heads), bf16),
            pltpu.VMEM((1, model), f32),
            pltpu.VMEM((1, model), f32),
            pltpu.VMEM((plane, head), f32),
            pltpu.VMEM((plane, head), f32),
            pltpu.VMEM((plane, head), f32),
            pltpu.VMEM((1, 2 * plane), f32),
            pltpu.VMEM((Z_SIZE, 8, o_rows, own_tokens), bf16),
            pltpu.VMEM((Z_SIZE, 8, o_rows, own_tokens), bf16),
            pltpu.VMEM((model, own_tokens), f32),
            dma((8,)), dma((2,)), dma((2,)), dma((2,)), dma((8,)), dma((8,)), dma((4,)), dma((4,)), dma((4, 8)), dma((4, 8)),
            dma((3,)), dma((3,)), dma((7 * Z_SIZE + 7,)), dma((7 * Z_SIZE + 7,)),
            *line_semaphores(W_PIECES), *line_semaphores(O_PIECES),
        ],
        compiler_params=pltpu.CompilerParams(
            collective_id=0, has_side_effects=True, vmem_limit_bytes=60 * 2**20
        ),
        name="layer",
    )(
        tokens, w_query, key_matrix, value_matrix, w_out_t,
        gain_in, gain_post,
        gain_query.reshape(1, -1), gain_key.reshape(1, -1),
        positions.reshape(-1, head), frequency.reshape(1, -1),
    )


def attend(query_matrix, projected_keys, projected_values, query_offsets, key_offsets, key_valid):
    scores = jnp.einsum(
        "qkgd,skd->kgqs", query_matrix, projected_keys, preferred_element_type=jnp.float32
    ) * QS ** (-0.5)
    position_gap = query_offsets[:, None] - key_offsets[None, :]
    allowed = key_valid[None, :] & (position_gap >= 0) & (position_gap < LOOKBACK_WINDOW)
    scores = jnp.where(allowed[None, None], scores, -1e30)
    row_max = jnp.max(scores, axis=-1, keepdims=True)
    weights = jnp.where(allowed[None, None], jnp.exp(scores - row_max), 0.0)
    totals = jnp.sum(weights, axis=-1, keepdims=True)
    rounded = weights.astype(jnp.bfloat16)
    mixed = jnp.einsum(
        "kgqs,skd->qkgd", rounded, projected_values, preferred_element_type=jnp.float32
    )
    mixed = mixed / jnp.transpose(totals, (2, 0, 1, 3))
    return mixed.astype(jnp.bfloat16).reshape(query_matrix.shape[0], -1)


def shards(
    tokens,
    positions,
    w_query,
    key_matrix,
    value_matrix,
    w_out,
    gain_in,
    gain_query,
    gain_key,
    gain_post,
):
    if lax.axis_size("ctx") == 2 * Z_SIZE and lax.axis_size("tp") == 4:
        return layer(
            tokens, positions, w_query, key_matrix, value_matrix, w_out.T,
            gain_in, gain_query, gain_key, gain_post,
        )
    normed = row_norm(tokens.astype(jnp.float32), gain_in).astype(jnp.bfloat16)
    normalized_rows = lax.all_gather(normed, "tp", axis=0, tiled=True)
    weights_in = lax.all_gather(
        jnp.concatenate([w_query, key_matrix, value_matrix], axis=1), "ctx", axis=0, tiled=True
    )
    row_count = normalized_rows.shape[0]
    block_start = lax.axis_index("ctx") * row_count
    offsets_all = positions - positions[0]
    query_offsets = lax.dynamic_slice_in_dim(offsets_all, block_start, row_count, 0)
    query_width, key_width = w_query.shape[1], key_matrix.shape[1]

    def add_rows(weights):
        return jnp.dot(normalized_rows, weights, preferred_element_type=jnp.float32)

    key_value_raw = add_rows(weights_in[:, query_width:])
    query_raw = add_rows(weights_in[:, :query_width])
    unnormed_keys = key_value_raw[:, :key_width]
    value_raw = key_value_raw[:, key_width:]
    key_heads = key_matrix.shape[1] // HEAD_SIZE
    projected_keys = rotate(
        row_norm(unnormed_keys.reshape(row_count, key_heads, HEAD_SIZE), gain_key), query_offsets
    ).astype(jnp.bfloat16)
    projected_values = value_raw.astype(jnp.bfloat16).reshape(row_count, key_heads, HEAD_SIZE)
    own_pair = jnp.stack([projected_keys, projected_values])
    window_blocks = LOOKBACK_WINDOW // row_count
    earlier = [shifted(own_pair, "ctx", steps) for steps in range(window_blocks, 0, -1)]
    window_pair = jnp.concatenate(earlier + [own_pair], axis=1)
    query_heads = w_query.shape[1] // HEAD_SIZE
    query_matrix = rotate(
        row_norm(query_raw.reshape(row_count, query_heads, HEAD_SIZE), gain_query), query_offsets
    ).astype(jnp.bfloat16)
    query_matrix = query_matrix.reshape(row_count, key_heads, query_heads // key_heads, HEAD_SIZE)
    padded_offsets = jnp.concatenate(
        [jnp.zeros((LOOKBACK_WINDOW,), jnp.int32), offsets_all], axis=0
    )
    key_offsets = lax.dynamic_slice_in_dim(
        padded_offsets, block_start, LOOKBACK_WINDOW + row_count, 0
    )
    key_valid = (
        block_start + jnp.arange(LOOKBACK_WINDOW + row_count, dtype=jnp.int32) >= LOOKBACK_WINDOW
    )
    attended = attend(
        query_matrix, window_pair[0], window_pair[1], query_offsets, key_offsets, key_valid
    )
    projected = jnp.dot(
        attended,
        lax.all_gather(w_out, "ctx", axis=1, tiled=True),
        preferred_element_type=jnp.float32,
    )
    summed = lax.psum_scatter(
        projected.astype(jnp.bfloat16), "tp", scatter_dimension=0, tiled=True
    ).astype(jnp.float32)
    return (tokens.astype(jnp.float32) + row_norm(summed, gain_post)).astype(jnp.bfloat16)


def solution(mesh):
    in_specs = (
        P(("ctx", "tp"), None),
        P(),
        P("ctx", "tp"),
        P("ctx", "tp"),
        P("ctx", "tp"),
        P("tp", "ctx"),
        P(),
        P(),
        P(),
        P(),
    )
    out_specs = P(("ctx", "tp"), None)
    return jax.shard_map(shards, mesh=mesh, in_specs=in_specs, out_specs=out_specs, check_vma=False)
```

```python
import jax
import jax.numpy as jnp
import numpy as np
from jax import lax
from jax.experimental import pallas as pl
from jax.experimental.pallas import tpu as pltpu
from jax.sharding import PartitionSpec as P

HEAD_SIZE = 128
QS = 168
LOOKBACK_WINDOW = 1024


EPSILON = 1e-06
ROPE_BASE = 10000.0


def shifted(value, axis, steps):
    count = lax.axis_size(axis)
    leading, last = (max(0, -steps), min(count, count - steps))
    return lax.ppermute(value, axis, [(source, source + steps) for source in range(leading, last)])


def row_norm(values, scales):
    mean_square = jnp.mean(values * values, axis=-1, keepdims=True)
    return values * lax.rsqrt(mean_square + EPSILON) * scales


def rotate(head_rows, offsets):
    half_dim = head_rows.shape[-1] // 2
    frequency = ROPE_BASE ** (
        -(jnp.arange(half_dim, dtype=jnp.float32) * 2.0) / head_rows.shape[-1]
    )
    angles = offsets.astype(jnp.float32)[:, None] * frequency[None, :]
    cosine = jnp.cos(angles)[:, None, :]
    sine_wave = jnp.sin(angles)[:, None, :]
    first_half = head_rows[..., :half_dim]
    second_half = head_rows[..., half_dim:]
    return jnp.concatenate(
        [
            first_half * cosine - second_half * sine_wave,
            second_half * cosine + first_half * sine_wave,
        ],
        axis=-1,
    )


Z_SIZE = 4
TILE = 16
W_PIECES = 4
O_PIECES = 3
O_CUTS = (0, 112, 160, 176)
MATES = [(i // 4, i // 2 % 2, i % 2) for i in range(1, 8)]
MESH = pl.DeviceIdType.MESH
FAR_KEY = 1e9


def remote(source, target, send, recv, device):
    return pltpu.make_async_remote_copy(
        src_ref=source, dst_ref=target, send_sem=send, recv_sem=recv,
        device_id=device, device_id_type=MESH,
    )


def aligned(value, size, step=TILE):
    return pl.ds(pl.multiple_of(value, step), size)


class Places:
    def __init__(self):
        self.ctx = lax.axis_index("ctx")
        self.tp = lax.axis_index("tp")
        self.z, self.y = self.ctx // 2, self.ctx % 2
        self.x, self.c = self.tp // 2, self.tp % 2
        self.core_id = self.mate(0, 0, 1)
        self.x_id = self.mate(0, 1, 0)
        self.y_id = self.mate(1, 0, 0)
        self.diag_id = self.mate(1, 0, 1)
        self.up_id = (self.ctx + 2, self.tp)
        self.down_id = (self.ctx - 2, self.tp)

    def mate(self, dy, dx, dc):
        row, column, core = ((v + d) % 2 for v, d in ((self.y, dy), (self.x, dx), (self.c, dc)))
        return (self.z * 2 + row, column * 2 + core)

    def greet(self):
        barrier = pltpu.get_barrier_semaphore()

        def signal(target):
            pl.semaphore_signal(barrier, inc=1, device_id=target, device_id_type=MESH)

        for dy, dx, dc in MATES:
            signal(self.mate(dy, dx, dc))

        @pl.when(self.z < Z_SIZE - 1)
        def _():
            signal(self.up_id)

        @pl.when(self.z > 0)
        def _():
            signal(self.down_id)

    def meet(self):
        middle = ((self.z + 1) // 2) % 2
        pl.semaphore_wait(pltpu.get_barrier_semaphore(), 8 + middle)


class Line:
    def __init__(self, places, piece_ref, pieces, sems, guard=None):
        self.at, self.piece_ref, self.pieces = places, piece_ref, pieces
        self.guard = guard or (lambda piece, condition: condition)
        self.up_send, self.down_send, self.below, self.above = sems

    def copy(self, plane, distance, piece, upward):
        ref = self.piece_ref(plane, piece)
        slot = distance * self.pieces + piece
        if upward:
            return remote(ref, ref, self.up_send.at[slot], self.below.at[slot], self.at.up_id)
        return remote(ref, ref, self.down_send.at[slot], self.above.at[slot], self.at.down_id)

    def send_own(self, piece, upward=True, downward=True):
        z = self.at.z
        if upward:
            @pl.when(self.guard(piece, z < Z_SIZE - 1))
            def _():
                self.copy(z, 0, piece, True).start()

        if downward:
            @pl.when(self.guard(piece, z > 0))
            def _():
                self.copy(z, 0, piece, False).start()

    def forward(self, distance, piece):
        z = self.at.z
        if distance == Z_SIZE - 1:
            return

        @pl.when(self.guard(piece, (z >= distance) & (z < Z_SIZE - 1)))
        def _():
            self.copy(z - distance, distance - 1, piece, True).wait_recv()
            self.copy(z - distance, distance, piece, True).start()

        @pl.when(self.guard(piece, (z + distance < Z_SIZE) & (z > 0)))
        def _():
            self.copy(z + distance, distance - 1, piece, False).wait_recv()
            self.copy(z + distance, distance, piece, False).start()

    def arrive(self, distance, piece):
        z = self.at.z

        @pl.when(self.guard(piece, z == Z_SIZE - 1))
        def _():
            self.copy(z - distance, distance - 1, piece, True).wait_recv()

        @pl.when(self.guard(piece, z == 0))
        def _():
            self.copy(z + distance, distance - 1, piece, False).wait_recv()

    def drain(self, upward, last=None):
        z = self.at.z
        final = (Z_SIZE - 2, self.pieces - 1)
        for distance in range(Z_SIZE - 1):
            for piece in range(self.pieces):
                if last is not None and last != ((distance, piece) == final):
                    continue
                if upward:
                    plane, sent = z - distance, (z < Z_SIZE - 1) & (z >= distance)
                else:
                    plane, sent = z + distance, (z > 0) & (z + distance < Z_SIZE)

                @pl.when(self.guard(piece, sent))
                def _():
                    self.copy(plane, distance, piece, upward).wait_send()


class PlaneGather:
    def __init__(self, places, block_ref, send, recv):
        self.at, self.block_ref, self.send, self.recv = places, block_ref, send, recv

    def copy(self, slot):
        device, (dy, dx), part = (
            (self.at.x_id, (0, 0), None), (self.at.y_id, (0, 0), None),
            (self.at.x_id, (1, 0), 0), (self.at.y_id, (0, 1), 1),
            (self.at.core_id, (0, 0), None), (self.at.core_id, (0, 1), None),
            (self.at.core_id, (1, 0), None), (self.at.core_id, (1, 1), None),
        )[slot]
        ref = self.block_ref((self.at.y + dy) % 2, (self.at.x + dx) % 2, self.at.c, part)
        return remote(ref, ref, self.send.at[slot], self.recv.at[slot], device)

    def start(self, *slots):
        for slot in slots:
            self.copy(slot).start()

    def arrive(self, *slots):
        for slot in slots:
            (dy, dx, dc), part = (
                ((0, 1, 0), None), ((1, 0, 0), None), ((1, 1, 0), 0), ((1, 1, 0), 1),
                ((0, 0, 1), None), ((0, 1, 1), None), ((1, 0, 1), None), ((1, 1, 1), None),
            )[slot]
            ref = self.block_ref(
                (self.at.y + dy) % 2, (self.at.x + dx) % 2, (self.at.c + dc) % 2, part
            )
            remote(ref, ref, self.send.at[slot], self.recv.at[slot], self.at.core_id).wait_recv()

    def drain(self):
        for slot in range(8):
            self.copy(slot).wait_send()


def line_semaphores(pieces):
    return [pltpu.SemaphoreType.DMA(((Z_SIZE - 1) * pieces,)) for _ in range(4)]


def layer_kernel(
    tok_ref, wq_ref, wk_ref, wv_ref, wo_ref, gin_ref, gpost_ref, gq_ref, gk_ref, pos_ref, freq_ref,
    out_ref,
    xs, x_all, ws, w_all, acc, queries, kv, att_all, wo_own, wo_all, gin, gpost,
    cos_t, sin_t, q_off, k_off, result, got, turned_out,
    stage_sem, local_sem, w_send, w_recv, x_send, x_recv, halo_send, halo_recv, att_send, att_recv,
    o_send, o_recv, r_send, r_recv,
    *line_sems,
):
    at = Places()
    z, y, x, c = at.z, at.y, at.x, at.c
    same = c == y
    depth = wq_ref.shape[0]
    own_tokens, model = xs.shape
    plane_tokens = x_all.shape[0]
    head = HEAD_SIZE
    f32, bf16 = jnp.float32, jnp.bfloat16
    at.greet()

    loads = []
    for half in range(2):
        for ref, part, begin, width in (
            (wk_ref, 0, 0, head), (wv_ref, 0, head, head), (wq_ref, 1, 0, 2 * head)
        ):
            loads.append(pltpu.make_async_copy(
                ref.at[:, pl.ds(half * width, width)],
                ws.at[half, part, :, pl.ds(begin, width)],
                stage_sem.at[len(loads)],
            ))
    tok_load = pltpu.make_async_copy(tok_ref, xs, stage_sem.at[6])
    wo_load = pltpu.make_async_copy(wo_ref, wo_own, stage_sem.at[7])
    for copy in loads + [tok_load, wo_load]:
        copy.start()
    at.meet()
    for copy in loads:
        copy.wait()

    def block_rows(part, plane, row):
        return w_all.at[part, aligned((plane * 2 + row) * depth, depth)]

    def near_copy(part):
        return remote(
            ws.at[1 - c, part], block_rows(part, z, y), w_send.at[part], w_recv.at[part], at.core_id
        )

    def far_copy(part, half, slot, device):
        return remote(
            ws.at[half, part], block_rows(part, z, y),
            w_send.at[2 * slot + part], w_recv.at[2 + part], device,
        )

    def far_arrive(part):
        block = block_rows(part, z, 1 - y)
        remote(block, block, w_send.at[part], w_recv.at[2 + part], at.y_id).wait_recv()

    def own_block(part):
        return pltpu.make_async_copy(
            ws.at[c, part], block_rows(part, z, y), local_sem.at[(0, 2)[part]]
        )

    for part in range(2):
        @pl.when(same)
        def _():
            near_copy(part).start()
            own_block(part).start()

        @pl.when(jnp.logical_not(same))
        def _():
            far_copy(part, c, 0, at.y_id).start()
            far_copy(part, 1 - c, 1, at.diag_id).start()

    def w_piece(plane, piece):
        row = (at.y + piece % 2) % 2
        return w_all.at[piece // 2, aligned((plane * 2 + row) * depth, depth)]

    def o_piece(plane, piece):
        return wo_all.at[plane, pl.ds(O_CUTS[piece], O_CUTS[piece + 1] - O_CUTS[piece])]

    w_line = Line(at, w_piece, W_PIECES, line_sems[:4])
    o_line = Line(
        at, o_piece, O_PIECES, line_sems[4:],
        lambda piece, condition: condition & (c == 1) if piece == O_PIECES - 1 else condition,
    )

    for part in range(2):
        @pl.when(same)
        def _():
            own_block(part).wait()

        @pl.when(jnp.logical_not(same))
        def _():
            near_copy(part).wait_recv()

        w_line.send_own(2 * part)

    def block_of(row, column, core):
        return (row * 4 + column * 2 + core) * own_tokens

    tok_load.wait()
    gin[...] = gin_ref[...].reshape(1, model)
    gpost[...] = gpost_ref[...].reshape(1, model)
    own_begin = block_of(y, x, c)

    @pl.loop(0, own_tokens // TILE)
    def _(step):
        v = xs[aligned(step * TILE, TILE), :].astype(f32)
        mean_square = jnp.mean(v * v, axis=-1, keepdims=True)
        x_all[aligned(own_begin + step * TILE, TILE), :] = (
            v * lax.rsqrt(mean_square + EPSILON) * gin[...]
        ).astype(bf16)

    cut = own_tokens * 3 // 4

    def x_block(row, column, core, part):
        begin, size = ((0, own_tokens), (0, cut), (cut, own_tokens - cut))[0 if part is None else part + 1]
        return x_all.at[aligned(block_of(row, column, core) + begin, size)]

    tokens = PlaneGather(at, x_block, x_send, x_recv)
    tokens.start(0, 4)

    o_rows = O_CUTS[-1]
    o_width = wo_own.shape[1]

    def o_copy(slot):
        dx, dc = ((0, 1), (1, 0), (1, 1))[slot]
        part = (x + dx) % 2 * 2 + (c + dc) % 2
        begin = part * (depth // TILE) // 4 * TILE
        return remote(
            wo_own.at[aligned(begin, o_rows)],
            wo_all.at[z, :, aligned((x * 2 + c) * o_width, o_width, 128)],
            o_send.at[slot], o_recv.at[slot], at.mate(0, dx, dc),
        )

    def o_arrive(slot):
        dx, dc = ((0, 1), (1, 0), (1, 1))[slot]
        part = (x + dx) % 2 * 2 + (c + dc) % 2
        block = wo_all.at[z, :, aligned(part * o_width, o_width, 128)]
        remote(block, block, o_send.at[slot], o_recv.at[slot], at.mate(0, dx, dc)).wait_recv()

    wo_load.wait()
    for slot in range(3):
        o_copy(slot).start()
    own_part = x * 2 + c
    keep_o = pltpu.make_async_copy(
        wo_own.at[aligned(own_part * (depth // TILE) // 4 * TILE, o_rows)],
        wo_all.at[z, :, aligned(own_part * o_width, o_width, 128)],
        local_sem.at[1],
    )
    keep_o.start()

    for part in range(2):
        far_arrive(part)
        w_line.send_own(2 * part + 1)
    tokens.start(1)
    middle = (z == 1) | (z == 2)

    first = pos_ref[0:1, 0:1]
    blocks = plane_tokens // head

    @pl.loop(0, blocks)
    def _(block):
        row = (pos_ref[pl.ds(z * blocks + block, 1), :] - first).astype(f32)
        column = jnp.broadcast_to(row, (head, head)).T
        here = aligned(block * head, head)
        q_off[here, :] = column
        angles = column * freq_ref[...]
        cos_t[here, :] = jnp.cos(angles)
        lane = lax.broadcasted_iota(jnp.int32, (head, head), 1)
        sine = jnp.sin(angles)
        sin_t[here, :] = jnp.where(lane < head // 2, -sine, sine)

    for block in range(2 * blocks):
        index = jnp.maximum((z - 1) * blocks + block, 0)
        row = (pos_ref[pl.ds(index, 1), :] - first).astype(f32)
        if block < blocks:
            row = jnp.where(z > 0, row, FAR_KEY)
        k_off[:, block * head:(block + 1) * head] = row

    @pl.when(z == 0)
    def _():
        kv[:, pl.ds(0, plane_tokens), :] = jnp.zeros((2, plane_tokens, head), bf16)

    for piece in range(2):
        w_line.forward(1, piece)

    tokens.arrive(0)
    tokens.start(3, 5)
    for piece in range(2):
        w_line.forward(2, piece)
    tokens.arrive(1)
    tokens.start(2, 6)
    for distance in (1, 2):
        for piece in range(2, W_PIECES):
            w_line.forward(distance, piece)
    keep_o.wait()
    for slot in range(3):
        o_arrive(slot)

    @pl.when(jnp.logical_not(middle))
    def _():
        for piece in range(O_PIECES):
            o_line.send_own(piece)

    tokens.arrive(2, 3)
    tokens.start(7)
    tokens.arrive(4, 5, 6, 7)

    pair_depth = 4 * depth
    row_step = plane_tokens // 2

    def multiply(part, pair, add):
        @pl.loop(0, plane_tokens // row_step)
        def _(step):
            rows = aligned(step * row_step, row_step)
            product = jnp.dot(
                x_all[rows, aligned(pair * pair_depth, pair_depth, 128)],
                w_all[part, aligned(pair * pair_depth, pair_depth), :],
                preferred_element_type=f32,
            )
            columns = slice(part * 2 * head, (part + 1) * 2 * head)
            acc[rows, columns] = acc[rows, columns] + product if add else product

    def turned(v, gain, cosine, sine):
        mean_square = jnp.mean(v * v, axis=-1, keepdims=True)
        v = v * lax.rsqrt(mean_square + EPSILON) * gain
        return (v * cosine + pltpu.roll(v, head // 2, 1) * sine).astype(bf16)

    for distance in range(1, Z_SIZE):
        for piece in range(2):
            w_line.arrive(distance, piece)
    multiply(0, z // 2, False)
    multiply(0, 1 - z // 2, True)

    @pl.loop(0, blocks)
    def _(block):
        here = aligned(block * head, head)
        own = aligned(plane_tokens + block * head, head)
        kv[0, own, :] = turned(acc[here, 0:head], gk_ref[...], cos_t[here, :], sin_t[here, :])
        kv[1, own, :] = acc[here, head:2 * head].astype(bf16)

    q_step = 2 * own_tokens
    q_blocks = plane_tokens // q_step
    span = LOOKBACK_WINDOW + q_step

    def halo(block):
        return remote(
            kv.at[:, pl.ds(plane_tokens + block * q_step, q_step)],
            kv.at[:, pl.ds(block * q_step, q_step)],
            halo_send.at[block], halo_recv.at[block], at.up_id,
        )

    @pl.when(z < Z_SIZE - 1)
    def _():
        for block in reversed(range(q_blocks)):
            halo(block).start()

    def pass_o(upward):
        w_line.drain(upward, False)
        for piece in range(O_PIECES):
            o_line.send_own(piece, upward, not upward)

    @pl.when(z == 1)
    def _():
        pass_o(True)

    @pl.when(z == 2)
    def _():
        pass_o(False)

    for piece in range(2, W_PIECES):
        w_line.arrive(1, piece)
    multiply(1, z // 2, False)
    for distance in range(2, Z_SIZE):
        for piece in range(2, W_PIECES):
            w_line.arrive(distance, piece)
    multiply(1, 1 - z // 2, True)

    @pl.loop(0, blocks)
    def _(block):
        here = aligned(block * head, head)
        for h in range(2):
            raw = acc[here, (h + 2) * head:(h + 3) * head]
            queries[here, h * head:(h + 1) * head] = turned(
                raw, gq_ref[...], cos_t[here, :], sin_t[here, :]
            )

    width = 2 * head

    def att_block(block):
        def ref(row, column, core, part):
            half = q_step // 2
            begin, size = ((0, q_step), (0, half), (half, half))[0 if part is None else part + 1]
            return att_all.at[
                pl.ds(block * q_step + begin, size),
                aligned((column * 4 + row * 2 + core) * width, width, 128),
            ]

        return ref

    attended = [
        PlaneGather(at, att_block(block), att_send.at[block], att_recv.at[block])
        for block in range(q_blocks)
    ]
    own_heads = (x * 4 + y * 2 + c) * width

    def attend_block(block):
        rows, keys = pl.ds(block * q_step, q_step), pl.ds(block * q_step, span)
        gap = q_off[rows, 0:1] - k_off[:, keys]
        allowed = (gap >= 0) & (gap < LOOKBACK_WINDOW)
        k_rows, v_rows = kv[0, keys, :], kv[1, keys, :]
        for h in range(2):
            scores = lax.dot_general(
                queries[rows, h * head:(h + 1) * head], k_rows, (((1,), (1,)), ((), ())),
                preferred_element_type=f32,
            ) * QS ** (-0.5)
            scores = jnp.where(allowed, scores, -1e30)
            weights = jnp.exp(scores - jnp.max(scores, axis=-1, keepdims=True))
            totals = jnp.sum(weights, axis=-1, keepdims=True)
            mixed = jnp.dot(weights.astype(bf16), v_rows, preferred_element_type=f32) / totals
            att_all[rows, aligned(own_heads + h * head, head, 128)] = mixed.astype(bf16)

    def hand_on(block):
        attended[block].arrive(0)
        attended[block].start(3, 5)
        attended[block].arrive(1)
        attended[block].start(2, 6)

    def hand_across(block):
        attended[block].arrive(2, 3)
        attended[block].start(7)

    @pl.when(z == 1)
    def _():
        pass_o(False)

    for block in reversed(range(q_blocks)):
        @pl.when(z > 0)
        def _():
            halo(block).wait_recv()

        attend_block(block)
        attended[block].start(0, 1, 4)
        if block + 1 < q_blocks:
            hand_on(block + 1)
        if block + 2 < q_blocks:
            hand_across(block + 2)

    @pl.when(z == 2)
    def _():
        pass_o(True)

    @pl.when(middle)
    def _():
        for distance in (1, 2):
            for piece in range(O_PIECES):
                o_line.forward(distance, piece)

    @pl.when(jnp.logical_not(middle))
    def _():
        w_line.drain(True, False)
        w_line.drain(False, False)

    hand_on(0)
    hand_across(1)
    hand_across(0)
    for gather in attended:
        gather.arrive(4, 5, 6, 7)

    planes = [z, z + 1 - 2 * (z % 2), (z + 2) % 4, 3 - z]
    own_index = y * 4 + x * 2 + c

    def part_rows(part):
        return ((0, o_rows), (0, O_CUTS[1]), (O_CUTS[1], o_rows))[part]

    def r_refs(step, part, mate):
        dy, dx, dc = MATES[mate]
        owner = (y + dy) % 2 * 4 + (x + dx) % 2 * 2 + (c + dc) % 2
        begin, end = part_rows(part)
        rows = pl.ds(begin, end - begin)
        slot = (step + part // 2) * len(MATES) + mate
        return owner, rows, r_send.at[slot], r_recv.at[slot]

    def r_copy(step, part, mate):
        owner, rows, send, recv = r_refs(step, part, mate)
        return remote(
            result.at[step, owner, rows], got.at[step, own_index, rows], send, recv,
            at.mate(*MATES[mate]),
        )

    def r_arrive(step, part, mate):
        owner, rows, send, recv = r_refs(step, part, mate)
        block = got.at[step, owner, rows]
        remote(block, block, send, recv, at.core_id).wait_recv()

    def project(step, part=0):
        begin, end = part_rows(part)
        sums = lax.dot_general(
            wo_all[planes[step], begin:end], att_all[...], (((1,), (1,)), ((), ())),
            preferred_element_type=f32,
        ).astype(bf16)
        for owner in range(8):
            result[step, owner, begin:end] = sums[:, owner * own_tokens:(owner + 1) * own_tokens]
        for mate in range(len(MATES)):
            r_copy(step, part, mate).start()
        got[step, own_index, begin:end] = result[step, own_index, begin:end]

    def finish(step, square, part=0):
        for mate in range(len(MATES)):
            r_arrive(step, part, mate)
        for owner in range(8):
            row, quarter = owner // 4, owner % 4
            start = quarter * (depth // TILE) // 4 * TILE
            size = (quarter + 1) * (depth // TILE) // 4 * TILE - start
            begin, end = part_rows(part)
            end = min(end, size)
            v = got[step, owner, begin:end].astype(f32)
            there = (planes[step] * 2 + row) * depth + start + begin
            turned_out[aligned(there, end - begin), :] = v
            square = square + jnp.sum(v * v, axis=0, keepdims=True)
        return square

    square = jnp.zeros((1, own_tokens), f32)
    last = Z_SIZE - 1
    for step in range(last):
        if step > 0:
            for piece in range(O_PIECES):
                o_line.arrive(step, piece)
        project(step)
        if step > 0:
            square = finish(step - 1, square)
    o_line.arrive(last, 0)
    project(last, 1)
    square = finish(last - 1, square)
    for piece in range(1, O_PIECES):
        o_line.arrive(last, piece)
    project(last, 2)
    square = finish(last, square, 1)
    square = finish(last, square, 2)

    scale = lax.rsqrt(square / model + EPSILON)
    for begin in range(0, model, head):
        columns = slice(begin, begin + head)
        normed = (turned_out[columns, :] * scale).T * gpost[:, columns]
        out_ref[:, columns] = (xs[:, columns].astype(f32) + normed).astype(bf16)

    @pl.when(same)
    def _():
        for part in range(2):
            near_copy(part).wait_send()

    @pl.when(jnp.logical_not(same))
    def _():
        for part in range(2):
            far_copy(part, c, 0, at.y_id).wait_send()
            far_copy(part, 1 - c, 1, at.diag_id).wait_send()

    tokens.drain()
    for gather in attended:
        gather.drain()
    for slot in range(3):
        o_copy(slot).wait_send()

    @pl.when(z < Z_SIZE - 1)
    def _():
        for block in range(q_blocks):
            halo(block).wait_send()

    w_line.drain(True, True)
    w_line.drain(False, True)
    o_line.drain(True)
    o_line.drain(False)
    for step, part in [(step, 0) for step in range(last)] + [(last, 1), (last, 2)]:
        for mate in range(len(MATES)):
            r_copy(step, part, mate).wait_send()


def layer(tokens, positions, w_query, key_matrix, value_matrix, w_out_t, gain_in, gain_query, gain_key, gain_post):
    own_tokens, model = tokens.shape
    depth = w_query.shape[0]
    columns, heads = w_out_t.shape
    head = HEAD_SIZE
    plane = 8 * own_tokens
    bf16, f32, dma = jnp.bfloat16, jnp.float32, pltpu.SemaphoreType.DMA
    frequency = jnp.asarray(ROPE_BASE ** (-2.0 * (np.arange(head) % (head // 2)) / head), f32)
    vmem, anywhere = pl.BlockSpec(memory_space=pltpu.VMEM), pl.BlockSpec(memory_space=pl.ANY)
    o_rows = O_CUTS[-1]
    return pl.pallas_call(
        layer_kernel,
        out_shape=jax.ShapeDtypeStruct((own_tokens, model), bf16),
        in_specs=[anywhere] * 5 + [vmem] * 6,
        out_specs=vmem,
        scratch_shapes=[
            pltpu.VMEM((own_tokens, model), bf16),
            pltpu.VMEM((plane, model), bf16),
            pltpu.VMEM((2, 2, depth, 2 * head), bf16),
            pltpu.VMEM((2, model, 2 * head), bf16),
            pltpu.VMEM((plane, 4 * head), f32),
            pltpu.VMEM((plane, 2 * head), bf16),
            pltpu.VMEM((2, 2 * plane, head), bf16),
            pltpu.VMEM((plane, 4 * heads), bf16),
            pltpu.VMEM((columns, heads), bf16),
            pltpu.VMEM((Z_SIZE, o_rows, 4 * heads), bf16),
            pltpu.VMEM((1, model), f32),
            pltpu.VMEM((1, model), f32),
            pltpu.VMEM((plane, head), f32),
            pltpu.VMEM((plane, head), f32),
            pltpu.VMEM((plane, head), f32),
            pltpu.VMEM((1, 2 * plane), f32),
            pltpu.VMEM((Z_SIZE, 8, o_rows, own_tokens), bf16),
            pltpu.VMEM((Z_SIZE, 8, o_rows, own_tokens), bf16),
            pltpu.VMEM((model, own_tokens), f32),
            dma((8,)), dma((3,)), dma((4,)), dma((4,)), dma((8,)), dma((8,)), dma((4,)), dma((4,)), dma((4, 8)), dma((4, 8)),
            dma((3,)), dma((3,)), dma((7 * Z_SIZE + 7,)), dma((7 * Z_SIZE + 7,)),
            *line_semaphores(W_PIECES), *line_semaphores(O_PIECES),
        ],
        compiler_params=pltpu.CompilerParams(
            collective_id=0, has_side_effects=True, vmem_limit_bytes=60 * 2**20
        ),
        name="layer",
    )(
        tokens, w_query, key_matrix, value_matrix, w_out_t,
        gain_in, gain_post,
        gain_query.reshape(1, -1), gain_key.reshape(1, -1),
        positions.reshape(-1, head), frequency.reshape(1, -1),
    )


def attend(query_matrix, projected_keys, projected_values, query_offsets, key_offsets, key_valid):
    scores = jnp.einsum(
        "qkgd,skd->kgqs", query_matrix, projected_keys, preferred_element_type=jnp.float32
    ) * QS ** (-0.5)
    position_gap = query_offsets[:, None] - key_offsets[None, :]
    allowed = key_valid[None, :] & (position_gap >= 0) & (position_gap < LOOKBACK_WINDOW)
    scores = jnp.where(allowed[None, None], scores, -1e30)
    row_max = jnp.max(scores, axis=-1, keepdims=True)
    weights = jnp.where(allowed[None, None], jnp.exp(scores - row_max), 0.0)
    totals = jnp.sum(weights, axis=-1, keepdims=True)
    rounded = weights.astype(jnp.bfloat16)
    mixed = jnp.einsum(
        "kgqs,skd->qkgd", rounded, projected_values, preferred_element_type=jnp.float32
    )
    mixed = mixed / jnp.transpose(totals, (2, 0, 1, 3))
    return mixed.astype(jnp.bfloat16).reshape(query_matrix.shape[0], -1)


def shards(
    tokens,
    positions,
    w_query,
    key_matrix,
    value_matrix,
    w_out,
    gain_in,
    gain_query,
    gain_key,
    gain_post,
):
    if lax.axis_size("ctx") == 2 * Z_SIZE and lax.axis_size("tp") == 4:
        return layer(
            tokens, positions, w_query, key_matrix, value_matrix, w_out.T,
            gain_in, gain_query, gain_key, gain_post,
        )
    normed = row_norm(tokens.astype(jnp.float32), gain_in).astype(jnp.bfloat16)
    normalized_rows = lax.all_gather(normed, "tp", axis=0, tiled=True)
    weights_in = lax.all_gather(
        jnp.concatenate([w_query, key_matrix, value_matrix], axis=1), "ctx", axis=0, tiled=True
    )
    row_count = normalized_rows.shape[0]
    block_start = lax.axis_index("ctx") * row_count
    offsets_all = positions - positions[0]
    query_offsets = lax.dynamic_slice_in_dim(offsets_all, block_start, row_count, 0)
    query_width, key_width = w_query.shape[1], key_matrix.shape[1]

    def add_rows(weights):
        return jnp.dot(normalized_rows, weights, preferred_element_type=jnp.float32)

    key_value_raw = add_rows(weights_in[:, query_width:])
    query_raw = add_rows(weights_in[:, :query_width])
    unnormed_keys = key_value_raw[:, :key_width]
    value_raw = key_value_raw[:, key_width:]
    key_heads = key_matrix.shape[1] // HEAD_SIZE
    projected_keys = rotate(
        row_norm(unnormed_keys.reshape(row_count, key_heads, HEAD_SIZE), gain_key), query_offsets
    ).astype(jnp.bfloat16)
    projected_values = value_raw.astype(jnp.bfloat16).reshape(row_count, key_heads, HEAD_SIZE)
    own_pair = jnp.stack([projected_keys, projected_values])
    window_blocks = LOOKBACK_WINDOW // row_count
    earlier = [shifted(own_pair, "ctx", steps) for steps in range(window_blocks, 0, -1)]
    window_pair = jnp.concatenate(earlier + [own_pair], axis=1)
    query_heads = w_query.shape[1] // HEAD_SIZE
    query_matrix = rotate(
        row_norm(query_raw.reshape(row_count, query_heads, HEAD_SIZE), gain_query), query_offsets
    ).astype(jnp.bfloat16)
    query_matrix = query_matrix.reshape(row_count, key_heads, query_heads // key_heads, HEAD_SIZE)
    padded_offsets = jnp.concatenate(
        [jnp.zeros((LOOKBACK_WINDOW,), jnp.int32), offsets_all], axis=0
    )
    key_offsets = lax.dynamic_slice_in_dim(
        padded_offsets, block_start, LOOKBACK_WINDOW + row_count, 0
    )
    key_valid = (
        block_start + jnp.arange(LOOKBACK_WINDOW + row_count, dtype=jnp.int32) >= LOOKBACK_WINDOW
    )
    attended = attend(
        query_matrix, window_pair[0], window_pair[1], query_offsets, key_offsets, key_valid
    )
    projected = jnp.dot(
        attended,
        lax.all_gather(w_out, "ctx", axis=1, tiled=True),
        preferred_element_type=jnp.float32,
    )
    summed = lax.psum_scatter(
        projected.astype(jnp.bfloat16), "tp", scatter_dimension=0, tiled=True
    ).astype(jnp.float32)
    return (tokens.astype(jnp.float32) + row_norm(summed, gain_post)).astype(jnp.bfloat16)


def solution(mesh):
    in_specs = (
        P(("ctx", "tp"), None),
        P(),
        P("ctx", "tp"),
        P("ctx", "tp"),
        P("ctx", "tp"),
        P("tp", "ctx"),
        P(),
        P(),
        P(),
        P(),
    )
    out_specs = P(("ctx", "tp"), None)
    return jax.shard_map(shards, mesh=mesh, in_specs=in_specs, out_specs=out_specs, check_vma=False)
```
